256 devices in a mesh: dp: 8 (over z), tensor: 32 (over x, y, core).
Axes of the slice: x: 4, y: 4, z: 8, core: 2. Of those that a mesh axis runs over, the one named last changes fastest.
Arguments:
- hidden: bfloat16 [16384, 2048], P(('dp', 'tensor')), may hold values from -190 to 190
- norm_gain: float32 [2048], replicated, may hold values from 0.1 to 1.9
- head_weight: bfloat16 [2048, 50304], P(None, 'tensor'), may hold values from -0.3 to 0.3
- value_weight: bfloat16 [2048], replicated, may hold values from -0.125 to 0.125
- token_ids: int32 [16384], P(('dp', 'tensor')), may hold values from 0 to 50303
- slot_mask: int32 [16384], P(('dp', 'tensor')), may hold values from 0 to 1, as said below
- lengths: int32 [8, 8], P('dp'), may hold values from 1 to 512, 2048 in all within a row
- request_order: int32 [64], P('dp'), may hold values from 0 to 63, each once
Outputs:
- token_logprob: float32 [16384], P(('dp', 'tensor'))
- token_entropy: float32 [16384], P(('dp', 'tensor'))
- token_value: float32 [16384], P(('dp', 'tensor'))
- request_score: float32 [64], P('dp')
The draws below stay inside these ranges and needn't reach their ends.
Inputs may be any that keep to these rules, and one draw needn't show every extreme that they name: `slot_mask`: 0 or 1. Among the 64 slots of one device at most 48 are 1 and at least half of 48, rounded down; in every draw some device has exactly 48.
All inputs are finite; a program needn't handle non-finite values.
Results may differ from the reference program's by a relative error of at most 0.0029.
Values may be sent and summed in bfloat16 or wider, within the bound.
A program may use at most 64 MiB of HBM per device.

```python
import math
import jax
import jax.numpy as jnp
import numpy as np
from jax import lax

D = 2048
VOCAB = 50304
TOK_DEV = 64
REQS = 8
SLOTS = 2048
TOKENS = 16384
LIVE = 48
MAXLEN = 512
REQ_ALL = 64
N_DP = 8


def draw_hidden(key, part):
    noise_key = jax.random.fold_in(key, 1)
    row_key = jax.random.fold_in(key, 2)
    col_key = jax.random.fold_in(key, 3)
    col_scale = jnp.exp(jax.random.uniform(col_key, (1, D), minval=math.log(0.3), maxval=math.log(3.0)))
    base_draw = jnp.clip(jax.random.normal(noise_key, (TOKENS, D)), -5.0, 5.0)
    row_scale = jnp.exp(jax.random.uniform(row_key, (TOKENS, 1)) * math.log(10.0))
    values = base_draw * row_scale * col_scale
    return values.astype(jnp.float32).astype(jnp.bfloat16)


def draw_head_weight(key, part):
    weight_scale = 3.2 * D ** (-0.5)
    base_key = jax.random.fold_in(key, 21)
    values = jnp.clip(jax.random.normal(base_key, (D, VOCAB)), -4.0, 4.0) * weight_scale
    return values.astype(jnp.float32).astype(jnp.bfloat16)


def draw_slot_mask(key, part):
    block_count = TOKENS // TOK_DEV
    live_counts = jax.random.randint(jax.random.fold_in(key, 41), (block_count,), LIVE // 2, LIVE + 1)
    full_block = jax.random.randint(jax.random.fold_in(key, 42), (), 0, block_count)
    live_counts = jnp.where(jnp.arange(block_count) == full_block, LIVE, live_counts)
    block_keys = jax.random.split(jax.random.fold_in(key, 43), block_count)
    orders = jax.vmap(lambda block_key: jax.random.permutation(block_key, TOK_DEV))(block_keys)
    return (orders < live_counts[:, None]).astype(jnp.int32).reshape(TOKENS)


def plant(array, own_key, least, largest):
    longest = array.shape.index(max(array.shape))
    spots = []
    for shift in (0, 1):
        where = [jax.random.randint(jax.random.fold_in(own_key, axis), (), 0, length) for axis, length in enumerate(array.shape)]
        where[longest] = (where[longest] + shift) % array.shape[longest]
        spots.append(tuple(where))
    return array.at[spots[0]].set(least).at[spots[1]].set(largest)


def rank_table(number_of, lean):
    weights = [(1 << 20) // math.isqrt(grade ** lean) + 1 for grade in range(1, number_of + 1)]
    width = 1 + sum(weights) // (1 << 30)
    return np.cumsum(np.array([max(1, weight // width) for weight in weights]))


def ranked_ids(rng, dims, count, skew):
    table = rank_table(count, skew)
    pick = jax.random.randint(jax.random.fold_in(rng, 1), dims, 0, int(table[count - 1]))
    rank = jnp.searchsorted(jnp.asarray(table, jnp.int32), pick, side="right")
    return jax.random.permutation(jax.random.fold_in(rng, 2), count)[rank].astype(jnp.int32)


def length_profile(amount, total, most, skew):
    portions = [(1 << 20) // math.isqrt(standing ** skew) + 1 for standing in range(2, amount + 1)]
    surplus, holding = total - most - (amount - 1), [1] * (amount - 1)
    while surplus > 0:
        candidates = [i for i in range(amount - 1) if holding[i] < most]
        pool, remaining = sum([portions[i] for i in candidates]), surplus
        for i in candidates:
            extra = min(most - holding[i], max(1, remaining * portions[i] // pool), surplus)
            holding[i] = holding[i] + extra
            surplus = surplus - extra
    return np.array([most] + holding)


def ragged_sizes(rng, amount, total, limit, skew):
    if amount == 2:
        one = jax.random.randint(rng, (), max(1, total - limit), min(limit, total - 1) + 1)
        return jnp.stack([one, total - one])
    tallies = jnp.asarray(length_profile(amount, total, limit, skew), jnp.int32)
    pairs = (amount - 1) // 2
    donor, taker = tallies[1:1 + 2 * pairs:2], tallies[2:2 + 2 * pairs:2]
    slack = jnp.minimum(donor - 1, limit - taker)
    passed = jax.random.randint(jax.random.fold_in(rng, 1), (pairs,), 0, 1 << 20) % (slack + 1)
    tallies = tallies.at[1:1 + 2 * pairs:2].set(donor - passed).at[2:2 + 2 * pairs:2].set(taker + passed)
    return tallies[jax.random.permutation(jax.random.fold_in(rng, 2), amount)]


def bell_draw(stream_key, shape, spread, reach, kind=jnp.bfloat16):
    values = spread * jax.random.normal(stream_key, shape, jnp.float32)
    return jnp.clip(values, min=-reach, max=reach).astype(kind)


def setup_inputs(seed: int = 0) -> dict:
    splits = jax.random.split(jax.random.key(seed), 9)
    hidden = draw_hidden(jax.random.fold_in(splits[8], 71), 0)
    norm_gain = jnp.clip(1.0 + 0.18 * jax.random.normal(splits[1], (D,), jnp.float32), 0.1, 1.9)
    head_weight = draw_head_weight(jax.random.fold_in(splits[8], 71), 0)
    value_weight = bell_draw(splits[3], (D,), D ** -0.5, 0.125)
    token_ids = plant(ranked_ids(splits[4], (TOKENS,), VOCAB, 2), jax.random.fold_in(splits[4], 3), 0, VOCAB - 1).astype(jnp.int32)
    slot_mask = draw_slot_mask(jax.random.fold_in(splits[8], 71), 0)
    lengths = jax.vmap(lambda own: ragged_sizes(own, REQS, SLOTS, MAXLEN, 2))(jax.random.split(splits[6], N_DP)).reshape((N_DP, REQS)).astype(jnp.int32)
    request_order = jax.random.permutation(splits[7], REQ_ALL).astype(jnp.int32)
    return dict(hidden=hidden, norm_gain=norm_gain, head_weight=head_weight, value_weight=value_weight, token_ids=token_ids, slot_mask=slot_mask, lengths=lengths, request_order=request_order)


EPSILON = 1e-06

def normalize(hidden, norm_gain):
    widened = hidden.astype(jnp.float32)
    inverse_rms = lax.rsqrt(lax.optimization_barrier(jnp.mean(widened * widened, axis=-1, keepdims=True)) + EPSILON)
    return (widened * inverse_rms * norm_gain).astype(jnp.bfloat16)

def reference(hidden, norm_gain, head_weight, value_weight, token_ids, slot_mask, lengths, request_order):
    normed = normalize(hidden, norm_gain)
    weight_mask = slot_mask.astype(jnp.float32)
    token_value = weight_mask * jnp.dot(normed, value_weight, preferred_element_type=jnp.float32)
    group_rows = normed.reshape(N_DP, SLOTS, D)
    group_ids = token_ids.reshape(N_DP, SLOTS)

    def score_group(group_pair):
        piece_rows, piece_ids = group_pair
        logits = jnp.dot(piece_rows, head_weight, preferred_element_type=jnp.float32)
        row_peak = lax.optimization_barrier(jnp.max(logits, axis=1, keepdims=True))
        shifted = logits - row_peak
        weights = jnp.exp(shifted)
        row_mass = lax.optimization_barrier(jnp.sum(weights, axis=1))
        row_spread = lax.optimization_barrier(jnp.sum(weights * shifted, axis=1))
        row_target = jnp.take_along_axis(shifted, piece_ids[:, None].astype(jnp.int32), axis=1)[:, 0]
        log_mass = jnp.log(row_mass)
        return (row_target - log_mass, log_mass - row_spread / row_mass)
    logprob_all, entropy_all = lax.map(score_group, (group_rows, group_ids))
    token_logprob = weight_mask * logprob_all.reshape(TOKENS)
    token_entropy = weight_mask * entropy_all.reshape(TOKENS)
    span_ends = jnp.cumsum(lengths, axis=1).astype(jnp.int32)
    slot_index = jnp.arange(SLOTS, dtype=jnp.int32)
    position = lax.optimization_barrier(jnp.sum((slot_index[None, :, None] >= span_ends[:, None, :]).astype(jnp.int32), axis=2)).astype(jnp.int32)
    onehot = position[:, :, None] == jnp.arange(REQS, dtype=jnp.int32)[None, None, :]
    grouped = token_logprob.reshape(N_DP, SLOTS)
    by_pos = lax.optimization_barrier(jnp.sum(jnp.where(onehot, grouped[:, :, None], jnp.float32(0.0)), axis=1)) / lengths.astype(jnp.float32)
    request_score = jnp.zeros((REQ_ALL,), jnp.float32).at[request_order].add(by_pos.reshape(REQ_ALL))
    return (token_logprob, token_entropy, token_value, request_score)
```

```python
import jax
import jax.numpy as jnp
from jax import lax
from jax.sharding import PartitionSpec as P

EPSILON = 1e-06


def on_device(
    hidden, norm_gain, head_weight, value_weight, token_ids, slot_mask, lengths, request_order
):
    own_rows = hidden.shape[0]
    vocab_local = head_weight.shape[1]
    tensor_index = lax.axis_index("tensor")
    widened = hidden.astype(jnp.float32)
    inverse_rms = lax.rsqrt(jnp.mean(widened * widened, axis=1, keepdims=True) + EPSILON)
    normed = (widened * inverse_rms * norm_gain).astype(jnp.bfloat16)
    weight_mask = slot_mask.astype(jnp.float32)
    token_value = weight_mask * jnp.dot(normed, value_weight, preferred_element_type=jnp.float32)

    columns = tensor_index * vocab_local + jnp.arange(vocab_local, dtype=jnp.int32)
    piece_rows = lax.all_gather(normed, "tensor", axis=0, tiled=True)
    piece_meta = lax.all_gather(jnp.stack([token_ids, slot_mask]), "tensor", axis=1, tiled=True)
    piece_ids = piece_meta[0]
    piece_mask = piece_meta[1].astype(jnp.float32)

    logits = jnp.dot(piece_rows, head_weight, preferred_element_type=jnp.float32)
    row_peak = jnp.max(logits, axis=1)
    shifted = logits - row_peak[:, None]
    weights = jnp.exp(shifted)
    row_mass = jnp.sum(weights, axis=1)
    row_spread = jnp.sum(weights * shifted, axis=1)
    row_target = jnp.sum(jnp.where(columns[None, :] == piece_ids[:, None], logits, 0.0), axis=1)

    stats = jnp.stack([row_peak, row_mass, row_spread, row_target])
    parts = lax.all_gather(stats, "tensor", axis=0)
    part_peak, part_mass, part_spread, part_target = parts[:, 0], parts[:, 1], parts[:, 2], parts[:, 3]
    peak = jnp.max(part_peak, axis=0)
    gap = part_peak - peak[None, :]
    factor = jnp.exp(gap)
    mass = jnp.sum(factor * part_mass, axis=0)
    spread = jnp.sum(factor * (part_spread + gap * part_mass), axis=0)
    target = jnp.sum(part_target, axis=0)
    log_mass = jnp.log(mass)
    group_logprob = piece_mask * (target - peak - log_mass)
    group_entropy = log_mass - spread / mass

    own_start = tensor_index * own_rows
    token_logprob = lax.dynamic_slice_in_dim(group_logprob, own_start, own_rows)
    token_entropy = weight_mask * lax.dynamic_slice_in_dim(group_entropy, own_start, own_rows)

    request_count = lengths.shape[1]
    span_lengths = lengths[0]
    span_ends = jnp.cumsum(span_lengths)
    slot_ids = jnp.arange(group_logprob.shape[0], dtype=jnp.int32)
    position = jnp.sum((slot_ids[:, None] >= span_ends[None, :]).astype(jnp.int32), axis=1)
    onehot = position[:, None] == jnp.arange(request_count, dtype=jnp.int32)[None, :]
    by_pos = jnp.sum(jnp.where(onehot, group_logprob[:, None], 0.0), axis=0) / span_lengths.astype(
        jnp.float32
    )
    routed = lax.all_gather(
        jnp.concatenate([by_pos, request_order.astype(jnp.float32)]), "dp", axis=0
    )
    all_totals = routed[:, :request_count].reshape(-1)
    all_owners = routed[:, request_count:].reshape(-1)
    wanted = (lax.axis_index("dp") * request_count + jnp.arange(request_count)).astype(jnp.float32)
    route_table = all_owners[:, None] == wanted[None, :]
    request_score = jnp.sum(jnp.where(route_table, all_totals[:, None], 0.0), axis=0)
    return (token_logprob, token_entropy, token_value, request_score)


def solution(mesh):
    return jax.shard_map(
        on_device,
        mesh=mesh,
        in_specs=(
            P(("dp", "tensor"), None),
            P(),
            P(None, "tensor"),
            P(),
            P(("dp", "tensor")),
            P(("dp", "tensor")),
            P("dp", None),
            P("dp"),
        ),
        out_specs=(P(("dp", "tensor")), P(("dp", "tensor")), P(("dp", "tensor")), P("dp")),
        check_vma=False,
    )
```

```python
import jax
import jax.numpy as jnp
from jax import lax
from jax.experimental import pallas as pl
from jax.experimental.pallas import tpu as pltpu
from jax.sharding import PartitionSpec as P

EPSILON = 1e-06
MESH = pl.DeviceIdType.MESH


def exchange_kernel(n_tensor, send_ref, out_ref, held, send_sem, recv_sem):
    me = lax.axis_index("tensor")
    dp = lax.axis_index("dp")
    barrier = pltpu.get_barrier_semaphore()
    for offset in range(1, n_tensor):
        peer = lax.rem(me + offset, n_tensor)
        pl.semaphore_signal(barrier, inc=1, device_id=(dp, peer), device_id_type=MESH)
    pl.semaphore_wait(barrier, n_tensor - 1)
    held[me] = send_ref[me]
    copies = []
    for offset in range(1, n_tensor):
        peer = lax.rem(me + offset, n_tensor)
        copy = pltpu.make_async_remote_copy(
            src_ref=send_ref.at[peer],
            dst_ref=held.at[me],
            send_sem=send_sem.at[offset],
            recv_sem=recv_sem.at[offset],
            device_id=(dp, peer),
            device_id_type=MESH,
        )
        copy.start()
        copies.append(copy)
    for copy in copies:
        copy.wait_send()
    for offset in range(1, n_tensor):
        source = lax.rem(me + n_tensor - offset, n_tensor)
        pltpu.make_async_remote_copy(
            src_ref=send_ref.at[source],
            dst_ref=held.at[source],
            send_sem=send_sem.at[offset],
            recv_sem=recv_sem.at[offset],
            device_id=(dp, source),
            device_id_type=MESH,
        ).wait_recv()
    out_ref[...] = held[...]


def exchange(blocks, n_tensor):
    return pl.pallas_call(
        lambda *refs: exchange_kernel(n_tensor, *refs),
        out_shape=jax.ShapeDtypeStruct(blocks.shape, blocks.dtype),
        in_specs=[pl.BlockSpec(memory_space=pltpu.VMEM)],
        out_specs=pl.BlockSpec(memory_space=pltpu.VMEM),
        scratch_shapes=[
            pltpu.VMEM(blocks.shape, blocks.dtype),
            pltpu.SemaphoreType.DMA((n_tensor,)),
            pltpu.SemaphoreType.DMA((n_tensor,)),
        ],
        compiler_params=pltpu.CompilerParams(collective_id=0, has_side_effects=True),
    )(blocks)


def route_kernel(n_tensor, n_dp, part_ref, ids_ref, out_ref, t_held, d_held, msg,
                 t_send, t_recv, d_send, d_recv):
    me = lax.axis_index("tensor")
    dp = lax.axis_index("dp")
    barrier = pltpu.get_barrier_semaphore()
    for offset in range(1, n_tensor):
        peer = lax.rem(me + offset, n_tensor)
        pl.semaphore_signal(barrier, inc=1, device_id=(dp, peer), device_id_type=MESH)
    for offset in range(1, n_dp):
        peer = lax.rem(dp + offset, n_dp)
        pl.semaphore_signal(barrier, inc=1, device_id=(peer, me), device_id_type=MESH)
    pl.semaphore_wait(barrier, n_tensor - 1 + n_dp - 1)
    t_held[me] = part_ref[...]
    copies = []
    for offset in range(1, n_tensor):
        peer = lax.rem(me + offset, n_tensor)
        copy = pltpu.make_async_remote_copy(
            src_ref=part_ref,
            dst_ref=t_held.at[me],
            send_sem=t_send.at[offset],
            recv_sem=t_recv.at[offset],
            device_id=(dp, peer),
            device_id_type=MESH,
        )
        copy.start()
        copies.append(copy)
    for copy in copies:
        copy.wait_send()
    for offset in range(1, n_tensor):
        source = lax.rem(me + n_tensor - offset, n_tensor)
        pltpu.make_async_remote_copy(
            src_ref=part_ref,
            dst_ref=t_held.at[source],
            send_sem=t_send.at[offset],
            recv_sem=t_recv.at[offset],
            device_id=(dp, source),
            device_id_type=MESH,
        ).wait_recv()
    total = jnp.sum(t_held[...], axis=0)
    row = lax.broadcasted_iota(jnp.int32, total.shape, 0)
    msg[...] = jnp.where(row == 0, total, jnp.where(row == 1, ids_ref[...], 0.0))
    d_held[dp] = msg[...]
    copies = []
    for offset in range(1, n_dp):
        peer = lax.rem(dp + offset, n_dp)
        copy = pltpu.make_async_remote_copy(
            src_ref=msg,
            dst_ref=d_held.at[dp],
            send_sem=d_send.at[offset],
            recv_sem=d_recv.at[offset],
            device_id=(peer, me),
            device_id_type=MESH,
        )
        copy.start()
        copies.append(copy)
    for copy in copies:
        copy.wait_send()
    for offset in range(1, n_dp):
        source = lax.rem(dp + n_dp - offset, n_dp)
        pltpu.make_async_remote_copy(
            src_ref=msg,
            dst_ref=d_held.at[source],
            send_sem=d_send.at[offset],
            recv_sem=d_recv.at[offset],
            device_id=(source, me),
            device_id_type=MESH,
        ).wait_recv()
    out_ref[...] = d_held[...]


def route(part, ids, n_tensor, n_dp):
    tile = part.shape
    return pl.pallas_call(
        lambda *refs: route_kernel(n_tensor, n_dp, *refs),
        out_shape=jax.ShapeDtypeStruct((n_dp,) + tile, jnp.float32),
        in_specs=[pl.BlockSpec(memory_space=pltpu.VMEM)] * 2,
        out_specs=pl.BlockSpec(memory_space=pltpu.VMEM),
        scratch_shapes=[
            pltpu.VMEM((n_tensor,) + tile, jnp.float32),
            pltpu.VMEM((n_dp,) + tile, jnp.float32),
            pltpu.VMEM(tile, jnp.float32),
            pltpu.SemaphoreType.DMA((n_tensor,)),
            pltpu.SemaphoreType.DMA((n_tensor,)),
            pltpu.SemaphoreType.DMA((n_dp,)),
            pltpu.SemaphoreType.DMA((n_dp,)),
        ],
        compiler_params=pltpu.CompilerParams(collective_id=1, has_side_effects=True),
    )(part, ids)


def on_device(
    hidden, norm_gain, head_weight, value_weight, token_ids, slot_mask, lengths, request_order
):
    own_rows = hidden.shape[0]
    vocab_local = head_weight.shape[1]
    n_tensor = lax.axis_size("tensor")
    n_dp = lax.axis_size("dp")
    tensor_index = lax.axis_index("tensor")
    widened = hidden.astype(jnp.float32)
    inverse_rms = lax.rsqrt(jnp.mean(widened * widened, axis=1, keepdims=True) + EPSILON)
    normed = (widened * inverse_rms * norm_gain).astype(jnp.bfloat16)
    weight_mask = slot_mask.astype(jnp.float32)
    token_value = weight_mask * jnp.dot(normed, value_weight, preferred_element_type=jnp.float32)

    columns = tensor_index * vocab_local + jnp.arange(vocab_local, dtype=jnp.int32)
    piece_rows = lax.all_gather(normed, "tensor", axis=0, tiled=True)
    piece_ids = lax.all_gather(token_ids, "tensor", axis=0, tiled=True)

    logits = jnp.dot(piece_rows, head_weight, preferred_element_type=jnp.float32)
    row_peak = jnp.max(logits, axis=1)
    shifted = logits - row_peak[:, None]
    weights = jnp.exp(shifted)
    row_mass = jnp.sum(weights, axis=1)
    row_spread = jnp.sum(weights * shifted, axis=1)
    row_target = jnp.sum(jnp.where(columns[None, :] == piece_ids[:, None], logits, 0.0), axis=1)

    stats = jnp.stack([row_peak, row_mass, row_spread, row_target])
    blocks = stats.reshape(4, n_tensor, own_rows).transpose(1, 0, 2)
    parts = exchange(blocks, n_tensor)
    part_peak, part_mass, part_spread, part_target = parts[:, 0], parts[:, 1], parts[:, 2], parts[:, 3]
    peak = jnp.max(part_peak, axis=0)
    gap = part_peak - peak[None, :]
    factor = jnp.exp(gap)
    mass = jnp.sum(factor * part_mass, axis=0)
    spread = jnp.sum(factor * (part_spread + gap * part_mass), axis=0)
    target = jnp.sum(part_target, axis=0)
    log_mass = jnp.log(mass)
    token_logprob = weight_mask * (target - peak - log_mass)
    token_entropy = weight_mask * (log_mass - spread / mass)

    request_count = lengths.shape[1]
    span_lengths = lengths[0]
    span_ends = jnp.cumsum(span_lengths)
    slot_ids = tensor_index * own_rows + jnp.arange(own_rows, dtype=jnp.int32)
    position = jnp.sum((slot_ids[:, None] >= span_ends[None, :]).astype(jnp.int32), axis=1)
    onehot = position[:, None] == jnp.arange(request_count, dtype=jnp.int32)[None, :]
    by_pos = jnp.sum(jnp.where(onehot, token_logprob[:, None], 0.0), axis=0) / span_lengths.astype(
        jnp.float32
    )
    tile = jnp.zeros((8, 128), jnp.float32)
    part_tile = tile.at[0, :request_count].set(by_pos)
    ids_tile = tile.at[1, :request_count].set(request_order.astype(jnp.float32))
    routed = route(part_tile, ids_tile, n_tensor, n_dp)
    all_totals = routed[:, 0, :request_count].reshape(-1)
    all_owners = routed[:, 1, :request_count].reshape(-1)
    wanted = (lax.axis_index("dp") * request_count + jnp.arange(request_count)).astype(jnp.float32)
    route_table = all_owners[:, None] == wanted[None, :]
    request_score = jnp.sum(jnp.where(route_table, all_totals[:, None], 0.0), axis=0)
    return (token_logprob, token_entropy, token_value, request_score)


def solution(mesh):
    return jax.shard_map(
        on_device,
        mesh=mesh,
        in_specs=(
            P(("dp", "tensor"), None),
            P(),
            P(None, "tensor"),
            P(),
            P(("dp", "tensor")),
            P(("dp", "tensor")),
            P("dp", None),
            P("dp"),
        ),
        out_specs=(P(("dp", "tensor")), P(("dp", "tensor")), P(("dp", "tensor")), P("dp")),
        check_vma=False,
    )
```

```python
import jax
import jax.numpy as jnp
from jax import lax
from jax.experimental import pallas as pl
from jax.experimental.pallas import tpu as pltpu
from jax.sharding import PartitionSpec as P

EPSILON = 1e-06
MESH = pl.DeviceIdType.MESH
LIVE = 48


def exchange_kernel(n_tensor, send_ref, out_ref, held, send_sem, recv_sem):
    me = lax.axis_index("tensor")
    dp = lax.axis_index("dp")
    barrier = pltpu.get_barrier_semaphore()
    for offset in range(1, n_tensor):
        peer = lax.rem(me + offset, n_tensor)
        pl.semaphore_signal(barrier, inc=1, device_id=(dp, peer), device_id_type=MESH)
    pl.semaphore_wait(barrier, n_tensor - 1)
    held[me] = send_ref[me]
    copies = []
    for offset in range(1, n_tensor):
        peer = lax.rem(me + offset, n_tensor)
        copy = pltpu.make_async_remote_copy(
            src_ref=send_ref.at[peer],
            dst_ref=held.at[me],
            send_sem=send_sem.at[offset],
            recv_sem=recv_sem.at[offset],
            device_id=(dp, peer),
            device_id_type=MESH,
        )
        copy.start()
        copies.append(copy)
    for copy in copies:
        copy.wait_send()
    for offset in range(1, n_tensor):
        source = lax.rem(me + n_tensor - offset, n_tensor)
        pltpu.make_async_remote_copy(
            src_ref=send_ref.at[source],
            dst_ref=held.at[source],
            send_sem=send_sem.at[offset],
            recv_sem=recv_sem.at[offset],
            device_id=(dp, source),
            device_id_type=MESH,
        ).wait_recv()
    out_ref[...] = held[...]


def exchange(blocks, n_tensor):
    return pl.pallas_call(
        lambda *refs: exchange_kernel(n_tensor, *refs),
        out_shape=jax.ShapeDtypeStruct(blocks.shape, blocks.dtype),
        in_specs=[pl.BlockSpec(memory_space=pltpu.VMEM)],
        out_specs=pl.BlockSpec(memory_space=pltpu.VMEM),
        scratch_shapes=[
            pltpu.VMEM(blocks.shape, blocks.dtype),
            pltpu.SemaphoreType.DMA((n_tensor,)),
            pltpu.SemaphoreType.DMA((n_tensor,)),
        ],
        compiler_params=pltpu.CompilerParams(collective_id=0, has_side_effects=True),
    )(blocks)


def route_kernel(n_tensor, n_dp, part_ref, ids_ref, out_ref, t_held, d_held, msg,
                 t_send, t_recv, d_send, d_recv):
    me = lax.axis_index("tensor")
    dp = lax.axis_index("dp")
    barrier = pltpu.get_barrier_semaphore()
    for offset in range(1, n_tensor):
        peer = lax.rem(me + offset, n_tensor)
        pl.semaphore_signal(barrier, inc=1, device_id=(dp, peer), device_id_type=MESH)
    for offset in range(1, n_dp):
        peer = lax.rem(dp + offset, n_dp)
        pl.semaphore_signal(barrier, inc=1, device_id=(peer, me), device_id_type=MESH)
    pl.semaphore_wait(barrier, n_tensor - 1 + n_dp - 1)
    t_held[me] = part_ref[...]
    copies = []
    for offset in range(1, n_tensor):
        peer = lax.rem(me + offset, n_tensor)
        copy = pltpu.make_async_remote_copy(
            src_ref=part_ref,
            dst_ref=t_held.at[me],
            send_sem=t_send.at[offset],
            recv_sem=t_recv.at[offset],
            device_id=(dp, peer),
            device_id_type=MESH,
        )
        copy.start()
        copies.append(copy)
    for copy in copies:
        copy.wait_send()
    for offset in range(1, n_tensor):
        source = lax.rem(me + n_tensor - offset, n_tensor)
        pltpu.make_async_remote_copy(
            src_ref=part_ref,
            dst_ref=t_held.at[source],
            send_sem=t_send.at[offset],
            recv_sem=t_recv.at[offset],
            device_id=(dp, source),
            device_id_type=MESH,
        ).wait_recv()
    total = jnp.sum(t_held[...], axis=0)
    row = lax.broadcasted_iota(jnp.int32, total.shape, 0)
    msg[...] = jnp.where(row == 0, total, jnp.where(row == 1, ids_ref[...], 0.0))
    d_held[dp] = msg[...]
    copies = []
    for offset in range(1, n_dp):
        peer = lax.rem(dp + offset, n_dp)
        copy = pltpu.make_async_remote_copy(
            src_ref=msg,
            dst_ref=d_held.at[dp],
            send_sem=d_send.at[offset],
            recv_sem=d_recv.at[offset],
            device_id=(peer, me),
            device_id_type=MESH,
        )
        copy.start()
        copies.append(copy)
    for copy in copies:
        copy.wait_send()
    for offset in range(1, n_dp):
        source = lax.rem(dp + n_dp - offset, n_dp)
        pltpu.make_async_remote_copy(
            src_ref=msg,
            dst_ref=d_held.at[source],
            send_sem=d_send.at[offset],
            recv_sem=d_recv.at[offset],
            device_id=(source, me),
            device_id_type=MESH,
        ).wait_recv()
    out_ref[...] = d_held[...]


def route(part, ids, n_tensor, n_dp):
    tile = part.shape
    return pl.pallas_call(
        lambda *refs: route_kernel(n_tensor, n_dp, *refs),
        out_shape=jax.ShapeDtypeStruct((n_dp,) + tile, jnp.float32),
        in_specs=[pl.BlockSpec(memory_space=pltpu.VMEM)] * 2,
        out_specs=pl.BlockSpec(memory_space=pltpu.VMEM),
        scratch_shapes=[
            pltpu.VMEM((n_tensor,) + tile, jnp.float32),
            pltpu.VMEM((n_dp,) + tile, jnp.float32),
            pltpu.VMEM(tile, jnp.float32),
            pltpu.SemaphoreType.DMA((n_tensor,)),
            pltpu.SemaphoreType.DMA((n_tensor,)),
            pltpu.SemaphoreType.DMA((n_dp,)),
            pltpu.SemaphoreType.DMA((n_dp,)),
        ],
        compiler_params=pltpu.CompilerParams(collective_id=1, has_side_effects=True),
    )(part, ids)


def on_device(
    hidden, norm_gain, head_weight, value_weight, token_ids, slot_mask, lengths, request_order
):
    own_rows = hidden.shape[0]
    vocab_local = head_weight.shape[1]
    n_tensor = lax.axis_size("tensor")
    n_dp = lax.axis_size("dp")
    tensor_index = lax.axis_index("tensor")
    widened = hidden.astype(jnp.float32)
    inverse_rms = lax.rsqrt(jnp.mean(widened * widened, axis=1, keepdims=True) + EPSILON)
    normed = (widened * inverse_rms * norm_gain).astype(jnp.bfloat16)
    weight_mask = slot_mask.astype(jnp.float32)
    token_value = weight_mask * jnp.dot(normed, value_weight, preferred_element_type=jnp.float32)

    columns = tensor_index * vocab_local + jnp.arange(vocab_local, dtype=jnp.int32)
    width = hidden.shape[1]
    live_sum = jnp.cumsum(slot_mask)
    slot_index = jnp.arange(own_rows, dtype=jnp.int32)
    chosen = (slot_mask[None, :] == 1) & (
        live_sum[None, :] - 1 == jnp.arange(LIVE, dtype=jnp.int32)[:, None]
    )
    source = jnp.sum(jnp.where(chosen, slot_index[None, :], 0), axis=1)
    compact_rows = jnp.take(normed, source, axis=0)
    compact_ids = jnp.take(token_ids, source)
    meta = (
        jnp.zeros((1, width), jnp.bfloat16)
        .at[0, :LIVE].set((compact_ids // 256).astype(jnp.bfloat16))
        .at[0, 128:128 + LIVE].set((compact_ids % 256).astype(jnp.bfloat16))
    )
    block = jnp.concatenate([compact_rows, meta], axis=0)
    piece_rows = lax.all_gather(block, "tensor", axis=0, tiled=True)
    block_rows = LIVE + 1
    meta_rows = piece_rows.reshape(n_tensor, block_rows, width)[:, LIVE, :].astype(jnp.float32)
    gathered_ids = (meta_rows[:, :LIVE] * 256.0 + meta_rows[:, 128:128 + LIVE]).astype(jnp.int32)
    piece_ids = jnp.concatenate(
        [gathered_ids, jnp.full((n_tensor, 1), -1, jnp.int32)], axis=1
    ).reshape(-1)

    logits = jnp.dot(piece_rows, head_weight, preferred_element_type=jnp.float32)
    row_peak = jnp.max(logits, axis=1)
    shifted = logits - row_peak[:, None]
    weights = jnp.exp(shifted)
    row_mass = jnp.sum(weights, axis=1)
    row_spread = jnp.sum(weights * shifted, axis=1)
    row_target = jnp.sum(jnp.where(columns[None, :] == piece_ids[:, None], logits, 0.0), axis=1)

    stats = jnp.stack([row_peak, row_mass, row_spread, row_target])
    blocks = stats.reshape(4, n_tensor, block_rows)[:, :, :LIVE].transpose(1, 0, 2)
    parts = exchange(blocks, n_tensor)
    part_peak, part_mass, part_spread, part_target = parts[:, 0], parts[:, 1], parts[:, 2], parts[:, 3]
    peak = jnp.max(part_peak, axis=0)
    gap = part_peak - peak[None, :]
    factor = jnp.exp(gap)
    mass = jnp.sum(factor * part_mass, axis=0)
    spread = jnp.sum(factor * (part_spread + gap * part_mass), axis=0)
    target = jnp.sum(part_target, axis=0)
    log_mass = jnp.log(mass)
    place = jnp.clip(live_sum - 1, 0, LIVE - 1)
    token_logprob = weight_mask * jnp.take(target - peak - log_mass, place)
    token_entropy = weight_mask * jnp.take(log_mass - spread / mass, place)

    request_count = lengths.shape[1]
    span_lengths = lengths[0]
    span_ends = jnp.cumsum(span_lengths)
    slot_ids = tensor_index * own_rows + jnp.arange(own_rows, dtype=jnp.int32)
    position = jnp.sum((slot_ids[:, None] >= span_ends[None, :]).astype(jnp.int32), axis=1)
    onehot = position[:, None] == jnp.arange(request_count, dtype=jnp.int32)[None, :]
    by_pos = jnp.sum(jnp.where(onehot, token_logprob[:, None], 0.0), axis=0) / span_lengths.astype(
        jnp.float32
    )
    tile = jnp.zeros((8, 128), jnp.float32)
    part_tile = tile.at[0, :request_count].set(by_pos)
    ids_tile = tile.at[1, :request_count].set(request_order.astype(jnp.float32))
    routed = route(part_tile, ids_tile, n_tensor, n_dp)
    all_totals = routed[:, 0, :request_count].reshape(-1)
    all_owners = routed[:, 1, :request_count].reshape(-1)
    wanted = (lax.axis_index("dp") * request_count + jnp.arange(request_count)).astype(jnp.float32)
    route_table = all_owners[:, None] == wanted[None, :]
    request_score = jnp.sum(jnp.where(route_table, all_totals[:, None], 0.0), axis=0)
    return (token_logprob, token_entropy, token_value, request_score)


def solution(mesh):
    return jax.shard_map(
        on_device,
        mesh=mesh,
        in_specs=(
            P(("dp", "tensor"), None),
            P(),
            P(None, "tensor"),
            P(),
            P(("dp", "tensor")),
            P(("dp", "tensor")),
            P("dp", None),
            P("dp"),
        ),
        out_specs=(P(("dp", "tensor")), P(("dp", "tensor")), P(("dp", "tensor")), P("dp")),
        check_vma=False,
    )
```

```python
import jax
import jax.numpy as jnp
from jax import lax
from jax.experimental import pallas as pl
from jax.experimental.pallas import tpu as pltpu
from jax.sharding import PartitionSpec as P

EPSILON = 1e-06
MESH = pl.DeviceIdType.MESH
LIVE = 48


def exchange_kernel(n_tensor, send_ref, out_ref, held, send_sem, recv_sem):
    me = lax.axis_index("tensor")
    dp = lax.axis_index("dp")
    barrier = pltpu.get_barrier_semaphore()
    for offset in range(1, n_tensor):
        peer = lax.rem(me + offset, n_tensor)
        pl.semaphore_signal(barrier, inc=1, device_id=(dp, peer), device_id_type=MESH)
    pl.semaphore_wait(barrier, n_tensor - 1)
    held[me] = send_ref[me]
    copies = []
    for offset in range(1, n_tensor):
        peer = lax.rem(me + offset, n_tensor)
        copy = pltpu.make_async_remote_copy(
            src_ref=send_ref.at[peer],
            dst_ref=held.at[me],
            send_sem=send_sem.at[offset],
            recv_sem=recv_sem.at[offset],
            device_id=(dp, peer),
            device_id_type=MESH,
        )
        copy.start()
        copies.append(copy)
    for copy in copies:
        copy.wait_send()
    for offset in range(1, n_tensor):
        source = lax.rem(me + n_tensor - offset, n_tensor)
        pltpu.make_async_remote_copy(
            src_ref=send_ref.at[source],
            dst_ref=held.at[source],
            send_sem=send_sem.at[offset],
            recv_sem=recv_sem.at[offset],
            device_id=(dp, source),
            device_id_type=MESH,
        ).wait_recv()
    out_ref[...] = held[...]


def exchange(blocks, n_tensor):
    return pl.pallas_call(
        lambda *refs: exchange_kernel(n_tensor, *refs),
        out_shape=jax.ShapeDtypeStruct(blocks.shape, blocks.dtype),
        in_specs=[pl.BlockSpec(memory_space=pltpu.VMEM)],
        out_specs=pl.BlockSpec(memory_space=pltpu.VMEM),
        scratch_shapes=[
            pltpu.VMEM(blocks.shape, blocks.dtype),
            pltpu.SemaphoreType.DMA((n_tensor,)),
            pltpu.SemaphoreType.DMA((n_tensor,)),
        ],
        compiler_params=pltpu.CompilerParams(collective_id=0, has_side_effects=True),
    )(blocks)


def route_kernel(n_tensor, n_dp, part_ref, ids_ref, out_ref, t_held, d_held, msg,
                 t_send, t_recv, d_send, d_recv):
    me = lax.axis_index("tensor")
    dp = lax.axis_index("dp")
    barrier = pltpu.get_barrier_semaphore()
    for offset in range(1, n_tensor):
        peer = lax.rem(me + offset, n_tensor)
        pl.semaphore_signal(barrier, inc=1, device_id=(dp, peer), device_id_type=MESH)
    for offset in range(1, n_dp):
        peer = lax.rem(dp + offset, n_dp)
        pl.semaphore_signal(barrier, inc=1, device_id=(peer, me), device_id_type=MESH)
    pl.semaphore_wait(barrier, n_tensor - 1 + n_dp - 1)
    t_held[me] = part_ref[...]
    copies = []
    for offset in range(1, n_tensor):
        peer = lax.rem(me + offset, n_tensor)
        copy = pltpu.make_async_remote_copy(
            src_ref=part_ref,
            dst_ref=t_held.at[me],
            send_sem=t_send.at[offset],
            recv_sem=t_recv.at[offset],
            device_id=(dp, peer),
            device_id_type=MESH,
        )
        copy.start()
        copies.append(copy)
    for copy in copies:
        copy.wait_send()
    for offset in range(1, n_tensor):
        source = lax.rem(me + n_tensor - offset, n_tensor)
        pltpu.make_async_remote_copy(
            src_ref=part_ref,
            dst_ref=t_held.at[source],
            send_sem=t_send.at[offset],
            recv_sem=t_recv.at[offset],
            device_id=(dp, source),
            device_id_type=MESH,
        ).wait_recv()
    total = jnp.sum(t_held[...], axis=0)
    row = lax.broadcasted_iota(jnp.int32, total.shape, 0)
    msg[...] = jnp.where(row == 0, total, jnp.where(row == 1, ids_ref[...], 0.0))
    d_held[dp] = msg[...]
    copies = []
    for offset in range(1, n_dp):
        peer = lax.rem(dp + offset, n_dp)
        copy = pltpu.make_async_remote_copy(
            src_ref=msg,
            dst_ref=d_held.at[dp],
            send_sem=d_send.at[offset],
            recv_sem=d_recv.at[offset],
            device_id=(peer, me),
            device_id_type=MESH,
        )
        copy.start()
        copies.append(copy)
    for copy in copies:
        copy.wait_send()
    for offset in range(1, n_dp):
        source = lax.rem(dp + n_dp - offset, n_dp)
        pltpu.make_async_remote_copy(
            src_ref=msg,
            dst_ref=d_held.at[source],
            send_sem=d_send.at[offset],
            recv_sem=d_recv.at[offset],
            device_id=(source, me),
            device_id_type=MESH,
        ).wait_recv()
    out_ref[...] = d_held[...]


def route(part, ids, n_tensor, n_dp):
    tile = part.shape
    return pl.pallas_call(
        lambda *refs: route_kernel(n_tensor, n_dp, *refs),
        out_shape=jax.ShapeDtypeStruct((n_dp,) + tile, jnp.float32),
        in_specs=[pl.BlockSpec(memory_space=pltpu.VMEM)] * 2,
        out_specs=pl.BlockSpec(memory_space=pltpu.VMEM),
        scratch_shapes=[
            pltpu.VMEM((n_tensor,) + tile, jnp.float32),
            pltpu.VMEM((n_dp,) + tile, jnp.float32),
            pltpu.VMEM(tile, jnp.float32),
            pltpu.SemaphoreType.DMA((n_tensor,)),
            pltpu.SemaphoreType.DMA((n_tensor,)),
            pltpu.SemaphoreType.DMA((n_dp,)),
            pltpu.SemaphoreType.DMA((n_dp,)),
        ],
        compiler_params=pltpu.CompilerParams(collective_id=1, has_side_effects=True),
    )(part, ids)


def on_device(
    hidden, norm_gain, head_weight, value_weight, token_ids, slot_mask, lengths, request_order
):
    own_rows = hidden.shape[0]
    vocab_local = head_weight.shape[1]
    n_tensor = lax.axis_size("tensor")
    n_dp = lax.axis_size("dp")
    tensor_index = lax.axis_index("tensor")
    widened = hidden.astype(jnp.float32)
    inverse_rms = lax.rsqrt(jnp.mean(widened * widened, axis=1, keepdims=True) + EPSILON)
    normed = (widened * inverse_rms * norm_gain).astype(jnp.bfloat16)
    weight_mask = slot_mask.astype(jnp.float32)
    token_value = weight_mask * jnp.dot(normed, value_weight, preferred_element_type=jnp.float32)

    columns = tensor_index * vocab_local + jnp.arange(vocab_local, dtype=jnp.int32)
    width = hidden.shape[1]
    live_sum = jnp.cumsum(slot_mask)
    slot_index = jnp.arange(own_rows, dtype=jnp.int32)
    chosen = (slot_mask[None, :] == 1) & (
        live_sum[None, :] - 1 == jnp.arange(LIVE, dtype=jnp.int32)[:, None]
    )
    source = jnp.sum(jnp.where(chosen, slot_index[None, :], 0), axis=1)
    compact_rows = jnp.take(normed, source, axis=0)
    compact_ids = jnp.take(token_ids, source)
    meta = (
        jnp.zeros((LIVE, 128), jnp.bfloat16)
        .at[:, 0].set((compact_ids // 256).astype(jnp.bfloat16))
        .at[:, 1].set((compact_ids % 256).astype(jnp.bfloat16))
    )
    block = jnp.concatenate([compact_rows, meta], axis=1)
    gathered = lax.all_gather(block, "tensor", axis=0, tiled=True)
    piece_rows = gathered[:, :width]
    meta_cols = gathered[:, width:width + 2].astype(jnp.float32)
    piece_ids = (meta_cols[:, 0] * 256.0 + meta_cols[:, 1]).astype(jnp.int32)

    logits = jnp.dot(piece_rows, head_weight, preferred_element_type=jnp.float32)
    row_peak = jnp.max(logits, axis=1)
    shifted = logits - row_peak[:, None]
    weights = jnp.exp(shifted)
    row_mass = jnp.sum(weights, axis=1)
    row_spread = jnp.sum(weights * shifted, axis=1)
    row_target = jnp.sum(jnp.where(columns[None, :] == piece_ids[:, None], logits, 0.0), axis=1)

    stats = jnp.stack([row_peak, row_mass, row_spread, row_target])
    blocks = stats.reshape(4, n_tensor, LIVE).transpose(1, 0, 2)
    parts = exchange(blocks, n_tensor)
    part_peak, part_mass, part_spread, part_target = parts[:, 0], parts[:, 1], parts[:, 2], parts[:, 3]
    peak = jnp.max(part_peak, axis=0)
    gap = part_peak - peak[None, :]
    factor = jnp.exp(gap)
    mass = jnp.sum(factor * part_mass, axis=0)
    spread = jnp.sum(factor * (part_spread + gap * part_mass), axis=0)
    target = jnp.sum(part_target, axis=0)
    log_mass = jnp.log(mass)
    place = jnp.clip(live_sum - 1, 0, LIVE - 1)
    token_logprob = weight_mask * jnp.take(target - peak - log_mass, place)
    token_entropy = weight_mask * jnp.take(log_mass - spread / mass, place)

    request_count = lengths.shape[1]
    span_lengths = lengths[0]
    span_ends = jnp.cumsum(span_lengths)
    slot_ids = tensor_index * own_rows + jnp.arange(own_rows, dtype=jnp.int32)
    position = jnp.sum((slot_ids[:, None] >= span_ends[None, :]).astype(jnp.int32), axis=1)
    onehot = position[:, None] == jnp.arange(request_count, dtype=jnp.int32)[None, :]
    by_pos = jnp.sum(jnp.where(onehot, token_logprob[:, None], 0.0), axis=0) / span_lengths.astype(
        jnp.float32
    )
    tile = jnp.zeros((8, 128), jnp.float32)
    part_tile = tile.at[0, :request_count].set(by_pos)
    ids_tile = tile.at[1, :request_count].set(request_order.astype(jnp.float32))
    routed = route(part_tile, ids_tile, n_tensor, n_dp)
    all_totals = routed[:, 0, :request_count].reshape(-1)
    all_owners = routed[:, 1, :request_count].reshape(-1)
    wanted = (lax.axis_index("dp") * request_count + jnp.arange(request_count)).astype(jnp.float32)
    route_table = all_owners[:, None] == wanted[None, :]
    request_score = jnp.sum(jnp.where(route_table, all_totals[:, None], 0.0), axis=0)
    return (token_logprob, token_entropy, token_value, request_score)


def solution(mesh):
    return jax.shard_map(
        on_device,
        mesh=mesh,
        in_specs=(
            P(("dp", "tensor"), None),
            P(),
            P(None, "tensor"),
            P(),
            P(("dp", "tensor")),
            P(("dp", "tensor")),
            P("dp", None),
            P("dp"),
        ),
        out_specs=(P(("dp", "tensor")), P(("dp", "tensor")), P(("dp", "tensor")), P("dp")),
        check_vma=False,
    )
```

```python
import jax
import jax.numpy as jnp
from jax import lax
from jax.experimental import pallas as pl
from jax.experimental.pallas import tpu as pltpu
from jax.sharding import PartitionSpec as P

EPSILON = 1e-06
MESH = pl.DeviceIdType.MESH
LIVE = 48


def exchange_kernel(n_tensor, send_ref, out_ref, held, send_sem, recv_sem):
    me = lax.axis_index("tensor")
    dp = lax.axis_index("dp")
    barrier = pltpu.get_barrier_semaphore()
    for offset in range(1, n_tensor):
        peer = lax.rem(me + offset, n_tensor)
        pl.semaphore_signal(barrier, inc=1, device_id=(dp, peer), device_id_type=MESH)
    pl.semaphore_wait(barrier, n_tensor - 1)
    held[me] = send_ref[me]
    copies = []
    for offset in range(1, n_tensor):
        peer = lax.rem(me + offset, n_tensor)
        copy = pltpu.make_async_remote_copy(
            src_ref=send_ref.at[peer],
            dst_ref=held.at[me],
            send_sem=send_sem.at[offset],
            recv_sem=recv_sem.at[offset],
            device_id=(dp, peer),
            device_id_type=MESH,
        )
        copy.start()
        copies.append(copy)
    for copy in copies:
        copy.wait_send()
    for offset in range(1, n_tensor):
        source = lax.rem(me + n_tensor - offset, n_tensor)
        pltpu.make_async_remote_copy(
            src_ref=send_ref.at[source],
            dst_ref=held.at[source],
            send_sem=send_sem.at[offset],
            recv_sem=recv_sem.at[offset],
            device_id=(dp, source),
            device_id_type=MESH,
        ).wait_recv()
    out_ref[...] = held[...]


def exchange(blocks, n_tensor):
    return pl.pallas_call(
        lambda *refs: exchange_kernel(n_tensor, *refs),
        out_shape=jax.ShapeDtypeStruct(blocks.shape, blocks.dtype),
        in_specs=[pl.BlockSpec(memory_space=pltpu.VMEM)],
        out_specs=pl.BlockSpec(memory_space=pltpu.VMEM),
        scratch_shapes=[
            pltpu.VMEM(blocks.shape, blocks.dtype),
            pltpu.SemaphoreType.DMA((n_tensor,)),
            pltpu.SemaphoreType.DMA((n_tensor,)),
        ],
        compiler_params=pltpu.CompilerParams(collective_id=0, has_side_effects=True),
    )(blocks)


def route_kernel(n_tensor, n_dp, part_ref, ids_ref, out_ref, t_held, d_held, msg,
                 t_send, t_recv, d_send, d_recv):
    me = lax.axis_index("tensor")
    dp = lax.axis_index("dp")
    barrier = pltpu.get_barrier_semaphore()
    for offset in range(1, n_tensor):
        peer = lax.rem(me + offset, n_tensor)
        pl.semaphore_signal(barrier, inc=1, device_id=(dp, peer), device_id_type=MESH)
    for offset in range(1, n_dp):
        peer = lax.rem(dp + offset, n_dp)
        pl.semaphore_signal(barrier, inc=1, device_id=(peer, me), device_id_type=MESH)
    pl.semaphore_wait(barrier, n_tensor - 1 + n_dp - 1)
    t_held[me] = part_ref[...]
    copies = []
    for offset in range(1, n_tensor):
        peer = lax.rem(me + offset, n_tensor)
        copy = pltpu.make_async_remote_copy(
            src_ref=part_ref,
            dst_ref=t_held.at[me],
            send_sem=t_send.at[offset],
            recv_sem=t_recv.at[offset],
            device_id=(dp, peer),
            device_id_type=MESH,
        )
        copy.start()
        copies.append(copy)
    for copy in copies:
        copy.wait_send()
    for offset in range(1, n_tensor):
        source = lax.rem(me + n_tensor - offset, n_tensor)
        pltpu.make_async_remote_copy(
            src_ref=part_ref,
            dst_ref=t_held.at[source],
            send_sem=t_send.at[offset],
            recv_sem=t_recv.at[offset],
            device_id=(dp, source),
            device_id_type=MESH,
        ).wait_recv()
    total = jnp.sum(t_held[...], axis=0)
    row = lax.broadcasted_iota(jnp.int32, total.shape, 0)
    msg[...] = jnp.where(row == 0, total, jnp.where(row == 1, ids_ref[...], 0.0))
    d_held[dp] = msg[...]
    copies = []
    for offset in range(1, n_dp):
        peer = lax.rem(dp + offset, n_dp)
        copy = pltpu.make_async_remote_copy(
            src_ref=msg,
            dst_ref=d_held.at[dp],
            send_sem=d_send.at[offset],
            recv_sem=d_recv.at[offset],
            device_id=(peer, me),
            device_id_type=MESH,
        )
        copy.start()
        copies.append(copy)
    for copy in copies:
        copy.wait_send()
    for offset in range(1, n_dp):
        source = lax.rem(dp + n_dp - offset, n_dp)
        pltpu.make_async_remote_copy(
            src_ref=msg,
            dst_ref=d_held.at[source],
            send_sem=d_send.at[offset],
            recv_sem=d_recv.at[offset],
            device_id=(source, me),
            device_id_type=MESH,
        ).wait_recv()
    out_ref[...] = d_held[...]


def route(part, ids, n_tensor, n_dp):
    tile = part.shape
    return pl.pallas_call(
        lambda *refs: route_kernel(n_tensor, n_dp, *refs),
        out_shape=jax.ShapeDtypeStruct((n_dp,) + tile, jnp.float32),
        in_specs=[pl.BlockSpec(memory_space=pltpu.VMEM)] * 2,
        out_specs=pl.BlockSpec(memory_space=pltpu.VMEM),
        scratch_shapes=[
            pltpu.VMEM((n_tensor,) + tile, jnp.float32),
            pltpu.VMEM((n_dp,) + tile, jnp.float32),
            pltpu.VMEM(tile, jnp.float32),
            pltpu.SemaphoreType.DMA((n_tensor,)),
            pltpu.SemaphoreType.DMA((n_tensor,)),
            pltpu.SemaphoreType.DMA((n_dp,)),
            pltpu.SemaphoreType.DMA((n_dp,)),
        ],
        compiler_params=pltpu.CompilerParams(collective_id=1, has_side_effects=True),
    )(part, ids)


def stats_kernel(x_ref, w_ref, id_ref, out_ref):
    logits = jnp.dot(x_ref[...], w_ref[...], preferred_element_type=jnp.float32)
    peak = jnp.max(logits, axis=1, keepdims=True)
    shifted = logits - peak
    weights = jnp.exp(shifted)
    mass = jnp.sum(weights, axis=1, keepdims=True)
    spread = jnp.sum(weights * shifted, axis=1, keepdims=True)
    column = lax.broadcasted_iota(jnp.int32, logits.shape, 1)
    target = jnp.sum(jnp.where(column == id_ref[...], logits, 0.0), axis=1, keepdims=True)
    lane = lax.broadcasted_iota(jnp.int32, out_ref.shape, 1)
    out_ref[...] = jnp.where(
        lane == 0, peak, jnp.where(lane == 1, mass, jnp.where(lane == 2, spread, target))
    )


def row_stats(rows, weight, local_ids, width, tile):
    count = rows.shape[0]
    depth, vocab = weight.shape
    return pl.pallas_call(
        stats_kernel,
        out_shape=jax.ShapeDtypeStruct((count, 128), jnp.float32),
        grid=(count // tile,),
        in_specs=[
            pl.BlockSpec((tile, width), lambda i: (i, 0)),
            pl.BlockSpec((depth, vocab), lambda i: (0, 0)),
            pl.BlockSpec((tile, 1), lambda i: (i, 0)),
        ],
        out_specs=pl.BlockSpec((tile, 128), lambda i: (i, 0)),
        compiler_params=pltpu.CompilerParams(vmem_limit_bytes=56 * 1024 * 1024),
        cost_estimate=pl.CostEstimate(
            flops=2 * count * depth * vocab,
            transcendentals=count * vocab,
            bytes_accessed=2 * count * width + 2 * depth * vocab + 512 * count,
        ),
    )(rows, weight, local_ids)


def on_device(
    hidden, norm_gain, head_weight, value_weight, token_ids, slot_mask, lengths, request_order
):
    own_rows = hidden.shape[0]
    vocab_local = head_weight.shape[1]
    n_tensor = lax.axis_size("tensor")
    n_dp = lax.axis_size("dp")
    tensor_index = lax.axis_index("tensor")
    widened = hidden.astype(jnp.float32)
    inverse_rms = lax.rsqrt(jnp.mean(widened * widened, axis=1, keepdims=True) + EPSILON)
    normed = (widened * inverse_rms * norm_gain).astype(jnp.bfloat16)
    weight_mask = slot_mask.astype(jnp.float32)
    token_value = weight_mask * jnp.dot(normed, value_weight, preferred_element_type=jnp.float32)

    width = hidden.shape[1]
    live_sum = jnp.cumsum(slot_mask)
    slot_index = jnp.arange(own_rows, dtype=jnp.int32)
    chosen = (slot_mask[None, :] == 1) & (
        live_sum[None, :] - 1 == jnp.arange(LIVE, dtype=jnp.int32)[:, None]
    )
    source = jnp.sum(jnp.where(chosen, slot_index[None, :], 0), axis=1)
    compact_rows = jnp.take(normed, source, axis=0)
    compact_ids = jnp.take(token_ids, source)
    meta = (
        jnp.zeros((LIVE, 128), jnp.bfloat16)
        .at[:, 0].set((compact_ids // 256).astype(jnp.bfloat16))
        .at[:, 1].set((compact_ids % 256).astype(jnp.bfloat16))
    )
    block = jnp.concatenate([compact_rows, meta], axis=1)
    gathered = lax.all_gather(block, "tensor", axis=0, tiled=True)
    meta_cols = gathered[:, width:width + 2].astype(jnp.float32)
    piece_ids = (meta_cols[:, 0] * 256.0 + meta_cols[:, 1]).astype(jnp.int32)
    local_ids = (piece_ids - tensor_index * vocab_local)[:, None]
    row_count = gathered.shape[0]
    stats = row_stats(gathered, head_weight, local_ids, width, 256 if row_count % 256 == 0 else row_count)
    blocks = stats[:, :4].reshape(n_tensor, LIVE, 4).transpose(0, 2, 1)
    parts = exchange(blocks, n_tensor)
    part_peak, part_mass, part_spread, part_target = parts[:, 0], parts[:, 1], parts[:, 2], parts[:, 3]
    peak = jnp.max(part_peak, axis=0)
    gap = part_peak - peak[None, :]
    factor = jnp.exp(gap)
    mass = jnp.sum(factor * part_mass, axis=0)
    spread = jnp.sum(factor * (part_spread + gap * part_mass), axis=0)
    target = jnp.sum(part_target, axis=0)
    log_mass = jnp.log(mass)
    place = jnp.clip(live_sum - 1, 0, LIVE - 1)
    token_logprob = weight_mask * jnp.take(target - peak - log_mass, place)
    token_entropy = weight_mask * jnp.take(log_mass - spread / mass, place)

    request_count = lengths.shape[1]
    span_lengths = lengths[0]
    span_ends = jnp.cumsum(span_lengths)
    slot_ids = tensor_index * own_rows + jnp.arange(own_rows, dtype=jnp.int32)
    position = jnp.sum((slot_ids[:, None] >= span_ends[None, :]).astype(jnp.int32), axis=1)
    onehot = position[:, None] == jnp.arange(request_count, dtype=jnp.int32)[None, :]
    by_pos = jnp.sum(jnp.where(onehot, token_logprob[:, None], 0.0), axis=0) / span_lengths.astype(
        jnp.float32
    )
    tile = jnp.zeros((8, 128), jnp.float32)
    part_tile = tile.at[0, :request_count].set(by_pos)
    ids_tile = tile.at[1, :request_count].set(request_order.astype(jnp.float32))
    routed = route(part_tile, ids_tile, n_tensor, n_dp)
    all_totals = routed[:, 0, :request_count].reshape(-1)
    all_owners = routed[:, 1, :request_count].reshape(-1)
    wanted = (lax.axis_index("dp") * request_count + jnp.arange(request_count)).astype(jnp.float32)
    route_table = all_owners[:, None] == wanted[None, :]
    request_score = jnp.sum(jnp.where(route_table, all_totals[:, None], 0.0), axis=0)
    return (token_logprob, token_entropy, token_value, request_score)


def solution(mesh):
    return jax.shard_map(
        on_device,
        mesh=mesh,
        in_specs=(
            P(("dp", "tensor"), None),
            P(),
            P(None, "tensor"),
            P(),
            P(("dp", "tensor")),
            P(("dp", "tensor")),
            P("dp", None),
            P("dp"),
        ),
        out_specs=(P(("dp", "tensor")), P(("dp", "tensor")), P(("dp", "tensor")), P("dp")),
        check_vma=False,
    )
```

```python
import jax
import jax.numpy as jnp
from jax import lax
from jax.experimental import pallas as pl
from jax.experimental.pallas import tpu as pltpu
from jax.sharding import PartitionSpec as P

EPSILON = 1e-06
MESH = pl.DeviceIdType.MESH
LIVE = 48


def exchange_kernel(n_tensor, send_ref, out_ref, held, send_sem, recv_sem):
    me = lax.axis_index("tensor")
    dp = lax.axis_index("dp")
    barrier = pltpu.get_barrier_semaphore()
    for offset in range(1, n_tensor):
        peer = lax.rem(me + offset, n_tensor)
        pl.semaphore_signal(barrier, inc=1, device_id=(dp, peer), device_id_type=MESH)
    pl.semaphore_wait(barrier, n_tensor - 1)
    held[me] = send_ref[me]
    copies = []
    for offset in range(1, n_tensor):
        peer = lax.rem(me + offset, n_tensor)
        copy = pltpu.make_async_remote_copy(
            src_ref=send_ref.at[peer],
            dst_ref=held.at[me],
            send_sem=send_sem.at[offset],
            recv_sem=recv_sem.at[offset],
            device_id=(dp, peer),
            device_id_type=MESH,
        )
        copy.start()
        copies.append(copy)
    for copy in copies:
        copy.wait_send()
    for offset in range(1, n_tensor):
        source = lax.rem(me + n_tensor - offset, n_tensor)
        pltpu.make_async_remote_copy(
            src_ref=send_ref.at[source],
            dst_ref=held.at[source],
            send_sem=send_sem.at[offset],
            recv_sem=recv_sem.at[offset],
            device_id=(dp, source),
            device_id_type=MESH,
        ).wait_recv()
    out_ref[...] = held[...]


def exchange(blocks, n_tensor):
    return pl.pallas_call(
        lambda *refs: exchange_kernel(n_tensor, *refs),
        out_shape=jax.ShapeDtypeStruct(blocks.shape, blocks.dtype),
        in_specs=[pl.BlockSpec(memory_space=pltpu.VMEM)],
        out_specs=pl.BlockSpec(memory_space=pltpu.VMEM),
        scratch_shapes=[
            pltpu.VMEM(blocks.shape, blocks.dtype),
            pltpu.SemaphoreType.DMA((n_tensor,)),
            pltpu.SemaphoreType.DMA((n_tensor,)),
        ],
        compiler_params=pltpu.CompilerParams(collective_id=0, has_side_effects=True),
    )(blocks)


def route_kernel(n_tensor, n_dp, part_ref, ids_ref, out_ref, t_held, d_held, msg,
                 t_send, t_recv, d_send, d_recv):
    me = lax.axis_index("tensor")
    dp = lax.axis_index("dp")
    barrier = pltpu.get_barrier_semaphore()
    for offset in range(1, n_tensor):
        peer = lax.rem(me + offset, n_tensor)
        pl.semaphore_signal(barrier, inc=1, device_id=(dp, peer), device_id_type=MESH)
    for offset in range(1, n_dp):
        peer = lax.rem(dp + offset, n_dp)
        pl.semaphore_signal(barrier, inc=1, device_id=(peer, me), device_id_type=MESH)
    pl.semaphore_wait(barrier, n_tensor - 1 + n_dp - 1)
    t_held[me] = part_ref[...]
    copies = []
    for offset in range(1, n_tensor):
        peer = lax.rem(me + offset, n_tensor)
        copy = pltpu.make_async_remote_copy(
            src_ref=part_ref,
            dst_ref=t_held.at[me],
            send_sem=t_send.at[offset],
            recv_sem=t_recv.at[offset],
            device_id=(dp, peer),
            device_id_type=MESH,
        )
        copy.start()
        copies.append(copy)
    for copy in copies:
        copy.wait_send()
    for offset in range(1, n_tensor):
        source = lax.rem(me + n_tensor - offset, n_tensor)
        pltpu.make_async_remote_copy(
            src_ref=part_ref,
            dst_ref=t_held.at[source],
            send_sem=t_send.at[offset],
            recv_sem=t_recv.at[offset],
            device_id=(dp, source),
            device_id_type=MESH,
        ).wait_recv()
    total = jnp.sum(t_held[...], axis=0)
    row = lax.broadcasted_iota(jnp.int32, total.shape, 0)
    msg[...] = jnp.where(row == 0, total, jnp.where(row == 1, ids_ref[...], 0.0))
    d_held[dp] = msg[...]
    copies = []
    for offset in range(1, n_dp):
        peer = lax.rem(dp + offset, n_dp)
        copy = pltpu.make_async_remote_copy(
            src_ref=msg,
            dst_ref=d_held.at[dp],
            send_sem=d_send.at[offset],
            recv_sem=d_recv.at[offset],
            device_id=(peer, me),
            device_id_type=MESH,
        )
        copy.start()
        copies.append(copy)
    for copy in copies:
        copy.wait_send()
    for offset in range(1, n_dp):
        source = lax.rem(dp + n_dp - offset, n_dp)
        pltpu.make_async_remote_copy(
            src_ref=msg,
            dst_ref=d_held.at[source],
            send_sem=d_send.at[offset],
            recv_sem=d_recv.at[offset],
            device_id=(source, me),
            device_id_type=MESH,
        ).wait_recv()
    out_ref[...] = d_held[...]


def route(part, ids, n_tensor, n_dp):
    tile = part.shape
    return pl.pallas_call(
        lambda *refs: route_kernel(n_tensor, n_dp, *refs),
        out_shape=jax.ShapeDtypeStruct((n_dp,) + tile, jnp.float32),
        in_specs=[pl.BlockSpec(memory_space=pltpu.VMEM)] * 2,
        out_specs=pl.BlockSpec(memory_space=pltpu.VMEM),
        scratch_shapes=[
            pltpu.VMEM((n_tensor,) + tile, jnp.float32),
            pltpu.VMEM((n_dp,) + tile, jnp.float32),
            pltpu.VMEM(tile, jnp.float32),
            pltpu.SemaphoreType.DMA((n_tensor,)),
            pltpu.SemaphoreType.DMA((n_tensor,)),
            pltpu.SemaphoreType.DMA((n_dp,)),
            pltpu.SemaphoreType.DMA((n_dp,)),
        ],
        compiler_params=pltpu.CompilerParams(collective_id=1, has_side_effects=True),
    )(part, ids)


def gather_kernel(n_tensor, block_ref, out_ref, send_sem, recv_sem, local_sem):
    me = lax.axis_index("tensor")
    dp = lax.axis_index("dp")
    barrier = pltpu.get_barrier_semaphore()
    for offset in range(1, n_tensor):
        peer = lax.rem(me + offset, n_tensor)
        pl.semaphore_signal(barrier, inc=1, device_id=(dp, peer), device_id_type=MESH)
    pl.semaphore_wait(barrier, n_tensor - 1)
    local = pltpu.make_async_copy(block_ref, out_ref.at[me], local_sem)
    local.start()
    copies = []
    for offset in range(1, n_tensor):
        peer = lax.rem(me + offset, n_tensor)
        copy = pltpu.make_async_remote_copy(
            src_ref=block_ref,
            dst_ref=out_ref.at[me],
            send_sem=send_sem.at[offset],
            recv_sem=recv_sem.at[offset],
            device_id=(dp, peer),
            device_id_type=MESH,
        )
        copy.start()
        copies.append(copy)
    for copy in copies:
        copy.wait_send()
    for offset in range(1, n_tensor):
        source = lax.rem(me + n_tensor - offset, n_tensor)
        pltpu.make_async_remote_copy(
            src_ref=block_ref,
            dst_ref=out_ref.at[source],
            send_sem=send_sem.at[offset],
            recv_sem=recv_sem.at[offset],
            device_id=(dp, source),
            device_id_type=MESH,
        ).wait_recv()
    local.wait()


def gather_rows(block, n_tensor):
    return pl.pallas_call(
        lambda *refs: gather_kernel(n_tensor, *refs),
        out_shape=jax.ShapeDtypeStruct((n_tensor,) + block.shape, block.dtype),
        in_specs=[pl.BlockSpec(memory_space=pl.ANY)],
        out_specs=pl.BlockSpec(memory_space=pl.ANY),
        scratch_shapes=[
            pltpu.SemaphoreType.DMA((n_tensor,)),
            pltpu.SemaphoreType.DMA((n_tensor,)),
            pltpu.SemaphoreType.DMA(()),
        ],
        compiler_params=pltpu.CompilerParams(collective_id=2, has_side_effects=True),
    )(block)


def stats_kernel(x_ref, w_ref, id_ref, out_ref):
    logits = jnp.dot(x_ref[...], w_ref[...], preferred_element_type=jnp.float32)
    peak = jnp.max(logits, axis=1, keepdims=True)
    shifted = logits - peak
    weights = jnp.exp(shifted)
    mass = jnp.sum(weights, axis=1, keepdims=True)
    spread = jnp.sum(weights * shifted, axis=1, keepdims=True)
    column = lax.broadcasted_iota(jnp.int32, logits.shape, 1)
    target = jnp.sum(jnp.where(column == id_ref[...], logits, 0.0), axis=1, keepdims=True)
    lane = lax.broadcasted_iota(jnp.int32, out_ref.shape, 1)
    out_ref[...] = jnp.where(
        lane == 0, peak, jnp.where(lane == 1, mass, jnp.where(lane == 2, spread, target))
    )


def row_stats(rows, weight, local_ids, width, tile):
    count = rows.shape[0]
    depth, vocab = weight.shape
    return pl.pallas_call(
        stats_kernel,
        out_shape=jax.ShapeDtypeStruct((count, 128), jnp.float32),
        grid=(count // tile,),
        in_specs=[
            pl.BlockSpec((tile, width), lambda i: (i, 0)),
            pl.BlockSpec((depth, vocab), lambda i: (0, 0)),
            pl.BlockSpec((tile, 1), lambda i: (i, 0)),
        ],
        out_specs=pl.BlockSpec((tile, 128), lambda i: (i, 0)),
        compiler_params=pltpu.CompilerParams(vmem_limit_bytes=56 * 1024 * 1024),
        cost_estimate=pl.CostEstimate(
            flops=2 * count * depth * vocab,
            transcendentals=count * vocab,
            bytes_accessed=2 * count * width + 2 * depth * vocab + 512 * count,
        ),
    )(rows, weight, local_ids)


def on_device(
    hidden, norm_gain, head_weight, value_weight, token_ids, slot_mask, lengths, request_order
):
    own_rows = hidden.shape[0]
    vocab_local = head_weight.shape[1]
    n_tensor = lax.axis_size("tensor")
    n_dp = lax.axis_size("dp")
    tensor_index = lax.axis_index("tensor")
    widened = hidden.astype(jnp.float32)
    inverse_rms = lax.rsqrt(jnp.mean(widened * widened, axis=1, keepdims=True) + EPSILON)
    normed = (widened * inverse_rms * norm_gain).astype(jnp.bfloat16)
    weight_mask = slot_mask.astype(jnp.float32)
    token_value = weight_mask * jnp.dot(normed, value_weight, preferred_element_type=jnp.float32)

    width = hidden.shape[1]
    live_sum = jnp.cumsum(slot_mask)
    slot_index = jnp.arange(own_rows, dtype=jnp.int32)
    chosen = (slot_mask[None, :] == 1) & (
        live_sum[None, :] - 1 == jnp.arange(LIVE, dtype=jnp.int32)[:, None]
    )
    source = jnp.sum(jnp.where(chosen, slot_index[None, :], 0), axis=1)
    compact_rows = jnp.take(normed, source, axis=0)
    compact_ids = jnp.take(token_ids, source)
    meta = (
        jnp.zeros((LIVE, 128), jnp.bfloat16)
        .at[:, 0].set((compact_ids // 256).astype(jnp.bfloat16))
        .at[:, 1].set((compact_ids % 256).astype(jnp.bfloat16))
    )
    block = jnp.concatenate([compact_rows, meta], axis=1)
    gathered = gather_rows(block, n_tensor).reshape(n_tensor * LIVE, block.shape[1])
    meta_cols = gathered[:, width:width + 2].astype(jnp.float32)
    piece_ids = (meta_cols[:, 0] * 256.0 + meta_cols[:, 1]).astype(jnp.int32)
    local_ids = (piece_ids - tensor_index * vocab_local)[:, None]
    row_count = gathered.shape[0]
    stats = row_stats(gathered, head_weight, local_ids, width, 256 if row_count % 256 == 0 else row_count)
    blocks = stats[:, :4].reshape(n_tensor, LIVE, 4).transpose(0, 2, 1)
    parts = exchange(blocks, n_tensor)
    part_peak, part_mass, part_spread, part_target = parts[:, 0], parts[:, 1], parts[:, 2], parts[:, 3]
    peak = jnp.max(part_peak, axis=0)
    gap = part_peak - peak[None, :]
    factor = jnp.exp(gap)
    mass = jnp.sum(factor * part_mass, axis=0)
    spread = jnp.sum(factor * (part_spread + gap * part_mass), axis=0)
    target = jnp.sum(part_target, axis=0)
    log_mass = jnp.log(mass)
    place = jnp.clip(live_sum - 1, 0, LIVE - 1)
    token_logprob = weight_mask * jnp.take(target - peak - log_mass, place)
    token_entropy = weight_mask * jnp.take(log_mass - spread / mass, place)

    request_count = lengths.shape[1]
    span_lengths = lengths[0]
    span_ends = jnp.cumsum(span_lengths)
    slot_ids = tensor_index * own_rows + jnp.arange(own_rows, dtype=jnp.int32)
    position = jnp.sum((slot_ids[:, None] >= span_ends[None, :]).astype(jnp.int32), axis=1)
    onehot = position[:, None] == jnp.arange(request_count, dtype=jnp.int32)[None, :]
    by_pos = jnp.sum(jnp.where(onehot, token_logprob[:, None], 0.0), axis=0) / span_lengths.astype(
        jnp.float32
    )
    tile = jnp.zeros((8, 128), jnp.float32)
    part_tile = tile.at[0, :request_count].set(by_pos)
    ids_tile = tile.at[1, :request_count].set(request_order.astype(jnp.float32))
    routed = route(part_tile, ids_tile, n_tensor, n_dp)
    all_totals = routed[:, 0, :request_count].reshape(-1)
    all_owners = routed[:, 1, :request_count].reshape(-1)
    wanted = (lax.axis_index("dp") * request_count + jnp.arange(request_count)).astype(jnp.float32)
    route_table = all_owners[:, None] == wanted[None, :]
    request_score = jnp.sum(jnp.where(route_table, all_totals[:, None], 0.0), axis=0)
    return (token_logprob, token_entropy, token_value, request_score)


def solution(mesh):
    return jax.shard_map(
        on_device,
        mesh=mesh,
        in_specs=(
            P(("dp", "tensor"), None),
            P(),
            P(None, "tensor"),
            P(),
            P(("dp", "tensor")),
            P(("dp", "tensor")),
            P("dp", None),
            P("dp"),
        ),
        out_specs=(P(("dp", "tensor")), P(("dp", "tensor")), P(("dp", "tensor")), P("dp")),
        check_vma=False,
    )
```

```python
import jax
import jax.numpy as jnp
from jax import lax
from jax.experimental import pallas as pl
from jax.experimental.pallas import tpu as pltpu
from jax.sharding import PartitionSpec as P

EPSILON = 1e-06
MESH = pl.DeviceIdType.MESH
LIVE = 48


def exchange_kernel(n_tensor, send_ref, out_ref, held, send_sem, recv_sem):
    me = lax.axis_index("tensor")
    dp = lax.axis_index("dp")
    barrier = pltpu.get_barrier_semaphore()
    for offset in range(1, n_tensor):
        peer = lax.rem(me + offset, n_tensor)
        pl.semaphore_signal(barrier, inc=1, device_id=(dp, peer), device_id_type=MESH)
    pl.semaphore_wait(barrier, n_tensor - 1)
    held[me] = send_ref[me]
    copies = []
    for offset in range(1, n_tensor):
        peer = lax.rem(me + offset, n_tensor)
        copy = pltpu.make_async_remote_copy(
            src_ref=send_ref.at[peer],
            dst_ref=held.at[me],
            send_sem=send_sem.at[offset],
            recv_sem=recv_sem.at[offset],
            device_id=(dp, peer),
            device_id_type=MESH,
        )
        copy.start()
        copies.append(copy)
    for copy in copies:
        copy.wait_send()
    for offset in range(1, n_tensor):
        source = lax.rem(me + n_tensor - offset, n_tensor)
        pltpu.make_async_remote_copy(
            src_ref=send_ref.at[source],
            dst_ref=held.at[source],
            send_sem=send_sem.at[offset],
            recv_sem=recv_sem.at[offset],
            device_id=(dp, source),
            device_id_type=MESH,
        ).wait_recv()
    out_ref[...] = held[...]


def exchange(blocks, n_tensor):
    return pl.pallas_call(
        lambda *refs: exchange_kernel(n_tensor, *refs),
        out_shape=jax.ShapeDtypeStruct(blocks.shape, blocks.dtype),
        in_specs=[pl.BlockSpec(memory_space=pltpu.VMEM)],
        out_specs=pl.BlockSpec(memory_space=pltpu.VMEM),
        scratch_shapes=[
            pltpu.VMEM(blocks.shape, blocks.dtype),
            pltpu.SemaphoreType.DMA((n_tensor,)),
            pltpu.SemaphoreType.DMA((n_tensor,)),
        ],
        compiler_params=pltpu.CompilerParams(collective_id=0, has_side_effects=True),
    )(blocks)


def route_kernel(n_tensor, n_dp, part_ref, ids_ref, out_ref, t_held, d_held, msg,
                 t_send, t_recv, d_send, d_recv):
    me = lax.axis_index("tensor")
    dp = lax.axis_index("dp")
    barrier = pltpu.get_barrier_semaphore()
    for offset in range(1, n_tensor):
        peer = lax.rem(me + offset, n_tensor)
        pl.semaphore_signal(barrier, inc=1, device_id=(dp, peer), device_id_type=MESH)
    for offset in range(1, n_dp):
        peer = lax.rem(dp + offset, n_dp)
        pl.semaphore_signal(barrier, inc=1, device_id=(peer, me), device_id_type=MESH)
    pl.semaphore_wait(barrier, n_tensor - 1 + n_dp - 1)
    t_held[me] = part_ref[...]
    copies = []
    for offset in range(1, n_tensor):
        peer = lax.rem(me + offset, n_tensor)
        copy = pltpu.make_async_remote_copy(
            src_ref=part_ref,
            dst_ref=t_held.at[me],
            send_sem=t_send.at[offset],
            recv_sem=t_recv.at[offset],
            device_id=(dp, peer),
            device_id_type=MESH,
        )
        copy.start()
        copies.append(copy)
    for copy in copies:
        copy.wait_send()
    for offset in range(1, n_tensor):
        source = lax.rem(me + n_tensor - offset, n_tensor)
        pltpu.make_async_remote_copy(
            src_ref=part_ref,
            dst_ref=t_held.at[source],
            send_sem=t_send.at[offset],
            recv_sem=t_recv.at[offset],
            device_id=(dp, source),
            device_id_type=MESH,
        ).wait_recv()
    total = jnp.sum(t_held[...], axis=0)
    row = lax.broadcasted_iota(jnp.int32, total.shape, 0)
    msg[...] = jnp.where(row == 0, total, jnp.where(row == 1, ids_ref[...], 0.0))
    d_held[dp] = msg[...]
    copies = []
    for offset in range(1, n_dp):
        peer = lax.rem(dp + offset, n_dp)
        copy = pltpu.make_async_remote_copy(
            src_ref=msg,
            dst_ref=d_held.at[dp],
            send_sem=d_send.at[offset],
            recv_sem=d_recv.at[offset],
            device_id=(peer, me),
            device_id_type=MESH,
        )
        copy.start()
        copies.append(copy)
    for copy in copies:
        copy.wait_send()
    for offset in range(1, n_dp):
        source = lax.rem(dp + n_dp - offset, n_dp)
        pltpu.make_async_remote_copy(
            src_ref=msg,
            dst_ref=d_held.at[source],
            send_sem=d_send.at[offset],
            recv_sem=d_recv.at[offset],
            device_id=(source, me),
            device_id_type=MESH,
        ).wait_recv()
    out_ref[...] = d_held[...]


def route(part, ids, n_tensor, n_dp):
    tile = part.shape
    return pl.pallas_call(
        lambda *refs: route_kernel(n_tensor, n_dp, *refs),
        out_shape=jax.ShapeDtypeStruct((n_dp,) + tile, jnp.float32),
        in_specs=[pl.BlockSpec(memory_space=pltpu.VMEM)] * 2,
        out_specs=pl.BlockSpec(memory_space=pltpu.VMEM),
        scratch_shapes=[
            pltpu.VMEM((n_tensor,) + tile, jnp.float32),
            pltpu.VMEM((n_dp,) + tile, jnp.float32),
            pltpu.VMEM(tile, jnp.float32),
            pltpu.SemaphoreType.DMA((n_tensor,)),
            pltpu.SemaphoreType.DMA((n_tensor,)),
            pltpu.SemaphoreType.DMA((n_dp,)),
            pltpu.SemaphoreType.DMA((n_dp,)),
        ],
        compiler_params=pltpu.CompilerParams(collective_id=1, has_side_effects=True),
    )(part, ids)


def finish_kernel(n_tensor, n_dp, send_ref, span_ref, ids_ref, own_ref, routed_ref,
                  held, t_held, d_held, part_msg, route_msg,
                  a_send, a_recv, t_send, t_recv, d_send, d_recv):
    me = lax.axis_index("tensor")
    dp = lax.axis_index("dp")
    barrier = pltpu.get_barrier_semaphore()
    for offset in range(1, n_tensor):
        peer = lax.rem(me + offset, n_tensor)
        pl.semaphore_signal(barrier, inc=1, device_id=(dp, peer), device_id_type=MESH)
    for offset in range(1, n_dp):
        peer = lax.rem(dp + offset, n_dp)
        pl.semaphore_signal(barrier, inc=1, device_id=(peer, me), device_id_type=MESH)
    pl.semaphore_wait(barrier, n_tensor - 1 + n_dp - 1)

    held[me] = send_ref[me]
    copies = []
    for offset in range(1, n_tensor):
        peer = lax.rem(me + offset, n_tensor)
        copy = pltpu.make_async_remote_copy(
            src_ref=send_ref.at[peer], dst_ref=held.at[me],
            send_sem=a_send.at[offset], recv_sem=a_recv.at[offset],
            device_id=(dp, peer), device_id_type=MESH,
        )
        copy.start()
        copies.append(copy)
    for copy in copies:
        copy.wait_send()
    for offset in range(1, n_tensor):
        source = lax.rem(me + n_tensor - offset, n_tensor)
        pltpu.make_async_remote_copy(
            src_ref=send_ref.at[source], dst_ref=held.at[source],
            send_sem=a_send.at[offset], recv_sem=a_recv.at[offset],
            device_id=(dp, source), device_id_type=MESH,
        ).wait_recv()

    lanes = held.shape[2]
    peak = lax.fori_loop(
        0, n_tensor, lambda p, m: jnp.maximum(m, held[p][0:1, :]),
        jnp.full((1, lanes), -jnp.inf, jnp.float32),
    )

    def gather_sums(p, sums):
        mass, spread, target = sums
        block = held[p]
        gap = block[0:1, :] - peak
        factor = jnp.exp(gap)
        mass = mass + factor * block[1:2, :]
        spread = spread + factor * (block[2:3, :] + gap * block[1:2, :])
        return mass, spread, target + block[3:4, :]

    zero = jnp.zeros((1, lanes), jnp.float32)
    mass, spread, target = lax.fori_loop(0, n_tensor, gather_sums, (zero, zero, zero))
    log_mass = jnp.log(mass)
    logprob = target - peak - log_mass
    entropy = log_mass - spread / mass
    row = lax.broadcasted_iota(jnp.int32, own_ref.shape, 0)
    own_ref[...] = jnp.where(row == 0, logprob, jnp.where(row == 1, entropy, 0.0))

    spans = span_ref[...]
    partial = jnp.sum(spans[:, :lanes] * logprob, axis=1, keepdims=True) / spans[:, 127:128]
    part_msg[...] = jnp.broadcast_to(partial, part_msg.shape)
    t_held[me] = part_msg[...]
    copies = []
    for offset in range(1, n_tensor):
        peer = lax.rem(me + offset, n_tensor)
        copy = pltpu.make_async_remote_copy(
            src_ref=part_msg, dst_ref=t_held.at[me],
            send_sem=t_send.at[offset], recv_sem=t_recv.at[offset],
            device_id=(dp, peer), device_id_type=MESH,
        )
        copy.start()
        copies.append(copy)
    for copy in copies:
        copy.wait_send()
    for offset in range(1, n_tensor):
        source = lax.rem(me + n_tensor - offset, n_tensor)
        pltpu.make_async_remote_copy(
            src_ref=part_msg, dst_ref=t_held.at[source],
            send_sem=t_send.at[offset], recv_sem=t_recv.at[offset],
            device_id=(dp, source), device_id_type=MESH,
        ).wait_recv()

    total = jnp.sum(t_held[...], axis=0)
    lane = lax.broadcasted_iota(jnp.int32, total.shape, 1)
    route_msg[...] = jnp.where(lane == 0, total, jnp.where(lane == 1, ids_ref[...], 0.0))
    d_held[dp] = route_msg[...]
    copies = []
    for offset in range(1, n_dp):
        peer = lax.rem(dp + offset, n_dp)
        copy = pltpu.make_async_remote_copy(
            src_ref=route_msg, dst_ref=d_held.at[dp],
            send_sem=d_send.at[offset], recv_sem=d_recv.at[offset],
            device_id=(peer, me), device_id_type=MESH,
        )
        copy.start()
        copies.append(copy)
    for copy in copies:
        copy.wait_send()
    for offset in range(1, n_dp):
        source = lax.rem(dp + n_dp - offset, n_dp)
        pltpu.make_async_remote_copy(
            src_ref=route_msg, dst_ref=d_held.at[source],
            send_sem=d_send.at[offset], recv_sem=d_recv.at[offset],
            device_id=(source, me), device_id_type=MESH,
        ).wait_recv()
    routed_ref[...] = d_held[...]


def finish(blocks, spans, ids, n_tensor, n_dp):
    tile = spans.shape
    lanes = blocks.shape[2]
    return pl.pallas_call(
        lambda *refs: finish_kernel(n_tensor, n_dp, *refs),
        out_shape=(
            jax.ShapeDtypeStruct((8, lanes), jnp.float32),
            jax.ShapeDtypeStruct((n_dp,) + tile, jnp.float32),
        ),
        in_specs=[pl.BlockSpec(memory_space=pltpu.VMEM)] * 3,
        out_specs=(pl.BlockSpec(memory_space=pltpu.VMEM), pl.BlockSpec(memory_space=pltpu.VMEM)),
        scratch_shapes=[
            pltpu.VMEM(blocks.shape, jnp.float32),
            pltpu.VMEM((n_tensor,) + tile, jnp.float32),
            pltpu.VMEM((n_dp,) + tile, jnp.float32),
            pltpu.VMEM(tile, jnp.float32),
            pltpu.VMEM(tile, jnp.float32),
            pltpu.SemaphoreType.DMA((n_tensor,)),
            pltpu.SemaphoreType.DMA((n_tensor,)),
            pltpu.SemaphoreType.DMA((n_tensor,)),
            pltpu.SemaphoreType.DMA((n_tensor,)),
            pltpu.SemaphoreType.DMA((n_dp,)),
            pltpu.SemaphoreType.DMA((n_dp,)),
        ],
        compiler_params=pltpu.CompilerParams(collective_id=3, has_side_effects=True),
    )(blocks, spans, ids)


def stats_kernel(x_ref, w_ref, id_ref, out_ref):
    logits = jnp.dot(x_ref[...], w_ref[...], preferred_element_type=jnp.float32)
    peak = jnp.max(logits, axis=1, keepdims=True)
    shifted = logits - peak
    weights = jnp.exp(shifted)
    mass = jnp.sum(weights, axis=1, keepdims=True)
    spread = jnp.sum(weights * shifted, axis=1, keepdims=True)
    column = lax.broadcasted_iota(jnp.int32, logits.shape, 1)
    target = jnp.sum(jnp.where(column == id_ref[...], logits, 0.0), axis=1, keepdims=True)
    lane = lax.broadcasted_iota(jnp.int32, out_ref.shape, 1)
    out_ref[...] = jnp.where(
        lane == 0, peak, jnp.where(lane == 1, mass, jnp.where(lane == 2, spread, target))
    )


def row_stats(rows, weight, local_ids, width, tile):
    count = rows.shape[0]
    depth, vocab = weight.shape
    return pl.pallas_call(
        stats_kernel,
        out_shape=jax.ShapeDtypeStruct((count, 128), jnp.float32),
        grid=(count // tile,),
        in_specs=[
            pl.BlockSpec((tile, width), lambda i: (i, 0)),
            pl.BlockSpec((depth, vocab), lambda i: (0, 0)),
            pl.BlockSpec((tile, 1), lambda i: (i, 0)),
        ],
        out_specs=pl.BlockSpec((tile, 128), lambda i: (i, 0)),
        compiler_params=pltpu.CompilerParams(vmem_limit_bytes=56 * 1024 * 1024),
        cost_estimate=pl.CostEstimate(
            flops=2 * count * depth * vocab,
            transcendentals=count * vocab,
            bytes_accessed=2 * count * width + 2 * depth * vocab + 512 * count,
        ),
    )(rows, weight, local_ids)


def on_device(
    hidden, norm_gain, head_weight, value_weight, token_ids, slot_mask, lengths, request_order
):
    own_rows = hidden.shape[0]
    vocab_local = head_weight.shape[1]
    n_tensor = lax.axis_size("tensor")
    n_dp = lax.axis_size("dp")
    tensor_index = lax.axis_index("tensor")
    widened = hidden.astype(jnp.float32)
    inverse_rms = lax.rsqrt(jnp.mean(widened * widened, axis=1, keepdims=True) + EPSILON)
    normed = (widened * inverse_rms * norm_gain).astype(jnp.bfloat16)
    weight_mask = slot_mask.astype(jnp.float32)
    token_value = weight_mask * jnp.dot(normed, value_weight, preferred_element_type=jnp.float32)

    width = hidden.shape[1]
    live_sum = jnp.cumsum(slot_mask)
    slot_index = jnp.arange(own_rows, dtype=jnp.int32)
    chosen = (slot_mask[None, :] == 1) & (
        live_sum[None, :] - 1 == jnp.arange(LIVE, dtype=jnp.int32)[:, None]
    )
    source = jnp.sum(jnp.where(chosen, slot_index[None, :], 0), axis=1)
    compact_rows = jnp.take(normed, source, axis=0)
    compact_ids = jnp.take(token_ids, source)
    meta = (
        jnp.zeros((LIVE, 128), jnp.bfloat16)
        .at[:, 0].set((compact_ids // 256).astype(jnp.bfloat16))
        .at[:, 1].set((compact_ids % 256).astype(jnp.bfloat16))
    )
    block = jnp.concatenate([compact_rows, meta], axis=1)
    gathered = lax.all_gather(block, "tensor", axis=0, tiled=True)
    meta_cols = gathered[:, width:width + 2].astype(jnp.float32)
    piece_ids = (meta_cols[:, 0] * 256.0 + meta_cols[:, 1]).astype(jnp.int32)
    local_ids = (piece_ids - tensor_index * vocab_local)[:, None]
    row_count = gathered.shape[0]
    stats = row_stats(gathered, head_weight, local_ids, width, 256 if row_count % 256 == 0 else row_count)
    blocks = stats[:, :4].reshape(n_tensor, LIVE, 4).transpose(0, 2, 1)
    request_count = lengths.shape[1]
    span_lengths = lengths[0]
    span_ends = jnp.cumsum(span_lengths)
    slot_ids = tensor_index * own_rows + source
    position = jnp.sum((slot_ids[:, None] >= span_ends[None, :]).astype(jnp.int32), axis=1)
    live = jnp.arange(LIVE, dtype=jnp.int32) < live_sum[-1]
    member = (position[None, :] == jnp.arange(8, dtype=jnp.int32)[:, None]) & live[None, :]
    spans = (
        jnp.zeros((8, 128), jnp.float32)
        .at[:, :LIVE].set(member.astype(jnp.float32))
        .at[:, 127].set(jnp.ones((8,), jnp.float32).at[:request_count].set(span_lengths.astype(jnp.float32)))
    )
    ids_tile = jnp.zeros((8, 128), jnp.float32).at[:request_count, 1].set(request_order.astype(jnp.float32))
    own, routed = finish(blocks, spans, ids_tile, n_tensor, n_dp)
    place = jnp.clip(live_sum - 1, 0, LIVE - 1)
    token_logprob = weight_mask * jnp.take(own[0], place)
    token_entropy = weight_mask * jnp.take(own[1], place)
    all_totals = routed[:, :request_count, 0].reshape(-1)
    all_owners = routed[:, :request_count, 1].reshape(-1)
    wanted = (lax.axis_index("dp") * request_count + jnp.arange(request_count)).astype(jnp.float32)
    route_table = all_owners[:, None] == wanted[None, :]
    request_score = jnp.sum(jnp.where(route_table, all_totals[:, None], 0.0), axis=0)
    return (token_logprob, token_entropy, token_value, request_score)


def solution(mesh):
    return jax.shard_map(
        on_device,
        mesh=mesh,
        in_specs=(
            P(("dp", "tensor"), None),
            P(),
            P(None, "tensor"),
            P(),
            P(("dp", "tensor")),
            P(("dp", "tensor")),
            P("dp", None),
            P("dp"),
        ),
        out_specs=(P(("dp", "tensor")), P(("dp", "tensor")), P(("dp", "tensor")), P("dp")),
        check_vma=False,
    )
```

```python
import jax
import jax.numpy as jnp
from jax import lax
from jax.experimental import pallas as pl
from jax.experimental.pallas import tpu as pltpu
from jax.sharding import PartitionSpec as P

EPSILON = 1e-06
MESH = pl.DeviceIdType.MESH
LIVE = 48


def exchange_kernel(n_tensor, send_ref, out_ref, held, send_sem, recv_sem):
    me = lax.axis_index("tensor")
    dp = lax.axis_index("dp")
    barrier = pltpu.get_barrier_semaphore()
    for offset in range(1, n_tensor):
        peer = lax.rem(me + offset, n_tensor)
        pl.semaphore_signal(barrier, inc=1, device_id=(dp, peer), device_id_type=MESH)
    pl.semaphore_wait(barrier, n_tensor - 1)
    held[me] = send_ref[me]
    copies = []
    for offset in range(1, n_tensor):
        peer = lax.rem(me + offset, n_tensor)
        copy = pltpu.make_async_remote_copy(
            src_ref=send_ref.at[peer],
            dst_ref=held.at[me],
            send_sem=send_sem.at[offset],
            recv_sem=recv_sem.at[offset],
            device_id=(dp, peer),
            device_id_type=MESH,
        )
        copy.start()
        copies.append(copy)
    for copy in copies:
        copy.wait_send()
    for offset in range(1, n_tensor):
        source = lax.rem(me + n_tensor - offset, n_tensor)
        pltpu.make_async_remote_copy(
            src_ref=send_ref.at[source],
            dst_ref=held.at[source],
            send_sem=send_sem.at[offset],
            recv_sem=recv_sem.at[offset],
            device_id=(dp, source),
            device_id_type=MESH,
        ).wait_recv()
    out_ref[...] = held[...]


def exchange(blocks, n_tensor):
    return pl.pallas_call(
        lambda *refs: exchange_kernel(n_tensor, *refs),
        out_shape=jax.ShapeDtypeStruct(blocks.shape, blocks.dtype),
        in_specs=[pl.BlockSpec(memory_space=pltpu.VMEM)],
        out_specs=pl.BlockSpec(memory_space=pltpu.VMEM),
        scratch_shapes=[
            pltpu.VMEM(blocks.shape, blocks.dtype),
            pltpu.SemaphoreType.DMA((n_tensor,)),
            pltpu.SemaphoreType.DMA((n_tensor,)),
        ],
        compiler_params=pltpu.CompilerParams(collective_id=0, has_side_effects=True),
    )(blocks)


def route_kernel(n_tensor, n_dp, part_ref, ids_ref, out_ref, t_held, d_held, msg,
                 t_send, t_recv, d_send, d_recv):
    me = lax.axis_index("tensor")
    dp = lax.axis_index("dp")
    barrier = pltpu.get_barrier_semaphore()
    for offset in range(1, n_tensor):
        peer = lax.rem(me + offset, n_tensor)
        pl.semaphore_signal(barrier, inc=1, device_id=(dp, peer), device_id_type=MESH)
    for offset in range(1, n_dp):
        peer = lax.rem(dp + offset, n_dp)
        pl.semaphore_signal(barrier, inc=1, device_id=(peer, me), device_id_type=MESH)
    pl.semaphore_wait(barrier, n_tensor - 1 + n_dp - 1)
    t_held[me] = part_ref[...]
    copies = []
    for offset in range(1, n_tensor):
        peer = lax.rem(me + offset, n_tensor)
        copy = pltpu.make_async_remote_copy(
            src_ref=part_ref,
            dst_ref=t_held.at[me],
            send_sem=t_send.at[offset],
            recv_sem=t_recv.at[offset],
            device_id=(dp, peer),
            device_id_type=MESH,
        )
        copy.start()
        copies.append(copy)
    for copy in copies:
        copy.wait_send()
    for offset in range(1, n_tensor):
        source = lax.rem(me + n_tensor - offset, n_tensor)
        pltpu.make_async_remote_copy(
            src_ref=part_ref,
            dst_ref=t_held.at[source],
            send_sem=t_send.at[offset],
            recv_sem=t_recv.at[offset],
            device_id=(dp, source),
            device_id_type=MESH,
        ).wait_recv()
    total = jnp.sum(t_held[...], axis=0)
    row = lax.broadcasted_iota(jnp.int32, total.shape, 0)
    msg[...] = jnp.where(row == 0, total, jnp.where(row == 1, ids_ref[...], 0.0))
    d_held[dp] = msg[...]
    copies = []
    for offset in range(1, n_dp):
        peer = lax.rem(dp + offset, n_dp)
        copy = pltpu.make_async_remote_copy(
            src_ref=msg,
            dst_ref=d_held.at[dp],
            send_sem=d_send.at[offset],
            recv_sem=d_recv.at[offset],
            device_id=(peer, me),
            device_id_type=MESH,
        )
        copy.start()
        copies.append(copy)
    for copy in copies:
        copy.wait_send()
    for offset in range(1, n_dp):
        source = lax.rem(dp + n_dp - offset, n_dp)
        pltpu.make_async_remote_copy(
            src_ref=msg,
            dst_ref=d_held.at[source],
            send_sem=d_send.at[offset],
            recv_sem=d_recv.at[offset],
            device_id=(source, me),
            device_id_type=MESH,
        ).wait_recv()
    out_ref[...] = d_held[...]


def route(part, ids, n_tensor, n_dp):
    tile = part.shape
    return pl.pallas_call(
        lambda *refs: route_kernel(n_tensor, n_dp, *refs),
        out_shape=jax.ShapeDtypeStruct((n_dp,) + tile, jnp.float32),
        in_specs=[pl.BlockSpec(memory_space=pltpu.VMEM)] * 2,
        out_specs=pl.BlockSpec(memory_space=pltpu.VMEM),
        scratch_shapes=[
            pltpu.VMEM((n_tensor,) + tile, jnp.float32),
            pltpu.VMEM((n_dp,) + tile, jnp.float32),
            pltpu.VMEM(tile, jnp.float32),
            pltpu.SemaphoreType.DMA((n_tensor,)),
            pltpu.SemaphoreType.DMA((n_tensor,)),
            pltpu.SemaphoreType.DMA((n_dp,)),
            pltpu.SemaphoreType.DMA((n_dp,)),
        ],
        compiler_params=pltpu.CompilerParams(collective_id=1, has_side_effects=True),
    )(part, ids)


def finish_kernel(n_tensor, n_dp, send_ref, span_ref, ids_ref, own_ref, routed_ref,
                  held, t_held, d_held, part_msg, route_msg,
                  a_send, a_recv, t_send, t_recv, d_send, d_recv):
    me = lax.axis_index("tensor")
    dp = lax.axis_index("dp")
    barrier = pltpu.get_barrier_semaphore()
    for offset in range(1, n_tensor):
        peer = lax.rem(me + offset, n_tensor)
        pl.semaphore_signal(barrier, inc=1, device_id=(dp, peer), device_id_type=MESH)
    for offset in range(1, n_dp):
        peer = lax.rem(dp + offset, n_dp)
        pl.semaphore_signal(barrier, inc=1, device_id=(peer, me), device_id_type=MESH)
    pl.semaphore_wait(barrier, n_tensor - 1 + n_dp - 1)

    held[me] = send_ref[me]
    copies = []
    for offset in range(1, n_tensor):
        peer = lax.rem(me + offset, n_tensor)
        copy = pltpu.make_async_remote_copy(
            src_ref=send_ref.at[peer], dst_ref=held.at[me],
            send_sem=a_send.at[offset], recv_sem=a_recv.at[offset],
            device_id=(dp, peer), device_id_type=MESH,
        )
        copy.start()
        copies.append(copy)
    for copy in copies:
        copy.wait_send()
    for offset in range(1, n_tensor):
        source = lax.rem(me + n_tensor - offset, n_tensor)
        pltpu.make_async_remote_copy(
            src_ref=send_ref.at[source], dst_ref=held.at[source],
            send_sem=a_send.at[offset], recv_sem=a_recv.at[offset],
            device_id=(dp, source), device_id_type=MESH,
        ).wait_recv()

    lanes = held.shape[2]
    peak = lax.fori_loop(
        0, n_tensor, lambda p, m: jnp.maximum(m, held[p][0:1, :]),
        jnp.full((1, lanes), -jnp.inf, jnp.float32),
    )

    def gather_sums(p, sums):
        mass, spread, target = sums
        block = held[p]
        gap = block[0:1, :] - peak
        factor = jnp.exp(gap)
        mass = mass + factor * block[1:2, :]
        spread = spread + factor * (block[2:3, :] + gap * block[1:2, :])
        return mass, spread, target + block[3:4, :]

    zero = jnp.zeros((1, lanes), jnp.float32)
    mass, spread, target = lax.fori_loop(0, n_tensor, gather_sums, (zero, zero, zero))
    log_mass = jnp.log(mass)
    logprob = target - peak - log_mass
    entropy = log_mass - spread / mass
    row = lax.broadcasted_iota(jnp.int32, own_ref.shape, 0)
    own_ref[...] = jnp.where(row == 0, logprob, jnp.where(row == 1, entropy, 0.0))

    spans = span_ref[...]
    partial = jnp.sum(spans[:, :lanes] * logprob, axis=1, keepdims=True) / spans[:, 127:128]
    part_msg[...] = jnp.broadcast_to(partial, part_msg.shape)
    t_held[me] = part_msg[...]
    copies = []
    for offset in range(1, n_tensor):
        peer = lax.rem(me + offset, n_tensor)
        copy = pltpu.make_async_remote_copy(
            src_ref=part_msg, dst_ref=t_held.at[me],
            send_sem=t_send.at[offset], recv_sem=t_recv.at[offset],
            device_id=(dp, peer), device_id_type=MESH,
        )
        copy.start()
        copies.append(copy)
    for copy in copies:
        copy.wait_send()
    for offset in range(1, n_tensor):
        source = lax.rem(me + n_tensor - offset, n_tensor)
        pltpu.make_async_remote_copy(
            src_ref=part_msg, dst_ref=t_held.at[source],
            send_sem=t_send.at[offset], recv_sem=t_recv.at[offset],
            device_id=(dp, source), device_id_type=MESH,
        ).wait_recv()

    total = jnp.sum(t_held[...], axis=0)
    lane = lax.broadcasted_iota(jnp.int32, total.shape, 1)
    route_msg[...] = jnp.where(lane == 0, total, jnp.where(lane == 1, ids_ref[...], 0.0))
    d_held[dp] = route_msg[...]
    copies = []
    for offset in range(1, n_dp):
        peer = lax.rem(dp + offset, n_dp)
        copy = pltpu.make_async_remote_copy(
            src_ref=route_msg, dst_ref=d_held.at[dp],
            send_sem=d_send.at[offset], recv_sem=d_recv.at[offset],
            device_id=(peer, me), device_id_type=MESH,
        )
        copy.start()
        copies.append(copy)
    for copy in copies:
        copy.wait_send()
    for offset in range(1, n_dp):
        source = lax.rem(dp + n_dp - offset, n_dp)
        pltpu.make_async_remote_copy(
            src_ref=route_msg, dst_ref=d_held.at[source],
            send_sem=d_send.at[offset], recv_sem=d_recv.at[offset],
            device_id=(source, me), device_id_type=MESH,
        ).wait_recv()
    routed_ref[...] = d_held[...]


def finish(blocks, spans, ids, n_tensor, n_dp):
    tile = spans.shape
    lanes = blocks.shape[2]
    return pl.pallas_call(
        lambda *refs: finish_kernel(n_tensor, n_dp, *refs),
        out_shape=(
            jax.ShapeDtypeStruct((8, lanes), jnp.float32),
            jax.ShapeDtypeStruct((n_dp,) + tile, jnp.float32),
        ),
        in_specs=[pl.BlockSpec(memory_space=pltpu.VMEM)] * 3,
        out_specs=(pl.BlockSpec(memory_space=pltpu.VMEM), pl.BlockSpec(memory_space=pltpu.VMEM)),
        scratch_shapes=[
            pltpu.VMEM(blocks.shape, jnp.float32),
            pltpu.VMEM((n_tensor,) + tile, jnp.float32),
            pltpu.VMEM((n_dp,) + tile, jnp.float32),
            pltpu.VMEM(tile, jnp.float32),
            pltpu.VMEM(tile, jnp.float32),
            pltpu.SemaphoreType.DMA((n_tensor,)),
            pltpu.SemaphoreType.DMA((n_tensor,)),
            pltpu.SemaphoreType.DMA((n_tensor,)),
            pltpu.SemaphoreType.DMA((n_tensor,)),
            pltpu.SemaphoreType.DMA((n_dp,)),
            pltpu.SemaphoreType.DMA((n_dp,)),
        ],
        compiler_params=pltpu.CompilerParams(collective_id=3, has_side_effects=True),
    )(blocks, spans, ids)


def prep_kernel(hidden_ref, gain_ref, mask_ref, ids_ref, out_ref):
    width = hidden_ref.shape[1]
    own_rows = hidden_ref.shape[0]
    widened = hidden_ref[...].astype(jnp.float32)
    inverse_rms = lax.rsqrt(jnp.mean(widened * widened, axis=1, keepdims=True) + EPSILON)
    normed = (widened * inverse_rms * gain_ref[...]).astype(jnp.bfloat16)
    live = jnp.broadcast_to(mask_ref[...].astype(jnp.float32), (8, own_rows))
    upper = (
        lax.broadcasted_iota(jnp.int32, (own_rows, own_rows), 0)
        <= lax.broadcasted_iota(jnp.int32, (own_rows, own_rows), 1)
    ).astype(jnp.float32)
    live_sum = jnp.dot(live, upper, preferred_element_type=jnp.float32)[0:1, :]
    rank = lax.broadcasted_iota(jnp.int32, (LIVE, own_rows), 0).astype(jnp.float32)
    chosen = ((live[0:1, :] == 1.0) & (live_sum - 1.0 == rank)).astype(jnp.bfloat16)
    out_ref[:, :width] = jnp.dot(chosen, normed, preferred_element_type=jnp.float32).astype(jnp.bfloat16)
    ids = ids_ref[...]
    high = lax.shift_right_logical(ids, 8).astype(jnp.float32)
    low = jnp.bitwise_and(ids, 255).astype(jnp.float32)
    row = lax.broadcasted_iota(jnp.int32, (128, own_rows), 0)
    meta_in = jnp.where(row == 0, high, jnp.where(row == 1, low, 0.0)).astype(jnp.bfloat16)
    meta = lax.dot_general(
        chosen, meta_in, (((1,), (1,)), ((), ())), preferred_element_type=jnp.float32
    )
    out_ref[:, width:] = meta.astype(jnp.bfloat16)


def prep(hidden, norm_gain, slot_mask, token_ids):
    own_rows, width = hidden.shape
    return pl.pallas_call(
        prep_kernel,
        out_shape=jax.ShapeDtypeStruct((LIVE, width + 128), jnp.bfloat16),
        in_specs=[pl.BlockSpec(memory_space=pltpu.VMEM)] * 4,
        out_specs=pl.BlockSpec(memory_space=pltpu.VMEM),
    )(hidden, norm_gain.reshape(1, width), slot_mask.reshape(1, own_rows), token_ids.reshape(1, own_rows))


def stats_kernel(x_ref, w_ref, id_ref, out_ref):
    logits = jnp.dot(x_ref[...], w_ref[...], preferred_element_type=jnp.float32)
    peak = jnp.max(logits, axis=1, keepdims=True)
    shifted = logits - peak
    weights = jnp.exp(shifted)
    mass = jnp.sum(weights, axis=1, keepdims=True)
    spread = jnp.sum(weights * shifted, axis=1, keepdims=True)
    column = lax.broadcasted_iota(jnp.int32, logits.shape, 1)
    target = jnp.sum(jnp.where(column == id_ref[...], logits, 0.0), axis=1, keepdims=True)
    lane = lax.broadcasted_iota(jnp.int32, out_ref.shape, 1)
    out_ref[...] = jnp.where(
        lane == 0, peak, jnp.where(lane == 1, mass, jnp.where(lane == 2, spread, target))
    )


def row_stats(rows, weight, local_ids, width, tile):
    count = rows.shape[0]
    depth, vocab = weight.shape
    return pl.pallas_call(
        stats_kernel,
        out_shape=jax.ShapeDtypeStruct((count, 128), jnp.float32),
        grid=(count // tile,),
        in_specs=[
            pl.BlockSpec((tile, width), lambda i: (i, 0)),
            pl.BlockSpec((depth, vocab), lambda i: (0, 0)),
            pl.BlockSpec((tile, 1), lambda i: (i, 0)),
        ],
        out_specs=pl.BlockSpec((tile, 128), lambda i: (i, 0)),
        compiler_params=pltpu.CompilerParams(vmem_limit_bytes=56 * 1024 * 1024),
        cost_estimate=pl.CostEstimate(
            flops=2 * count * depth * vocab,
            transcendentals=count * vocab,
            bytes_accessed=2 * count * width + 2 * depth * vocab + 512 * count,
        ),
    )(rows, weight, local_ids)


def on_device(
    hidden, norm_gain, head_weight, value_weight, token_ids, slot_mask, lengths, request_order
):
    own_rows = hidden.shape[0]
    vocab_local = head_weight.shape[1]
    n_tensor = lax.axis_size("tensor")
    n_dp = lax.axis_size("dp")
    tensor_index = lax.axis_index("tensor")
    widened = hidden.astype(jnp.float32)
    inverse_rms = lax.rsqrt(jnp.mean(widened * widened, axis=1, keepdims=True) + EPSILON)
    normed = (widened * inverse_rms * norm_gain).astype(jnp.bfloat16)
    weight_mask = slot_mask.astype(jnp.float32)
    token_value = weight_mask * jnp.dot(normed, value_weight, preferred_element_type=jnp.float32)

    width = hidden.shape[1]
    live_sum = jnp.cumsum(slot_mask)
    slot_index = jnp.arange(own_rows, dtype=jnp.int32)
    chosen = (slot_mask[None, :] == 1) & (
        live_sum[None, :] - 1 == jnp.arange(LIVE, dtype=jnp.int32)[:, None]
    )
    source = jnp.sum(jnp.where(chosen, slot_index[None, :], 0), axis=1)
    block = prep(hidden, norm_gain, slot_mask, token_ids)
    gathered = lax.all_gather(block, "tensor", axis=0, tiled=True)
    meta_cols = gathered[:, width:width + 2].astype(jnp.float32)
    piece_ids = (meta_cols[:, 0] * 256.0 + meta_cols[:, 1]).astype(jnp.int32)
    local_ids = (piece_ids - tensor_index * vocab_local)[:, None]
    row_count = gathered.shape[0]
    stats = row_stats(gathered, head_weight, local_ids, width, 256 if row_count % 256 == 0 else row_count)
    blocks = stats[:, :4].reshape(n_tensor, LIVE, 4).transpose(0, 2, 1)
    request_count = lengths.shape[1]
    span_lengths = lengths[0]
    span_ends = jnp.cumsum(span_lengths)
    slot_ids = tensor_index * own_rows + source
    position = jnp.sum((slot_ids[:, None] >= span_ends[None, :]).astype(jnp.int32), axis=1)
    live = jnp.arange(LIVE, dtype=jnp.int32) < live_sum[-1]
    member = (position[None, :] == jnp.arange(8, dtype=jnp.int32)[:, None]) & live[None, :]
    spans = (
        jnp.zeros((8, 128), jnp.float32)
        .at[:, :LIVE].set(member.astype(jnp.float32))
        .at[:, 127].set(jnp.ones((8,), jnp.float32).at[:request_count].set(span_lengths.astype(jnp.float32)))
    )
    ids_tile = jnp.zeros((8, 128), jnp.float32).at[:request_count, 1].set(request_order.astype(jnp.float32))
    own, routed = finish(blocks, spans, ids_tile, n_tensor, n_dp)
    place = jnp.clip(live_sum - 1, 0, LIVE - 1)
    token_logprob = weight_mask * jnp.take(own[0], place)
    token_entropy = weight_mask * jnp.take(own[1], place)
    all_totals = routed[:, :request_count, 0].reshape(-1)
    all_owners = routed[:, :request_count, 1].reshape(-1)
    wanted = (lax.axis_index("dp") * request_count + jnp.arange(request_count)).astype(jnp.float32)
    route_table = all_owners[:, None] == wanted[None, :]
    request_score = jnp.sum(jnp.where(route_table, all_totals[:, None], 0.0), axis=0)
    return (token_logprob, token_entropy, token_value, request_score)


def solution(mesh):
    return jax.shard_map(
        on_device,
        mesh=mesh,
        in_specs=(
            P(("dp", "tensor"), None),
            P(),
            P(None, "tensor"),
            P(),
            P(("dp", "tensor")),
            P(("dp", "tensor")),
            P("dp", None),
            P("dp"),
        ),
        out_specs=(P(("dp", "tensor")), P(("dp", "tensor")), P(("dp", "tensor")), P("dp")),
        check_vma=False,
    )
```

```python
import jax
import jax.numpy as jnp
from jax import lax
from jax.experimental import pallas as pl
from jax.experimental.pallas import tpu as pltpu
from jax.sharding import Mesh, PartitionSpec as P

EPSILON = 1e-06
MESH = pl.DeviceIdType.MESH
LIVE = 48


def tensor_place(t, shape):
    return (t // (shape[1] * shape[2]), (t // shape[2]) % shape[1], t % shape[2])


def tensor_position(shape):
    return (lax.axis_index("x") * shape[1] + lax.axis_index("y")) * shape[2] + lax.axis_index("core")


def finish_kernel(n_tensor, n_dp, shape, send_ref, span_ref, ids_ref, own_ref, routed_ref,
                  held, t_held, d_held, part_msg, route_msg,
                  a_send, a_recv, t_send, t_recv, d_send, d_recv):
    me = tensor_position(shape)
    mine = (lax.axis_index("x"), lax.axis_index("y"), lax.axis_index("core"))
    dp = lax.axis_index("dp")
    barrier = pltpu.get_barrier_semaphore()
    for offset in range(1, n_tensor):
        peer = lax.rem(me + offset, n_tensor)
        pl.semaphore_signal(barrier, inc=1, device_id=(dp,) + tensor_place(peer, shape), device_id_type=MESH)
    for offset in range(1, n_dp):
        peer = lax.rem(dp + offset, n_dp)
        pl.semaphore_signal(barrier, inc=1, device_id=(peer,) + mine, device_id_type=MESH)
    pl.semaphore_wait(barrier, n_tensor - 1 + n_dp - 1)

    held[me] = send_ref[me]
    copies = []
    for offset in range(1, n_tensor):
        peer = lax.rem(me + offset, n_tensor)
        copy = pltpu.make_async_remote_copy(
            src_ref=send_ref.at[peer], dst_ref=held.at[me],
            send_sem=a_send.at[offset], recv_sem=a_recv.at[offset],
            device_id=(dp,) + tensor_place(peer, shape), device_id_type=MESH,
        )
        copy.start()
        copies.append(copy)
    for copy in copies:
        copy.wait_send()
    for offset in range(1, n_tensor):
        source = lax.rem(me + n_tensor - offset, n_tensor)
        pltpu.make_async_remote_copy(
            src_ref=send_ref.at[source], dst_ref=held.at[source],
            send_sem=a_send.at[offset], recv_sem=a_recv.at[offset],
            device_id=(dp,) + tensor_place(source, shape), device_id_type=MESH,
        ).wait_recv()

    lanes = held.shape[2]
    peak = lax.fori_loop(
        0, n_tensor, lambda p, m: jnp.maximum(m, held[p][0:1, :]),
        jnp.full((1, lanes), -jnp.inf, jnp.float32),
    )

    def gather_sums(p, sums):
        mass, spread, target = sums
        block = held[p]
        gap = block[0:1, :] - peak
        factor = jnp.exp(gap)
        mass = mass + factor * block[1:2, :]
        spread = spread + factor * (block[2:3, :] + gap * block[1:2, :])
        return mass, spread, target + block[3:4, :]

    zero = jnp.zeros((1, lanes), jnp.float32)
    mass, spread, target = lax.fori_loop(0, n_tensor, gather_sums, (zero, zero, zero))
    log_mass = jnp.log(mass)
    logprob = target - peak - log_mass
    entropy = log_mass - spread / mass
    row = lax.broadcasted_iota(jnp.int32, own_ref.shape, 0)
    own_ref[...] = jnp.where(row == 0, logprob, jnp.where(row == 1, entropy, 0.0))

    spans = span_ref[...]
    partial = jnp.sum(spans[:, :lanes] * logprob, axis=1, keepdims=True) / spans[:, 127:128]
    part_msg[...] = jnp.broadcast_to(partial, part_msg.shape)
    t_held[me] = part_msg[...]
    copies = []
    for offset in range(1, n_tensor):
        peer = lax.rem(me + offset, n_tensor)
        copy = pltpu.make_async_remote_copy(
            src_ref=part_msg, dst_ref=t_held.at[me],
            send_sem=t_send.at[offset], recv_sem=t_recv.at[offset],
            device_id=(dp,) + tensor_place(peer, shape), device_id_type=MESH,
        )
        copy.start()
        copies.append(copy)
    for copy in copies:
        copy.wait_send()
    for offset in range(1, n_tensor):
        source = lax.rem(me + n_tensor - offset, n_tensor)
        pltpu.make_async_remote_copy(
            src_ref=part_msg, dst_ref=t_held.at[source],
            send_sem=t_send.at[offset], recv_sem=t_recv.at[offset],
            device_id=(dp,) + tensor_place(source, shape), device_id_type=MESH,
        ).wait_recv()

    total = jnp.sum(t_held[...], axis=0)
    lane = lax.broadcasted_iota(jnp.int32, total.shape, 1)
    route_msg[...] = jnp.where(lane == 0, total, jnp.where(lane == 1, ids_ref[...], 0.0))
    d_held[dp] = route_msg[...]
    copies = []
    for offset in range(1, n_dp):
        peer = lax.rem(dp + offset, n_dp)
        copy = pltpu.make_async_remote_copy(
            src_ref=route_msg, dst_ref=d_held.at[dp],
            send_sem=d_send.at[offset], recv_sem=d_recv.at[offset],
            device_id=(peer,) + mine, device_id_type=MESH,
        )
        copy.start()
        copies.append(copy)
    for copy in copies:
        copy.wait_send()
    for offset in range(1, n_dp):
        source = lax.rem(dp + n_dp - offset, n_dp)
        pltpu.make_async_remote_copy(
            src_ref=route_msg, dst_ref=d_held.at[source],
            send_sem=d_send.at[offset], recv_sem=d_recv.at[offset],
            device_id=(source,) + mine, device_id_type=MESH,
        ).wait_recv()
    routed_ref[...] = d_held[...]


def finish(blocks, spans, ids, n_tensor, n_dp, shape):
    tile = spans.shape
    lanes = blocks.shape[2]
    return pl.pallas_call(
        lambda *refs: finish_kernel(n_tensor, n_dp, shape, *refs),
        out_shape=(
            jax.ShapeDtypeStruct((8, lanes), jnp.float32),
            jax.ShapeDtypeStruct((n_dp,) + tile, jnp.float32),
        ),
        in_specs=[pl.BlockSpec(memory_space=pltpu.VMEM)] * 3,
        out_specs=(pl.BlockSpec(memory_space=pltpu.VMEM), pl.BlockSpec(memory_space=pltpu.VMEM)),
        scratch_shapes=[
            pltpu.VMEM(blocks.shape, jnp.float32),
            pltpu.VMEM((n_tensor,) + tile, jnp.float32),
            pltpu.VMEM((n_dp,) + tile, jnp.float32),
            pltpu.VMEM(tile, jnp.float32),
            pltpu.VMEM(tile, jnp.float32),
            pltpu.SemaphoreType.DMA((n_tensor,)),
            pltpu.SemaphoreType.DMA((n_tensor,)),
            pltpu.SemaphoreType.DMA((n_tensor,)),
            pltpu.SemaphoreType.DMA((n_tensor,)),
            pltpu.SemaphoreType.DMA((n_dp,)),
            pltpu.SemaphoreType.DMA((n_dp,)),
        ],
        compiler_params=pltpu.CompilerParams(collective_id=3, has_side_effects=True),
    )(blocks, spans, ids)


def prep_kernel(hidden_ref, gain_ref, mask_ref, ids_ref, out_ref):
    width = hidden_ref.shape[1]
    own_rows = hidden_ref.shape[0]
    widened = hidden_ref[...].astype(jnp.float32)
    inverse_rms = lax.rsqrt(jnp.mean(widened * widened, axis=1, keepdims=True) + EPSILON)
    normed = (widened * inverse_rms * gain_ref[...]).astype(jnp.bfloat16)
    live = jnp.broadcast_to(mask_ref[...].astype(jnp.float32), (8, own_rows))
    upper = (
        lax.broadcasted_iota(jnp.int32, (own_rows, own_rows), 0)
        <= lax.broadcasted_iota(jnp.int32, (own_rows, own_rows), 1)
    ).astype(jnp.float32)
    live_sum = jnp.dot(live, upper, preferred_element_type=jnp.float32)[0:1, :]
    rank = lax.broadcasted_iota(jnp.int32, (LIVE, own_rows), 0).astype(jnp.float32)
    chosen = ((live[0:1, :] == 1.0) & (live_sum - 1.0 == rank)).astype(jnp.bfloat16)
    out_ref[:, :width] = jnp.dot(chosen, normed, preferred_element_type=jnp.float32).astype(jnp.bfloat16)
    ids = ids_ref[...]
    high = lax.shift_right_logical(ids, 8).astype(jnp.float32)
    low = jnp.bitwise_and(ids, 255).astype(jnp.float32)
    row = lax.broadcasted_iota(jnp.int32, (128, own_rows), 0)
    meta_in = jnp.where(row == 0, high, jnp.where(row == 1, low, 0.0)).astype(jnp.bfloat16)
    meta = lax.dot_general(
        chosen, meta_in, (((1,), (1,)), ((), ())), preferred_element_type=jnp.float32
    )
    out_ref[:, width:] = meta.astype(jnp.bfloat16)


def prep(hidden, norm_gain, slot_mask, token_ids):
    own_rows, width = hidden.shape
    return pl.pallas_call(
        prep_kernel,
        out_shape=jax.ShapeDtypeStruct((LIVE, width + 128), jnp.bfloat16),
        in_specs=[pl.BlockSpec(memory_space=pltpu.VMEM)] * 4,
        out_specs=pl.BlockSpec(memory_space=pltpu.VMEM),
    )(hidden, norm_gain.reshape(1, width), slot_mask.reshape(1, own_rows), token_ids.reshape(1, own_rows))


def stats_kernel(x_ref, w_ref, id_ref, out_ref):
    logits = jnp.dot(x_ref[...], w_ref[...], preferred_element_type=jnp.float32)
    peak = jnp.max(logits, axis=1, keepdims=True)
    shifted = logits - peak
    weights = jnp.exp(shifted)
    mass = jnp.sum(weights, axis=1, keepdims=True)
    spread = jnp.sum(weights * shifted, axis=1, keepdims=True)
    column = lax.broadcasted_iota(jnp.int32, logits.shape, 1)
    target = jnp.sum(jnp.where(column == id_ref[...], logits, 0.0), axis=1, keepdims=True)
    lane = lax.broadcasted_iota(jnp.int32, out_ref.shape, 1)
    out_ref[...] = jnp.where(
        lane == 0, peak, jnp.where(lane == 1, mass, jnp.where(lane == 2, spread, target))
    )


def row_stats(rows, weight, local_ids, width, tile):
    count = rows.shape[0]
    depth, vocab = weight.shape
    return pl.pallas_call(
        stats_kernel,
        out_shape=jax.ShapeDtypeStruct((count, 128), jnp.float32),
        grid=(count // tile,),
        in_specs=[
            pl.BlockSpec((tile, width), lambda i: (i, 0)),
            pl.BlockSpec((depth, vocab), lambda i: (0, 0)),
            pl.BlockSpec((tile, 1), lambda i: (i, 0)),
        ],
        out_specs=pl.BlockSpec((tile, 128), lambda i: (i, 0)),
        compiler_params=pltpu.CompilerParams(vmem_limit_bytes=56 * 1024 * 1024),
        cost_estimate=pl.CostEstimate(
            flops=2 * count * depth * vocab,
            transcendentals=count * vocab,
            bytes_accessed=2 * count * width + 2 * depth * vocab + 512 * count,
        ),
    )(rows, weight, local_ids)


def on_device(
    hidden, norm_gain, head_weight, value_weight, token_ids, slot_mask, lengths, request_order
):
    own_rows = hidden.shape[0]
    vocab_local = head_weight.shape[1]
    shape = (lax.axis_size("x"), lax.axis_size("y"), lax.axis_size("core"))
    n_tensor = shape[0] * shape[1] * shape[2]
    n_dp = lax.axis_size("dp")
    tensor_index = tensor_position(shape)
    widened = hidden.astype(jnp.float32)
    inverse_rms = lax.rsqrt(jnp.mean(widened * widened, axis=1, keepdims=True) + EPSILON)
    normed = (widened * inverse_rms * norm_gain).astype(jnp.bfloat16)
    weight_mask = slot_mask.astype(jnp.float32)
    token_value = weight_mask * jnp.dot(normed, value_weight, preferred_element_type=jnp.float32)

    width = hidden.shape[1]
    live_sum = jnp.cumsum(slot_mask)
    slot_index = jnp.arange(own_rows, dtype=jnp.int32)
    chosen = (slot_mask[None, :] == 1) & (
        live_sum[None, :] - 1 == jnp.arange(LIVE, dtype=jnp.int32)[:, None]
    )
    source = jnp.sum(jnp.where(chosen, slot_index[None, :], 0), axis=1)
    block = prep(hidden, norm_gain, slot_mask, token_ids)
    chip_rows = lax.all_gather(block, ("x", "y"), axis=0, tiled=True)
    gathered = lax.all_gather(
        chip_rows.reshape(shape[0] * shape[1], LIVE, block.shape[1]), "core", axis=1
    ).reshape(n_tensor * LIVE, block.shape[1])
    meta_cols = gathered[:, width:width + 2].astype(jnp.float32)
    piece_ids = (meta_cols[:, 0] * 256.0 + meta_cols[:, 1]).astype(jnp.int32)
    local_ids = (piece_ids - tensor_index * vocab_local)[:, None]
    row_count = gathered.shape[0]
    stats = row_stats(gathered, head_weight, local_ids, width, 256 if row_count % 256 == 0 else row_count)
    blocks = stats[:, :4].reshape(n_tensor, LIVE, 4).transpose(0, 2, 1)
    request_count = lengths.shape[1]
    span_lengths = lengths[0]
    span_ends = jnp.cumsum(span_lengths)
    slot_ids = tensor_index * own_rows + source
    position = jnp.sum((slot_ids[:, None] >= span_ends[None, :]).astype(jnp.int32), axis=1)
    live = jnp.arange(LIVE, dtype=jnp.int32) < live_sum[-1]
    member = (position[None, :] == jnp.arange(8, dtype=jnp.int32)[:, None]) & live[None, :]
    spans = (
        jnp.zeros((8, 128), jnp.float32)
        .at[:, :LIVE].set(member.astype(jnp.float32))
        .at[:, 127].set(jnp.ones((8,), jnp.float32).at[:request_count].set(span_lengths.astype(jnp.float32)))
    )
    ids_tile = jnp.zeros((8, 128), jnp.float32).at[:request_count, 1].set(request_order.astype(jnp.float32))
    own, routed = finish(blocks, spans, ids_tile, n_tensor, n_dp, shape)
    place = jnp.clip(live_sum - 1, 0, LIVE - 1)
    token_logprob = weight_mask * jnp.take(own[0], place)
    token_entropy = weight_mask * jnp.take(own[1], place)
    all_totals = routed[:, :request_count, 0].reshape(-1)
    all_owners = routed[:, :request_count, 1].reshape(-1)
    wanted = (lax.axis_index("dp") * request_count + jnp.arange(request_count)).astype(jnp.float32)
    route_table = all_owners[:, None] == wanted[None, :]
    request_score = jnp.sum(jnp.where(route_table, all_totals[:, None], 0.0), axis=0)
    return (token_logprob, token_entropy, token_value, request_score)


def solution(mesh):
    n_dp, n_tensor = mesh.devices.shape
    cores = 2
    rows = min(4, n_tensor // cores)
    split = Mesh(
        mesh.devices.reshape(n_dp, n_tensor // (rows * cores), rows, cores), ("dp", "x", "y", "core")
    )
    tensor = ("x", "y", "core")
    return jax.shard_map(
        on_device,
        mesh=split,
        in_specs=(
            P(("dp",) + tensor, None),
            P(),
            P(None, tensor),
            P(),
            P(("dp",) + tensor),
            P(("dp",) + tensor),
            P("dp", None),
            P("dp"),
        ),
        out_specs=(P(("dp",) + tensor), P(("dp",) + tensor), P(("dp",) + tensor), P("dp")),
        check_vma=False,
    )
```

```python
import jax
import jax.numpy as jnp
from jax import lax
from jax.experimental import pallas as pl
from jax.experimental.pallas import tpu as pltpu
from jax.sharding import PartitionSpec as P

EPSILON = 1e-06
MESH = pl.DeviceIdType.MESH
LIVE = 48


def score_kernel(n_tensor, n_dp, tile, x_ref, w_ref, id_ref, member_ref, len_ref, ids_ref,
                 own_ref, routed_ref, stats_buf, held, t_held, d_held, part_msg, route_msg,
                 a_send, a_recv, t_send, t_recv, d_send, d_recv):
    step = pl.program_id(0)
    last = pl.num_programs(0) - 1
    me = lax.axis_index("tensor")
    dp = lax.axis_index("dp")
    rows = held.shape[1]

    @pl.when(step == 0)
    def _():
        barrier = pltpu.get_barrier_semaphore()
        for offset in range(1, n_tensor):
            peer = lax.rem(me + offset, n_tensor)
            pl.semaphore_signal(barrier, inc=1, device_id=(dp, peer), device_id_type=MESH)
        for offset in range(1, n_dp):
            peer = lax.rem(dp + offset, n_dp)
            pl.semaphore_signal(barrier, inc=1, device_id=(peer, me), device_id_type=MESH)
        pl.semaphore_wait(barrier, n_tensor - 1 + n_dp - 1)

    logits = jnp.dot(x_ref[...], w_ref[...], preferred_element_type=jnp.float32)
    peak = jnp.max(logits, axis=1, keepdims=True)
    shifted = logits - peak
    weights = jnp.exp(shifted)
    mass = jnp.sum(weights, axis=1, keepdims=True)
    spread = jnp.sum(weights * shifted, axis=1, keepdims=True)
    column = lax.broadcasted_iota(jnp.int32, logits.shape, 1)
    target = jnp.sum(jnp.where(column == id_ref[...], logits, 0.0), axis=1, keepdims=True)
    lane = lax.broadcasted_iota(jnp.int32, (tile, 128), 1)
    start = pl.multiple_of(step * tile, 8)
    stats_buf[pl.ds(start, tile)] = jnp.where(
        lane == 0, peak, jnp.where(lane == 1, mass, jnp.where(lane == 2, spread, target))
    )

    for b in range(tile // rows):
        peer = step * (tile // rows) + b
        source_rows = stats_buf.at[pl.ds(pl.multiple_of(peer * rows, 8), rows)]

        @pl.when(peer == me)
        def _():
            held[me] = source_rows[...]

        @pl.when(peer != me)
        def _():
            pltpu.make_async_remote_copy(
                src_ref=source_rows, dst_ref=held.at[me],
                send_sem=a_send.at[peer], recv_sem=a_recv.at[me],
                device_id=(dp, peer), device_id_type=MESH,
            ).start()

    @pl.when(step == last)
    def _():
        for offset in range(1, n_tensor):
            peer = lax.rem(me + offset, n_tensor)
            pltpu.make_async_remote_copy(
                src_ref=stats_buf.at[pl.ds(pl.multiple_of(peer * rows, 8), rows)], dst_ref=held.at[me],
                send_sem=a_send.at[peer], recv_sem=a_recv.at[me],
                device_id=(dp, peer), device_id_type=MESH,
            ).wait_send()
        for offset in range(1, n_tensor):
            source = lax.rem(me + n_tensor - offset, n_tensor)
            pltpu.make_async_remote_copy(
                src_ref=stats_buf.at[pl.ds(pl.multiple_of(me * rows, 8), rows)], dst_ref=held.at[source],
                send_sem=a_send.at[me], recv_sem=a_recv.at[source],
                device_id=(dp, source), device_id_type=MESH,
            ).wait_recv()

        top = lax.fori_loop(
            0, n_tensor, lambda p, m: jnp.maximum(m, held[p][:, 0:1]),
            jnp.full((rows, 1), -jnp.inf, jnp.float32),
        )

        def gather_sums(p, sums):
            total_mass, total_spread, total_target = sums
            block = held[p]
            gap = block[:, 0:1] - top
            factor = jnp.exp(gap)
            total_mass = total_mass + factor * block[:, 1:2]
            total_spread = total_spread + factor * (block[:, 2:3] + gap * block[:, 1:2])
            return total_mass, total_spread, total_target + block[:, 3:4]

        zero = jnp.zeros((rows, 1), jnp.float32)
        total_mass, total_spread, total_target = lax.fori_loop(
            0, n_tensor, gather_sums, (zero, zero, zero)
        )
        log_mass = jnp.log(total_mass)
        logprob = total_target - top - log_mass
        entropy = log_mass - total_spread / total_mass
        own_lane = lax.broadcasted_iota(jnp.int32, own_ref.shape, 1)
        own_ref[...] = jnp.where(own_lane == 0, logprob, jnp.where(own_lane == 1, entropy, 0.0))

        partial = jnp.sum(member_ref[...] * logprob, axis=0, keepdims=True) / len_ref[0:1, :]
        part_msg[...] = jnp.broadcast_to(partial, part_msg.shape)
        t_held[me] = part_msg[...]
        copies = []
        for offset in range(1, n_tensor):
            peer = lax.rem(me + offset, n_tensor)
            copy = pltpu.make_async_remote_copy(
                src_ref=part_msg, dst_ref=t_held.at[me],
                send_sem=t_send.at[offset], recv_sem=t_recv.at[offset],
                device_id=(dp, peer), device_id_type=MESH,
            )
            copy.start()
            copies.append(copy)
        for copy in copies:
            copy.wait_send()
        for offset in range(1, n_tensor):
            source = lax.rem(me + n_tensor - offset, n_tensor)
            pltpu.make_async_remote_copy(
                src_ref=part_msg, dst_ref=t_held.at[source],
                send_sem=t_send.at[offset], recv_sem=t_recv.at[offset],
                device_id=(dp, source), device_id_type=MESH,
            ).wait_recv()

        total = jnp.sum(t_held[...], axis=0)
        row = lax.broadcasted_iota(jnp.int32, total.shape, 0)
        route_msg[...] = jnp.where(row == 0, total, jnp.where(row == 1, ids_ref[...], 0.0))
        d_held[dp] = route_msg[...]
        copies = []
        for offset in range(1, n_dp):
            peer = lax.rem(dp + offset, n_dp)
            copy = pltpu.make_async_remote_copy(
                src_ref=route_msg, dst_ref=d_held.at[dp],
                send_sem=d_send.at[offset], recv_sem=d_recv.at[offset],
                device_id=(peer, me), device_id_type=MESH,
            )
            copy.start()
            copies.append(copy)
        for copy in copies:
            copy.wait_send()
        for offset in range(1, n_dp):
            source = lax.rem(dp + n_dp - offset, n_dp)
            pltpu.make_async_remote_copy(
                src_ref=route_msg, dst_ref=d_held.at[source],
                send_sem=d_send.at[offset], recv_sem=d_recv.at[offset],
                device_id=(source, me), device_id_type=MESH,
            ).wait_recv()
        routed_ref[...] = d_held[...]


def score(rows, weight, local_ids, member, lens, ids, width, tile, n_tensor, n_dp):
    count = rows.shape[0]
    depth, vocab = weight.shape
    full = lambda shape: pl.BlockSpec(shape, lambda i: (0,) * len(shape))
    return pl.pallas_call(
        lambda *refs: score_kernel(n_tensor, n_dp, tile, *refs),
        out_shape=(
            jax.ShapeDtypeStruct((LIVE, 128), jnp.float32),
            jax.ShapeDtypeStruct((n_dp, 8, 128), jnp.float32),
        ),
        grid=(count // tile,),
        in_specs=[
            pl.BlockSpec((tile, width), lambda i: (i, 0)),
            full((depth, vocab)),
            pl.BlockSpec((tile, 1), lambda i: (i, 0)),
            full((LIVE, 128)),
            full((8, 128)),
            full((8, 128)),
        ],
        out_specs=(full((LIVE, 128)), full((n_dp, 8, 128))),
        scratch_shapes=[
            pltpu.VMEM((count, 128), jnp.float32),
            pltpu.VMEM((n_tensor, LIVE, 128), jnp.float32),
            pltpu.VMEM((n_tensor, 8, 128), jnp.float32),
            pltpu.VMEM((n_dp, 8, 128), jnp.float32),
            pltpu.VMEM((8, 128), jnp.float32),
            pltpu.VMEM((8, 128), jnp.float32),
            pltpu.SemaphoreType.DMA((n_tensor,)),
            pltpu.SemaphoreType.DMA((n_tensor,)),
            pltpu.SemaphoreType.DMA((n_tensor,)),
            pltpu.SemaphoreType.DMA((n_tensor,)),
            pltpu.SemaphoreType.DMA((n_dp,)),
            pltpu.SemaphoreType.DMA((n_dp,)),
        ],
        compiler_params=pltpu.CompilerParams(
            collective_id=4, has_side_effects=True, vmem_limit_bytes=56 * 1024 * 1024
        ),
        cost_estimate=pl.CostEstimate(
            flops=2 * count * depth * vocab,
            transcendentals=count * vocab,
            bytes_accessed=2 * count * width + 2 * depth * vocab + 512 * count,
        ),
    )(rows, weight, local_ids, member, lens, ids)


def prep_kernel(hidden_ref, gain_ref, mask_ref, ids_ref, out_ref):
    width = hidden_ref.shape[1]
    own_rows = hidden_ref.shape[0]
    widened = hidden_ref[...].astype(jnp.float32)
    inverse_rms = lax.rsqrt(jnp.mean(widened * widened, axis=1, keepdims=True) + EPSILON)
    normed = (widened * inverse_rms * gain_ref[...]).astype(jnp.bfloat16)
    live = jnp.broadcast_to(mask_ref[...].astype(jnp.float32), (8, own_rows))
    upper = (
        lax.broadcasted_iota(jnp.int32, (own_rows, own_rows), 0)
        <= lax.broadcasted_iota(jnp.int32, (own_rows, own_rows), 1)
    ).astype(jnp.float32)
    live_sum = jnp.dot(live, upper, preferred_element_type=jnp.float32)[0:1, :]
    rank = lax.broadcasted_iota(jnp.int32, (LIVE, own_rows), 0).astype(jnp.float32)
    chosen = ((live[0:1, :] == 1.0) & (live_sum - 1.0 == rank)).astype(jnp.bfloat16)
    out_ref[:, :width] = jnp.dot(chosen, normed, preferred_element_type=jnp.float32).astype(jnp.bfloat16)
    ids = ids_ref[...]
    high = lax.shift_right_logical(ids, 8).astype(jnp.float32)
    low = jnp.bitwise_and(ids, 255).astype(jnp.float32)
    row = lax.broadcasted_iota(jnp.int32, (128, own_rows), 0)
    meta_in = jnp.where(row == 0, high, jnp.where(row == 1, low, 0.0)).astype(jnp.bfloat16)
    meta = lax.dot_general(
        chosen, meta_in, (((1,), (1,)), ((), ())), preferred_element_type=jnp.float32
    )
    out_ref[:, width:] = meta.astype(jnp.bfloat16)


def prep(hidden, norm_gain, slot_mask, token_ids):
    own_rows, width = hidden.shape
    return pl.pallas_call(
        prep_kernel,
        out_shape=jax.ShapeDtypeStruct((LIVE, width + 128), jnp.bfloat16),
        in_specs=[pl.BlockSpec(memory_space=pltpu.VMEM)] * 4,
        out_specs=pl.BlockSpec(memory_space=pltpu.VMEM),
    )(hidden, norm_gain.reshape(1, width), slot_mask.reshape(1, own_rows), token_ids.reshape(1, own_rows))


def on_device(
    hidden, norm_gain, head_weight, value_weight, token_ids, slot_mask, lengths, request_order
):
    own_rows = hidden.shape[0]
    vocab_local = head_weight.shape[1]
    n_tensor = lax.axis_size("tensor")
    n_dp = lax.axis_size("dp")
    tensor_index = lax.axis_index("tensor")
    widened = hidden.astype(jnp.float32)
    inverse_rms = lax.rsqrt(jnp.mean(widened * widened, axis=1, keepdims=True) + EPSILON)
    normed = (widened * inverse_rms * norm_gain).astype(jnp.bfloat16)
    weight_mask = slot_mask.astype(jnp.float32)
    token_value = weight_mask * jnp.dot(normed, value_weight, preferred_element_type=jnp.float32)

    width = hidden.shape[1]
    live_sum = jnp.cumsum(slot_mask)
    slot_index = jnp.arange(own_rows, dtype=jnp.int32)
    chosen = (slot_mask[None, :] == 1) & (
        live_sum[None, :] - 1 == jnp.arange(LIVE, dtype=jnp.int32)[:, None]
    )
    source = jnp.sum(jnp.where(chosen, slot_index[None, :], 0), axis=1)
    block = prep(hidden, norm_gain, slot_mask, token_ids)
    gathered = lax.all_gather(block, "tensor", axis=0, tiled=True)
    meta_cols = gathered[:, width:width + 2].astype(jnp.float32)
    piece_ids = (meta_cols[:, 0] * 256.0 + meta_cols[:, 1]).astype(jnp.int32)
    local_ids = (piece_ids - tensor_index * vocab_local)[:, None]
    request_count = lengths.shape[1]
    span_lengths = lengths[0]
    span_ends = jnp.cumsum(span_lengths)
    slot_ids = tensor_index * own_rows + source
    position = jnp.sum((slot_ids[:, None] >= span_ends[None, :]).astype(jnp.int32), axis=1)
    live = jnp.arange(LIVE, dtype=jnp.int32) < live_sum[-1]
    member = (position[:, None] == jnp.arange(128, dtype=jnp.int32)[None, :]) & live[:, None]
    lens = jnp.ones((8, 128), jnp.float32).at[0, :request_count].set(span_lengths.astype(jnp.float32))
    ids_tile = jnp.zeros((8, 128), jnp.float32).at[1, :request_count].set(request_order.astype(jnp.float32))
    row_count = gathered.shape[0]
    tile = 4 * LIVE if row_count % (4 * LIVE) == 0 else row_count
    own, routed = score(
        gathered, head_weight, local_ids, member.astype(jnp.float32), lens, ids_tile,
        width, tile, n_tensor, n_dp,
    )
    place = jnp.clip(live_sum - 1, 0, LIVE - 1)
    token_logprob = weight_mask * jnp.take(own[:, 0], place)
    token_entropy = weight_mask * jnp.take(own[:, 1], place)
    all_totals = routed[:, 0, :request_count].reshape(-1)
    all_owners = routed[:, 1, :request_count].reshape(-1)
    wanted = (lax.axis_index("dp") * request_count + jnp.arange(request_count)).astype(jnp.float32)
    route_table = all_owners[:, None] == wanted[None, :]
    request_score = jnp.sum(jnp.where(route_table, all_totals[:, None], 0.0), axis=0)
    return (token_logprob, token_entropy, token_value, request_score)


def solution(mesh):
    return jax.shard_map(
        on_device,
        mesh=mesh,
        in_specs=(
            P(("dp", "tensor"), None),
            P(),
            P(None, "tensor"),
            P(),
            P(("dp", "tensor")),
            P(("dp", "tensor")),
            P("dp", None),
            P("dp"),
        ),
        out_specs=(P(("dp", "tensor")), P(("dp", "tensor")), P(("dp", "tensor")), P("dp")),
        check_vma=False,
    )
```

```python
import jax
import jax.numpy as jnp
from jax import lax
from jax.experimental import pallas as pl
from jax.experimental.pallas import tpu as pltpu
from jax.sharding import PartitionSpec as P

EPSILON = 1e-06
MESH = pl.DeviceIdType.MESH
LIVE = 48


def exchange_kernel(n_tensor, send_ref, out_ref, held, send_sem, recv_sem):
    me = lax.axis_index("tensor")
    dp = lax.axis_index("dp")
    barrier = pltpu.get_barrier_semaphore()
    for offset in range(1, n_tensor):
        peer = lax.rem(me + offset, n_tensor)
        pl.semaphore_signal(barrier, inc=1, device_id=(dp, peer), device_id_type=MESH)
    pl.semaphore_wait(barrier, n_tensor - 1)
    held[me] = send_ref[me]
    copies = []
    for offset in range(1, n_tensor):
        peer = lax.rem(me + offset, n_tensor)
        copy = pltpu.make_async_remote_copy(
            src_ref=send_ref.at[peer],
            dst_ref=held.at[me],
            send_sem=send_sem.at[offset],
            recv_sem=recv_sem.at[offset],
            device_id=(dp, peer),
            device_id_type=MESH,
        )
        copy.start()
        copies.append(copy)
    for copy in copies:
        copy.wait_send()
    for offset in range(1, n_tensor):
        source = lax.rem(me + n_tensor - offset, n_tensor)
        pltpu.make_async_remote_copy(
            src_ref=send_ref.at[source],
            dst_ref=held.at[source],
            send_sem=send_sem.at[offset],
            recv_sem=recv_sem.at[offset],
            device_id=(dp, source),
            device_id_type=MESH,
        ).wait_recv()
    out_ref[...] = held[...]


def exchange(blocks, n_tensor):
    return pl.pallas_call(
        lambda *refs: exchange_kernel(n_tensor, *refs),
        out_shape=jax.ShapeDtypeStruct(blocks.shape, blocks.dtype),
        in_specs=[pl.BlockSpec(memory_space=pltpu.VMEM)],
        out_specs=pl.BlockSpec(memory_space=pltpu.VMEM),
        scratch_shapes=[
            pltpu.VMEM(blocks.shape, blocks.dtype),
            pltpu.SemaphoreType.DMA((n_tensor,)),
            pltpu.SemaphoreType.DMA((n_tensor,)),
        ],
        compiler_params=pltpu.CompilerParams(collective_id=0, has_side_effects=True),
    )(blocks)


def route_kernel(n_tensor, n_dp, part_ref, ids_ref, out_ref, t_held, d_held, msg,
                 t_send, t_recv, d_send, d_recv):
    me = lax.axis_index("tensor")
    dp = lax.axis_index("dp")
    barrier = pltpu.get_barrier_semaphore()
    for offset in range(1, n_tensor):
        peer = lax.rem(me + offset, n_tensor)
        pl.semaphore_signal(barrier, inc=1, device_id=(dp, peer), device_id_type=MESH)
    for offset in range(1, n_dp):
        peer = lax.rem(dp + offset, n_dp)
        pl.semaphore_signal(barrier, inc=1, device_id=(peer, me), device_id_type=MESH)
    pl.semaphore_wait(barrier, n_tensor - 1 + n_dp - 1)
    t_held[me] = part_ref[...]
    copies = []
    for offset in range(1, n_tensor):
        peer = lax.rem(me + offset, n_tensor)
        copy = pltpu.make_async_remote_copy(
            src_ref=part_ref,
            dst_ref=t_held.at[me],
            send_sem=t_send.at[offset],
            recv_sem=t_recv.at[offset],
            device_id=(dp, peer),
            device_id_type=MESH,
        )
        copy.start()
        copies.append(copy)
    for copy in copies:
        copy.wait_send()
    for offset in range(1, n_tensor):
        source = lax.rem(me + n_tensor - offset, n_tensor)
        pltpu.make_async_remote_copy(
            src_ref=part_ref,
            dst_ref=t_held.at[source],
            send_sem=t_send.at[offset],
            recv_sem=t_recv.at[offset],
            device_id=(dp, source),
            device_id_type=MESH,
        ).wait_recv()
    total = jnp.sum(t_held[...], axis=0)
    row = lax.broadcasted_iota(jnp.int32, total.shape, 0)
    msg[...] = jnp.where(row == 0, total, jnp.where(row == 1, ids_ref[...], 0.0))
    d_held[dp] = msg[...]
    copies = []
    for offset in range(1, n_dp):
        peer = lax.rem(dp + offset, n_dp)
        copy = pltpu.make_async_remote_copy(
            src_ref=msg,
            dst_ref=d_held.at[dp],
            send_sem=d_send.at[offset],
            recv_sem=d_recv.at[offset],
            device_id=(peer, me),
            device_id_type=MESH,
        )
        copy.start()
        copies.append(copy)
    for copy in copies:
        copy.wait_send()
    for offset in range(1, n_dp):
        source = lax.rem(dp + n_dp - offset, n_dp)
        pltpu.make_async_remote_copy(
            src_ref=msg,
            dst_ref=d_held.at[source],
            send_sem=d_send.at[offset],
            recv_sem=d_recv.at[offset],
            device_id=(source, me),
            device_id_type=MESH,
        ).wait_recv()
    out_ref[...] = d_held[...]


def route(part, ids, n_tensor, n_dp):
    tile = part.shape
    return pl.pallas_call(
        lambda *refs: route_kernel(n_tensor, n_dp, *refs),
        out_shape=jax.ShapeDtypeStruct((n_dp,) + tile, jnp.float32),
        in_specs=[pl.BlockSpec(memory_space=pltpu.VMEM)] * 2,
        out_specs=pl.BlockSpec(memory_space=pltpu.VMEM),
        scratch_shapes=[
            pltpu.VMEM((n_tensor,) + tile, jnp.float32),
            pltpu.VMEM((n_dp,) + tile, jnp.float32),
            pltpu.VMEM(tile, jnp.float32),
            pltpu.SemaphoreType.DMA((n_tensor,)),
            pltpu.SemaphoreType.DMA((n_tensor,)),
            pltpu.SemaphoreType.DMA((n_dp,)),
            pltpu.SemaphoreType.DMA((n_dp,)),
        ],
        compiler_params=pltpu.CompilerParams(collective_id=1, has_side_effects=True),
    )(part, ids)


def finish_kernel(n_tensor, n_dp, send_ref, span_ref, ids_ref, own_ref, routed_ref,
                  held, t_held, d_held, part_msg, route_msg,
                  a_send, a_recv, t_send, t_recv, d_send, d_recv):
    me = lax.axis_index("tensor")
    dp = lax.axis_index("dp")
    barrier = pltpu.get_barrier_semaphore()
    for offset in range(1, n_tensor):
        peer = lax.rem(me + offset, n_tensor)
        pl.semaphore_signal(barrier, inc=1, device_id=(dp, peer), device_id_type=MESH)
    for offset in range(1, n_dp):
        peer = lax.rem(dp + offset, n_dp)
        pl.semaphore_signal(barrier, inc=1, device_id=(peer, me), device_id_type=MESH)
    pl.semaphore_wait(barrier, n_tensor - 1 + n_dp - 1)

    held[me] = send_ref[me]
    copies = []
    for offset in range(1, n_tensor):
        peer = lax.rem(me + offset, n_tensor)
        copy = pltpu.make_async_remote_copy(
            src_ref=send_ref.at[peer], dst_ref=held.at[me],
            send_sem=a_send.at[offset], recv_sem=a_recv.at[offset],
            device_id=(dp, peer), device_id_type=MESH,
        )
        copy.start()
        copies.append(copy)
    for copy in copies:
        copy.wait_send()
    for offset in range(1, n_tensor):
        source = lax.rem(me + n_tensor - offset, n_tensor)
        pltpu.make_async_remote_copy(
            src_ref=send_ref.at[source], dst_ref=held.at[source],
            send_sem=a_send.at[offset], recv_sem=a_recv.at[offset],
            device_id=(dp, source), device_id_type=MESH,
        ).wait_recv()

    lanes = held.shape[2]
    peak = lax.fori_loop(
        0, n_tensor, lambda p, m: jnp.maximum(m, held[p][0:1, :]),
        jnp.full((1, lanes), -jnp.inf, jnp.float32),
    )

    def gather_sums(p, sums):
        mass, spread, target = sums
        block = held[p]
        gap = block[0:1, :] - peak
        factor = jnp.exp(gap)
        mass = mass + factor * block[1:2, :]
        spread = spread + factor * (block[2:3, :] + gap * block[1:2, :])
        return mass, spread, target + block[3:4, :]

    zero = jnp.zeros((1, lanes), jnp.float32)
    mass, spread, target = lax.fori_loop(0, n_tensor, gather_sums, (zero, zero, zero))
    log_mass = jnp.log(mass)
    logprob = target - peak - log_mass
    entropy = log_mass - spread / mass
    row = lax.broadcasted_iota(jnp.int32, own_ref.shape, 0)
    own_ref[...] = jnp.where(row == 0, logprob, jnp.where(row == 1, entropy, 0.0))

    spans = span_ref[...]
    partial = jnp.sum(spans[:, :lanes] * logprob, axis=1, keepdims=True) / spans[:, 127:128]
    part_msg[...] = jnp.broadcast_to(partial, part_msg.shape)
    t_held[me] = part_msg[...]
    copies = []
    for offset in range(1, n_tensor):
        peer = lax.rem(me + offset, n_tensor)
        copy = pltpu.make_async_remote_copy(
            src_ref=part_msg, dst_ref=t_held.at[me],
            send_sem=t_send.at[offset], recv_sem=t_recv.at[offset],
            device_id=(dp, peer), device_id_type=MESH,
        )
        copy.start()
        copies.append(copy)
    for copy in copies:
        copy.wait_send()
    for offset in range(1, n_tensor):
        source = lax.rem(me + n_tensor - offset, n_tensor)
        pltpu.make_async_remote_copy(
            src_ref=part_msg, dst_ref=t_held.at[source],
            send_sem=t_send.at[offset], recv_sem=t_recv.at[offset],
            device_id=(dp, source), device_id_type=MESH,
        ).wait_recv()

    total = jnp.sum(t_held[...], axis=0)
    lane = lax.broadcasted_iota(jnp.int32, total.shape, 1)
    route_msg[...] = jnp.where(lane == 0, total, jnp.where(lane == 1, ids_ref[...], 0.0))
    d_held[dp] = route_msg[...]
    copies = []
    for offset in range(1, n_dp):
        peer = lax.rem(dp + offset, n_dp)
        copy = pltpu.make_async_remote_copy(
            src_ref=route_msg, dst_ref=d_held.at[dp],
            send_sem=d_send.at[offset], recv_sem=d_recv.at[offset],
            device_id=(peer, me), device_id_type=MESH,
        )
        copy.start()
        copies.append(copy)
    for copy in copies:
        copy.wait_send()
    for offset in range(1, n_dp):
        source = lax.rem(dp + n_dp - offset, n_dp)
        pltpu.make_async_remote_copy(
            src_ref=route_msg, dst_ref=d_held.at[source],
            send_sem=d_send.at[offset], recv_sem=d_recv.at[offset],
            device_id=(source, me), device_id_type=MESH,
        ).wait_recv()
    routed_ref[...] = d_held[...]


def finish(blocks, spans, ids, n_tensor, n_dp):
    tile = spans.shape
    lanes = blocks.shape[2]
    return pl.pallas_call(
        lambda *refs: finish_kernel(n_tensor, n_dp, *refs),
        out_shape=(
            jax.ShapeDtypeStruct((8, lanes), jnp.float32),
            jax.ShapeDtypeStruct((n_dp,) + tile, jnp.float32),
        ),
        in_specs=[pl.BlockSpec(memory_space=pltpu.VMEM)] * 3,
        out_specs=(pl.BlockSpec(memory_space=pltpu.VMEM), pl.BlockSpec(memory_space=pltpu.VMEM)),
        scratch_shapes=[
            pltpu.VMEM(blocks.shape, jnp.float32),
            pltpu.VMEM((n_tensor,) + tile, jnp.float32),
            pltpu.VMEM((n_dp,) + tile, jnp.float32),
            pltpu.VMEM(tile, jnp.float32),
            pltpu.VMEM(tile, jnp.float32),
            pltpu.SemaphoreType.DMA((n_tensor,)),
            pltpu.SemaphoreType.DMA((n_tensor,)),
            pltpu.SemaphoreType.DMA((n_tensor,)),
            pltpu.SemaphoreType.DMA((n_tensor,)),
            pltpu.SemaphoreType.DMA((n_dp,)),
            pltpu.SemaphoreType.DMA((n_dp,)),
        ],
        compiler_params=pltpu.CompilerParams(collective_id=3, has_side_effects=True),
    )(blocks, spans, ids)


def prep_kernel(hidden_ref, gain_ref, mask_ref, ids_ref, out_ref):
    width = hidden_ref.shape[1]
    own_rows = hidden_ref.shape[0]
    widened = hidden_ref[...].astype(jnp.float32)
    inverse_rms = lax.rsqrt(jnp.mean(widened * widened, axis=1, keepdims=True) + EPSILON)
    normed = (widened * inverse_rms * gain_ref[...]).astype(jnp.bfloat16)
    live = jnp.broadcast_to(mask_ref[...].astype(jnp.float32), (8, own_rows))
    upper = (
        lax.broadcasted_iota(jnp.int32, (own_rows, own_rows), 0)
        <= lax.broadcasted_iota(jnp.int32, (own_rows, own_rows), 1)
    ).astype(jnp.float32)
    live_sum = jnp.dot(live, upper, preferred_element_type=jnp.float32)[0:1, :]
    rank = lax.broadcasted_iota(jnp.int32, (LIVE, own_rows), 0).astype(jnp.float32)
    chosen = ((live[0:1, :] == 1.0) & (live_sum - 1.0 == rank)).astype(jnp.bfloat16)
    out_ref[:, :width] = jnp.dot(chosen, normed, preferred_element_type=jnp.float32).astype(jnp.bfloat16)
    ids = ids_ref[...]
    high = lax.shift_right_logical(ids, 8).astype(jnp.float32)
    low = jnp.bitwise_and(ids, 255).astype(jnp.float32)
    row = lax.broadcasted_iota(jnp.int32, (128, own_rows), 0)
    meta_in = jnp.where(row == 0, high, jnp.where(row == 1, low, 0.0)).astype(jnp.bfloat16)
    meta = lax.dot_general(
        chosen, meta_in, (((1,), (1,)), ((), ())), preferred_element_type=jnp.float32
    )
    out_ref[:, width:] = meta.astype(jnp.bfloat16)


def prep(hidden, norm_gain, slot_mask, token_ids):
    own_rows, width = hidden.shape
    return pl.pallas_call(
        prep_kernel,
        out_shape=jax.ShapeDtypeStruct((LIVE, width + 128), jnp.bfloat16),
        in_specs=[pl.BlockSpec(memory_space=pltpu.VMEM)] * 4,
        out_specs=pl.BlockSpec(memory_space=pltpu.VMEM),
    )(hidden, norm_gain.reshape(1, width), slot_mask.reshape(1, own_rows), token_ids.reshape(1, own_rows))


def stats_kernel(x_ref, w_ref, out_ref):
    depth, vocab = w_ref.shape
    logits = jnp.dot(x_ref[:, :depth], w_ref[...], preferred_element_type=jnp.float32)
    meta = x_ref[:, depth:depth + 128].astype(jnp.float32)
    token = (meta[:, 0:1] * 256.0 + meta[:, 1:2]).astype(jnp.int32) - lax.axis_index("tensor") * vocab
    peak = jnp.max(logits, axis=1, keepdims=True)
    shifted = logits - peak
    weights = jnp.exp(shifted)
    mass = jnp.sum(weights, axis=1, keepdims=True)
    spread = jnp.sum(weights * shifted, axis=1, keepdims=True)
    column = lax.broadcasted_iota(jnp.int32, logits.shape, 1)
    target = jnp.sum(jnp.where(column == token, logits, 0.0), axis=1, keepdims=True)
    lane = lax.broadcasted_iota(jnp.int32, out_ref.shape, 1)
    out_ref[...] = jnp.where(
        lane == 0, peak, jnp.where(lane == 1, mass, jnp.where(lane == 2, spread, target))
    )


def row_stats(rows, weight, tile):
    count = rows.shape[0]
    depth, vocab = weight.shape
    return pl.pallas_call(
        stats_kernel,
        out_shape=jax.ShapeDtypeStruct((count, 128), jnp.float32),
        grid=(count // tile,),
        in_specs=[
            pl.BlockSpec((tile, rows.shape[1]), lambda i: (i, 0)),
            pl.BlockSpec((depth, vocab), lambda i: (0, 0)),
        ],
        out_specs=pl.BlockSpec((tile, 128), lambda i: (i, 0)),
        compiler_params=pltpu.CompilerParams(vmem_limit_bytes=56 * 1024 * 1024),
        cost_estimate=pl.CostEstimate(
            flops=2 * count * depth * vocab,
            transcendentals=count * vocab,
            bytes_accessed=2 * count * rows.shape[1] + 2 * depth * vocab + 512 * count,
        ),
    )(rows, weight)


def on_device(
    hidden, norm_gain, head_weight, value_weight, token_ids, slot_mask, lengths, request_order
):
    own_rows = hidden.shape[0]
    vocab_local = head_weight.shape[1]
    n_tensor = lax.axis_size("tensor")
    n_dp = lax.axis_size("dp")
    tensor_index = lax.axis_index("tensor")
    widened = hidden.astype(jnp.float32)
    inverse_rms = lax.rsqrt(jnp.mean(widened * widened, axis=1, keepdims=True) + EPSILON)
    normed = (widened * inverse_rms * norm_gain).astype(jnp.bfloat16)
    weight_mask = slot_mask.astype(jnp.float32)
    token_value = weight_mask * jnp.dot(normed, value_weight, preferred_element_type=jnp.float32)

    width = hidden.shape[1]
    live_sum = jnp.cumsum(slot_mask)
    slot_index = jnp.arange(own_rows, dtype=jnp.int32)
    chosen = (slot_mask[None, :] == 1) & (
        live_sum[None, :] - 1 == jnp.arange(LIVE, dtype=jnp.int32)[:, None]
    )
    source = jnp.sum(jnp.where(chosen, slot_index[None, :], 0), axis=1)
    block = prep(hidden, norm_gain, slot_mask, token_ids)
    gathered = lax.all_gather(block, "tensor", axis=0, tiled=True)
    row_count = gathered.shape[0]
    stats = row_stats(gathered, head_weight, 256 if row_count % 256 == 0 else row_count)
    blocks = stats[:, :4].reshape(n_tensor, LIVE, 4).transpose(0, 2, 1)
    request_count = lengths.shape[1]
    span_lengths = lengths[0]
    span_ends = jnp.cumsum(span_lengths)
    slot_ids = tensor_index * own_rows + source
    position = jnp.sum((slot_ids[:, None] >= span_ends[None, :]).astype(jnp.int32), axis=1)
    live = jnp.arange(LIVE, dtype=jnp.int32) < live_sum[-1]
    member = (position[None, :] == jnp.arange(8, dtype=jnp.int32)[:, None]) & live[None, :]
    spans = (
        jnp.zeros((8, 128), jnp.float32)
        .at[:, :LIVE].set(member.astype(jnp.float32))
        .at[:, 127].set(jnp.ones((8,), jnp.float32).at[:request_count].set(span_lengths.astype(jnp.float32)))
    )
    ids_tile = jnp.zeros((8, 128), jnp.float32).at[:request_count, 1].set(request_order.astype(jnp.float32))
    own, routed = finish(blocks, spans, ids_tile, n_tensor, n_dp)
    place = jnp.clip(live_sum - 1, 0, LIVE - 1)
    token_logprob = weight_mask * jnp.take(own[0], place)
    token_entropy = weight_mask * jnp.take(own[1], place)
    all_totals = routed[:, :request_count, 0].reshape(-1)
    all_owners = routed[:, :request_count, 1].reshape(-1)
    wanted = (lax.axis_index("dp") * request_count + jnp.arange(request_count)).astype(jnp.float32)
    route_table = all_owners[:, None] == wanted[None, :]
    request_score = jnp.sum(jnp.where(route_table, all_totals[:, None], 0.0), axis=0)
    return (token_logprob, token_entropy, token_value, request_score)


def solution(mesh):
    return jax.shard_map(
        on_device,
        mesh=mesh,
        in_specs=(
            P(("dp", "tensor"), None),
            P(),
            P(None, "tensor"),
            P(),
            P(("dp", "tensor")),
            P(("dp", "tensor")),
            P("dp", None),
            P("dp"),
        ),
        out_specs=(P(("dp", "tensor")), P(("dp", "tensor")), P(("dp", "tensor")), P("dp")),
        check_vma=False,
    )
```

```python
import jax
import jax.numpy as jnp
from jax import lax
from jax.experimental import pallas as pl
from jax.experimental.pallas import tpu as pltpu
from jax.sharding import PartitionSpec as P

EPSILON = 1e-06
MESH = pl.DeviceIdType.MESH
LIVE = 48


def exchange_kernel(n_tensor, send_ref, out_ref, held, send_sem, recv_sem):
    me = lax.axis_index("tensor")
    dp = lax.axis_index("dp")
    barrier = pltpu.get_barrier_semaphore()
    for offset in range(1, n_tensor):
        peer = lax.rem(me + offset, n_tensor)
        pl.semaphore_signal(barrier, inc=1, device_id=(dp, peer), device_id_type=MESH)
    pl.semaphore_wait(barrier, n_tensor - 1)
    held[me] = send_ref[me]
    copies = []
    for offset in range(1, n_tensor):
        peer = lax.rem(me + offset, n_tensor)
        copy = pltpu.make_async_remote_copy(
            src_ref=send_ref.at[peer],
            dst_ref=held.at[me],
            send_sem=send_sem.at[offset],
            recv_sem=recv_sem.at[offset],
            device_id=(dp, peer),
            device_id_type=MESH,
        )
        copy.start()
        copies.append(copy)
    for copy in copies:
        copy.wait_send()
    for offset in range(1, n_tensor):
        source = lax.rem(me + n_tensor - offset, n_tensor)
        pltpu.make_async_remote_copy(
            src_ref=send_ref.at[source],
            dst_ref=held.at[source],
            send_sem=send_sem.at[offset],
            recv_sem=recv_sem.at[offset],
            device_id=(dp, source),
            device_id_type=MESH,
        ).wait_recv()
    out_ref[...] = held[...]


def exchange(blocks, n_tensor):
    return pl.pallas_call(
        lambda *refs: exchange_kernel(n_tensor, *refs),
        out_shape=jax.ShapeDtypeStruct(blocks.shape, blocks.dtype),
        in_specs=[pl.BlockSpec(memory_space=pltpu.VMEM)],
        out_specs=pl.BlockSpec(memory_space=pltpu.VMEM),
        scratch_shapes=[
            pltpu.VMEM(blocks.shape, blocks.dtype),
            pltpu.SemaphoreType.DMA((n_tensor,)),
            pltpu.SemaphoreType.DMA((n_tensor,)),
        ],
        compiler_params=pltpu.CompilerParams(collective_id=0, has_side_effects=True),
    )(blocks)


def route_kernel(n_tensor, n_dp, part_ref, ids_ref, out_ref, t_held, d_held, msg,
                 t_send, t_recv, d_send, d_recv):
    me = lax.axis_index("tensor")
    dp = lax.axis_index("dp")
    barrier = pltpu.get_barrier_semaphore()
    for offset in range(1, n_tensor):
        peer = lax.rem(me + offset, n_tensor)
        pl.semaphore_signal(barrier, inc=1, device_id=(dp, peer), device_id_type=MESH)
    for offset in range(1, n_dp):
        peer = lax.rem(dp + offset, n_dp)
        pl.semaphore_signal(barrier, inc=1, device_id=(peer, me), device_id_type=MESH)
    pl.semaphore_wait(barrier, n_tensor - 1 + n_dp - 1)
    t_held[me] = part_ref[...]
    copies = []
    for offset in range(1, n_tensor):
        peer = lax.rem(me + offset, n_tensor)
        copy = pltpu.make_async_remote_copy(
            src_ref=part_ref,
            dst_ref=t_held.at[me],
            send_sem=t_send.at[offset],
            recv_sem=t_recv.at[offset],
            device_id=(dp, peer),
            device_id_type=MESH,
        )
        copy.start()
        copies.append(copy)
    for copy in copies:
        copy.wait_send()
    for offset in range(1, n_tensor):
        source = lax.rem(me + n_tensor - offset, n_tensor)
        pltpu.make_async_remote_copy(
            src_ref=part_ref,
            dst_ref=t_held.at[source],
            send_sem=t_send.at[offset],
            recv_sem=t_recv.at[offset],
            device_id=(dp, source),
            device_id_type=MESH,
        ).wait_recv()
    total = jnp.sum(t_held[...], axis=0)
    row = lax.broadcasted_iota(jnp.int32, total.shape, 0)
    msg[...] = jnp.where(row == 0, total, jnp.where(row == 1, ids_ref[...], 0.0))
    d_held[dp] = msg[...]
    copies = []
    for offset in range(1, n_dp):
        peer = lax.rem(dp + offset, n_dp)
        copy = pltpu.make_async_remote_copy(
            src_ref=msg,
            dst_ref=d_held.at[dp],
            send_sem=d_send.at[offset],
            recv_sem=d_recv.at[offset],
            device_id=(peer, me),
            device_id_type=MESH,
        )
        copy.start()
        copies.append(copy)
    for copy in copies:
        copy.wait_send()
    for offset in range(1, n_dp):
        source = lax.rem(dp + n_dp - offset, n_dp)
        pltpu.make_async_remote_copy(
            src_ref=msg,
            dst_ref=d_held.at[source],
            send_sem=d_send.at[offset],
            recv_sem=d_recv.at[offset],
            device_id=(source, me),
            device_id_type=MESH,
        ).wait_recv()
    out_ref[...] = d_held[...]


def route(part, ids, n_tensor, n_dp):
    tile = part.shape
    return pl.pallas_call(
        lambda *refs: route_kernel(n_tensor, n_dp, *refs),
        out_shape=jax.ShapeDtypeStruct((n_dp,) + tile, jnp.float32),
        in_specs=[pl.BlockSpec(memory_space=pltpu.VMEM)] * 2,
        out_specs=pl.BlockSpec(memory_space=pltpu.VMEM),
        scratch_shapes=[
            pltpu.VMEM((n_tensor,) + tile, jnp.float32),
            pltpu.VMEM((n_dp,) + tile, jnp.float32),
            pltpu.VMEM(tile, jnp.float32),
            pltpu.SemaphoreType.DMA((n_tensor,)),
            pltpu.SemaphoreType.DMA((n_tensor,)),
            pltpu.SemaphoreType.DMA((n_dp,)),
            pltpu.SemaphoreType.DMA((n_dp,)),
        ],
        compiler_params=pltpu.CompilerParams(collective_id=1, has_side_effects=True),
    )(part, ids)


def finish_kernel(n_tensor, n_dp, send_ref, span_ref, ids_ref, own_ref, routed_ref,
                  held, t_held, d_held, part_msg, route_msg,
                  a_send, a_recv, t_send, t_recv, d_send, d_recv):
    me = lax.axis_index("tensor")
    dp = lax.axis_index("dp")
    barrier = pltpu.get_barrier_semaphore()
    for offset in range(1, n_tensor):
        peer = lax.rem(me + offset, n_tensor)
        pl.semaphore_signal(barrier, inc=1, device_id=(dp, peer), device_id_type=MESH)
    for offset in range(1, n_dp):
        peer = lax.rem(dp + offset, n_dp)
        pl.semaphore_signal(barrier, inc=1, device_id=(peer, me), device_id_type=MESH)
    pl.semaphore_wait(barrier, n_tensor - 1 + n_dp - 1)

    held[me] = send_ref[me]
    copies = []
    for offset in range(1, n_tensor):
        peer = lax.rem(me + offset, n_tensor)
        copy = pltpu.make_async_remote_copy(
            src_ref=send_ref.at[peer], dst_ref=held.at[me],
            send_sem=a_send.at[offset], recv_sem=a_recv.at[offset],
            device_id=(dp, peer), device_id_type=MESH,
        )
        copy.start()
        copies.append(copy)
    for copy in copies:
        copy.wait_send()
    for offset in range(1, n_tensor):
        source = lax.rem(me + n_tensor - offset, n_tensor)
        pltpu.make_async_remote_copy(
            src_ref=send_ref.at[source], dst_ref=held.at[source],
            send_sem=a_send.at[offset], recv_sem=a_recv.at[offset],
            device_id=(dp, source), device_id_type=MESH,
        ).wait_recv()

    lanes = held.shape[2]
    peak = lax.fori_loop(
        0, n_tensor, lambda p, m: jnp.maximum(m, held[p][0:1, :]),
        jnp.full((1, lanes), -jnp.inf, jnp.float32),
    )

    def gather_sums(p, sums):
        mass, spread, target = sums
        block = held[p]
        gap = block[0:1, :] - peak
        factor = jnp.exp(gap)
        mass = mass + factor * block[1:2, :]
        spread = spread + factor * (block[2:3, :] + gap * block[1:2, :])
        return mass, spread, target + block[3:4, :]

    zero = jnp.zeros((1, lanes), jnp.float32)
    mass, spread, target = lax.fori_loop(0, n_tensor, gather_sums, (zero, zero, zero))
    log_mass = jnp.log(mass)
    logprob = target - peak - log_mass
    entropy = log_mass - spread / mass
    row = lax.broadcasted_iota(jnp.int32, own_ref.shape, 0)
    own_ref[...] = jnp.where(row == 0, logprob, jnp.where(row == 1, entropy, 0.0))

    spans = span_ref[...]
    partial = jnp.sum(spans[:, :lanes] * logprob, axis=1, keepdims=True) / spans[:, 127:128]
    part_msg[...] = jnp.broadcast_to(partial, part_msg.shape)
    t_held[me] = part_msg[...]
    copies = []
    for offset in range(1, n_tensor):
        peer = lax.rem(me + offset, n_tensor)
        copy = pltpu.make_async_remote_copy(
            src_ref=part_msg, dst_ref=t_held.at[me],
            send_sem=t_send.at[offset], recv_sem=t_recv.at[offset],
            device_id=(dp, peer), device_id_type=MESH,
        )
        copy.start()
        copies.append(copy)
    for copy in copies:
        copy.wait_send()
    for offset in range(1, n_tensor):
        source = lax.rem(me + n_tensor - offset, n_tensor)
        pltpu.make_async_remote_copy(
            src_ref=part_msg, dst_ref=t_held.at[source],
            send_sem=t_send.at[offset], recv_sem=t_recv.at[offset],
            device_id=(dp, source), device_id_type=MESH,
        ).wait_recv()

    total = jnp.sum(t_held[...], axis=0)
    lane = lax.broadcasted_iota(jnp.int32, total.shape, 1)
    route_msg[...] = jnp.where(lane == 0, total, jnp.where(lane == 1, ids_ref[...], 0.0))
    d_held[dp] = route_msg[...]
    copies = []
    for offset in range(1, n_dp):
        peer = lax.rem(dp + offset, n_dp)
        copy = pltpu.make_async_remote_copy(
            src_ref=route_msg, dst_ref=d_held.at[dp],
            send_sem=d_send.at[offset], recv_sem=d_recv.at[offset],
            device_id=(peer, me), device_id_type=MESH,
        )
        copy.start()
        copies.append(copy)
    for copy in copies:
        copy.wait_send()
    for offset in range(1, n_dp):
        source = lax.rem(dp + n_dp - offset, n_dp)
        pltpu.make_async_remote_copy(
            src_ref=route_msg, dst_ref=d_held.at[source],
            send_sem=d_send.at[offset], recv_sem=d_recv.at[offset],
            device_id=(source, me), device_id_type=MESH,
        ).wait_recv()
    routed_ref[...] = d_held[...]


def finish(blocks, spans, ids, n_tensor, n_dp):
    tile = spans.shape
    lanes = blocks.shape[2]
    return pl.pallas_call(
        lambda *refs: finish_kernel(n_tensor, n_dp, *refs),
        out_shape=(
            jax.ShapeDtypeStruct((8, lanes), jnp.float32),
            jax.ShapeDtypeStruct((n_dp,) + tile, jnp.float32),
        ),
        in_specs=[pl.BlockSpec(memory_space=pltpu.VMEM)] * 3,
        out_specs=(pl.BlockSpec(memory_space=pltpu.VMEM), pl.BlockSpec(memory_space=pltpu.VMEM)),
        scratch_shapes=[
            pltpu.VMEM(blocks.shape, jnp.float32),
            pltpu.VMEM((n_tensor,) + tile, jnp.float32),
            pltpu.VMEM((n_dp,) + tile, jnp.float32),
            pltpu.VMEM(tile, jnp.float32),
            pltpu.VMEM(tile, jnp.float32),
            pltpu.SemaphoreType.DMA((n_tensor,)),
            pltpu.SemaphoreType.DMA((n_tensor,)),
            pltpu.SemaphoreType.DMA((n_tensor,)),
            pltpu.SemaphoreType.DMA((n_tensor,)),
            pltpu.SemaphoreType.DMA((n_dp,)),
            pltpu.SemaphoreType.DMA((n_dp,)),
        ],
        compiler_params=pltpu.CompilerParams(collective_id=3, has_side_effects=True),
    )(blocks, spans, ids)


def prep_kernel(hidden_ref, gain_ref, mask_ref, ids_ref, out_ref):
    width = hidden_ref.shape[1]
    own_rows = hidden_ref.shape[0]
    widened = hidden_ref[...].astype(jnp.float32)
    inverse_rms = lax.rsqrt(jnp.mean(widened * widened, axis=1, keepdims=True) + EPSILON)
    normed = (widened * inverse_rms * gain_ref[...]).astype(jnp.bfloat16)
    live = jnp.broadcast_to(mask_ref[...].astype(jnp.float32), (8, own_rows))
    upper = (
        lax.broadcasted_iota(jnp.int32, (own_rows, own_rows), 0)
        <= lax.broadcasted_iota(jnp.int32, (own_rows, own_rows), 1)
    ).astype(jnp.float32)
    live_sum = jnp.dot(live, upper, preferred_element_type=jnp.float32)[0:1, :]
    rank = lax.broadcasted_iota(jnp.int32, (LIVE, own_rows), 0).astype(jnp.float32)
    chosen = ((live[0:1, :] == 1.0) & (live_sum - 1.0 == rank)).astype(jnp.bfloat16)
    out_ref[:, :width] = jnp.dot(chosen, normed, preferred_element_type=jnp.float32).astype(jnp.bfloat16)
    ids = ids_ref[...]
    high = lax.shift_right_logical(ids, 8).astype(jnp.float32)
    low = jnp.bitwise_and(ids, 255).astype(jnp.float32)
    row = lax.broadcasted_iota(jnp.int32, (128, own_rows), 0)
    meta_in = jnp.where(row == 0, high, jnp.where(row == 1, low, 0.0)).astype(jnp.bfloat16)
    meta = lax.dot_general(
        chosen, meta_in, (((1,), (1,)), ((), ())), preferred_element_type=jnp.float32
    )
    out_ref[:, width:] = meta.astype(jnp.bfloat16)


def prep(hidden, norm_gain, slot_mask, token_ids):
    own_rows, width = hidden.shape
    return pl.pallas_call(
        prep_kernel,
        out_shape=jax.ShapeDtypeStruct((LIVE, width + 128), jnp.bfloat16),
        in_specs=[pl.BlockSpec(memory_space=pltpu.VMEM)] * 4,
        out_specs=pl.BlockSpec(memory_space=pltpu.VMEM),
    )(hidden, norm_gain.reshape(1, width), slot_mask.reshape(1, own_rows), token_ids.reshape(1, own_rows))


def stats_kernel(x_ref, w_ref, out_ref):
    depth, vocab = w_ref.shape
    logits = jnp.dot(x_ref[:, :depth], w_ref[...], preferred_element_type=jnp.float32)
    meta = x_ref[:, depth:depth + 128].astype(jnp.float32)
    token = (meta[:, 0:1] * 256.0 + meta[:, 1:2]).astype(jnp.int32) - lax.axis_index("tensor") * vocab
    peak = jnp.max(logits, axis=1, keepdims=True)
    shifted = logits - peak
    weights = jnp.exp(shifted)
    mass = jnp.sum(weights, axis=1, keepdims=True)
    spread = jnp.sum(weights * shifted, axis=1, keepdims=True)
    column = lax.broadcasted_iota(jnp.int32, logits.shape, 1)
    target = jnp.sum(jnp.where(column == token, logits, 0.0), axis=1, keepdims=True)
    lane = lax.broadcasted_iota(jnp.int32, out_ref.shape, 1)
    out_ref[...] = jnp.where(
        lane == 0, peak, jnp.where(lane == 1, mass, jnp.where(lane == 2, spread, target))
    )


def row_stats(rows, weight, tile):
    count = rows.shape[0]
    depth, vocab = weight.shape
    return pl.pallas_call(
        stats_kernel,
        out_shape=jax.ShapeDtypeStruct((count, 128), jnp.float32),
        grid=(count // tile,),
        in_specs=[
            pl.BlockSpec((tile, rows.shape[1]), lambda i: (i, 0)),
            pl.BlockSpec((depth, vocab), lambda i: (0, 0)),
        ],
        out_specs=pl.BlockSpec((tile, 128), lambda i: (i, 0)),
        compiler_params=pltpu.CompilerParams(vmem_limit_bytes=56 * 1024 * 1024),
        cost_estimate=pl.CostEstimate(
            flops=2 * count * depth * vocab,
            transcendentals=count * vocab,
            bytes_accessed=2 * count * rows.shape[1] + 2 * depth * vocab + 512 * count,
        ),
    )(rows, weight)


def on_device(
    hidden, norm_gain, head_weight, value_weight, token_ids, slot_mask, lengths, request_order
):
    own_rows = hidden.shape[0]
    vocab_local = head_weight.shape[1]
    n_tensor = lax.axis_size("tensor")
    n_dp = lax.axis_size("dp")
    tensor_index = lax.axis_index("tensor")
    widened = hidden.astype(jnp.float32)
    inverse_rms = lax.rsqrt(jnp.mean(widened * widened, axis=1, keepdims=True) + EPSILON)
    normed = (widened * inverse_rms * norm_gain).astype(jnp.bfloat16)
    weight_mask = slot_mask.astype(jnp.float32)
    token_value = weight_mask * jnp.dot(normed, value_weight, preferred_element_type=jnp.float32)

    width = hidden.shape[1]
    live_sum = jnp.cumsum(slot_mask)
    slot_index = jnp.arange(own_rows, dtype=jnp.int32)
    chosen = (slot_mask[None, :] == 1) & (
        live_sum[None, :] - 1 == jnp.arange(LIVE, dtype=jnp.int32)[:, None]
    )
    source = jnp.sum(jnp.where(chosen, slot_index[None, :], 0), axis=1)
    block = prep(hidden, norm_gain, slot_mask, token_ids)
    gathered = lax.all_gather(block, "tensor", axis=0, tiled=True)
    row_count = gathered.shape[0]
    stats = row_stats(gathered, head_weight, 512 if row_count % 512 == 0 else row_count)
    blocks = stats[:, :4].reshape(n_tensor, LIVE, 4).transpose(0, 2, 1)
    request_count = lengths.shape[1]
    span_lengths = lengths[0]
    span_ends = jnp.cumsum(span_lengths)
    slot_ids = tensor_index * own_rows + source
    position = jnp.sum((slot_ids[:, None] >= span_ends[None, :]).astype(jnp.int32), axis=1)
    live = jnp.arange(LIVE, dtype=jnp.int32) < live_sum[-1]
    member = (position[None, :] == jnp.arange(8, dtype=jnp.int32)[:, None]) & live[None, :]
    spans = (
        jnp.zeros((8, 128), jnp.float32)
        .at[:, :LIVE].set(member.astype(jnp.float32))
        .at[:, 127].set(jnp.ones((8,), jnp.float32).at[:request_count].set(span_lengths.astype(jnp.float32)))
    )
    ids_tile = jnp.zeros((8, 128), jnp.float32).at[:request_count, 1].set(request_order.astype(jnp.float32))
    own, routed = finish(blocks, spans, ids_tile, n_tensor, n_dp)
    place = jnp.clip(live_sum - 1, 0, LIVE - 1)
    token_logprob = weight_mask * jnp.take(own[0], place)
    token_entropy = weight_mask * jnp.take(own[1], place)
    all_totals = routed[:, :request_count, 0].reshape(-1)
    all_owners = routed[:, :request_count, 1].reshape(-1)
    wanted = (lax.axis_index("dp") * request_count + jnp.arange(request_count)).astype(jnp.float32)
    route_table = all_owners[:, None] == wanted[None, :]
    request_score = jnp.sum(jnp.where(route_table, all_totals[:, None], 0.0), axis=0)
    return (token_logprob, token_entropy, token_value, request_score)


def solution(mesh):
    return jax.shard_map(
        on_device,
        mesh=mesh,
        in_specs=(
            P(("dp", "tensor"), None),
            P(),
            P(None, "tensor"),
            P(),
            P(("dp", "tensor")),
            P(("dp", "tensor")),
            P("dp", None),
            P("dp"),
        ),
        out_specs=(P(("dp", "tensor")), P(("dp", "tensor")), P(("dp", "tensor")), P("dp")),
        check_vma=False,
    )
```

```python
import jax
import jax.numpy as jnp
from jax import lax
from jax.experimental import pallas as pl
from jax.experimental.pallas import tpu as pltpu
from jax.sharding import PartitionSpec as P

EPSILON = 1e-06
MESH = pl.DeviceIdType.MESH
LIVE = 48


def finish_kernel(n_tensor, n_dp, send_ref, span_ref, ids_ref, spread_ref, logprob_ref, entropy_ref, score_ref,
                  held, t_held, d_held, part_msg, route_msg,
                  a_send, a_recv, t_send, t_recv, d_send, d_recv):
    me = lax.axis_index("tensor")
    dp = lax.axis_index("dp")
    barrier = pltpu.get_barrier_semaphore()
    for offset in range(1, n_tensor):
        peer = lax.rem(me + offset, n_tensor)
        pl.semaphore_signal(barrier, inc=1, device_id=(dp, peer), device_id_type=MESH)
    for offset in range(1, n_dp):
        peer = lax.rem(dp + offset, n_dp)
        pl.semaphore_signal(barrier, inc=1, device_id=(peer, me), device_id_type=MESH)
    pl.semaphore_wait(barrier, n_tensor - 1 + n_dp - 1)

    held[me] = send_ref[me]
    copies = []
    for offset in range(1, n_tensor):
        peer = lax.rem(me + offset, n_tensor)
        copy = pltpu.make_async_remote_copy(
            src_ref=send_ref.at[peer], dst_ref=held.at[me],
            send_sem=a_send.at[offset], recv_sem=a_recv.at[offset],
            device_id=(dp, peer), device_id_type=MESH,
        )
        copy.start()
        copies.append(copy)
    for copy in copies:
        copy.wait_send()
    for offset in range(1, n_tensor):
        source = lax.rem(me + n_tensor - offset, n_tensor)
        pltpu.make_async_remote_copy(
            src_ref=send_ref.at[source], dst_ref=held.at[source],
            send_sem=a_send.at[offset], recv_sem=a_recv.at[offset],
            device_id=(dp, source), device_id_type=MESH,
        ).wait_recv()

    lanes = held.shape[2]
    peak = lax.fori_loop(
        0, n_tensor, lambda p, m: jnp.maximum(m, held[p][0:1, :]),
        jnp.full((1, lanes), -jnp.inf, jnp.float32),
    )

    def gather_sums(p, sums):
        mass, spread, target = sums
        block = held[p]
        gap = block[0:1, :] - peak
        factor = jnp.exp(gap)
        mass = mass + factor * block[1:2, :]
        spread = spread + factor * (block[2:3, :] + gap * block[1:2, :])
        return mass, spread, target + block[3:4, :]

    zero = jnp.zeros((1, lanes), jnp.float32)
    mass, spread, target = lax.fori_loop(0, n_tensor, gather_sums, (zero, zero, zero))
    log_mass = jnp.log(mass)
    logprob = target - peak - log_mass
    entropy = log_mass - spread / mass
    slots = spread_ref.shape[0]
    placed = spread_ref[...] > 0.0
    same = (
        lax.broadcasted_iota(jnp.int32, (slots, slots), 0)
        == lax.broadcasted_iota(jnp.int32, (slots, slots), 1)
    )
    for value, out in ((logprob, logprob_ref), (entropy, entropy_ref)):
        column = jnp.sum(jnp.where(placed, value, 0.0), axis=1, keepdims=True)
        out[...] = jnp.sum(jnp.where(same, column, 0.0), axis=0, keepdims=True)

    spans = span_ref[...]
    partial = jnp.sum(spans[:, :lanes] * logprob, axis=1, keepdims=True) / spans[:, 127:128]
    part_msg[...] = jnp.broadcast_to(partial, part_msg.shape)
    t_held[me] = part_msg[...]
    copies = []
    for offset in range(1, n_tensor):
        peer = lax.rem(me + offset, n_tensor)
        copy = pltpu.make_async_remote_copy(
            src_ref=part_msg, dst_ref=t_held.at[me],
            send_sem=t_send.at[offset], recv_sem=t_recv.at[offset],
            device_id=(dp, peer), device_id_type=MESH,
        )
        copy.start()
        copies.append(copy)
    for copy in copies:
        copy.wait_send()
    for offset in range(1, n_tensor):
        source = lax.rem(me + n_tensor - offset, n_tensor)
        pltpu.make_async_remote_copy(
            src_ref=part_msg, dst_ref=t_held.at[source],
            send_sem=t_send.at[offset], recv_sem=t_recv.at[offset],
            device_id=(dp, source), device_id_type=MESH,
        ).wait_recv()

    total = jnp.sum(t_held[...], axis=0)
    lane = lax.broadcasted_iota(jnp.int32, total.shape, 1)
    route_msg[...] = jnp.where(lane == 0, total, jnp.where(lane == 1, ids_ref[...], 0.0))
    d_held[dp] = route_msg[...]
    copies = []
    for offset in range(1, n_dp):
        peer = lax.rem(dp + offset, n_dp)
        copy = pltpu.make_async_remote_copy(
            src_ref=route_msg, dst_ref=d_held.at[dp],
            send_sem=d_send.at[offset], recv_sem=d_recv.at[offset],
            device_id=(peer, me), device_id_type=MESH,
        )
        copy.start()
        copies.append(copy)
    for copy in copies:
        copy.wait_send()
    for offset in range(1, n_dp):
        source = lax.rem(dp + n_dp - offset, n_dp)
        pltpu.make_async_remote_copy(
            src_ref=route_msg, dst_ref=d_held.at[source],
            send_sem=d_send.at[offset], recv_sem=d_recv.at[offset],
            device_id=(source, me), device_id_type=MESH,
        ).wait_recv()
    count = score_ref.shape[1]
    wanted = (dp * count + lax.broadcasted_iota(jnp.int32, (1, count), 1)).astype(jnp.float32)
    score = jnp.zeros((1, count), jnp.float32)
    for group in range(n_dp):
        block = d_held[group]
        hit = block[:count, 1:2] == wanted
        score = score + jnp.sum(jnp.where(hit, block[:count, 0:1], 0.0), axis=0, keepdims=True)
    score_ref[...] = score


def finish(blocks, spans, ids, spread, n_tensor, n_dp, count):
    tile = spans.shape
    lanes = blocks.shape[2]
    return pl.pallas_call(
        lambda *refs: finish_kernel(n_tensor, n_dp, *refs),
        out_shape=(
            jax.ShapeDtypeStruct((1, spread.shape[0]), jnp.float32),
            jax.ShapeDtypeStruct((1, spread.shape[0]), jnp.float32),
            jax.ShapeDtypeStruct((1, count), jnp.float32),
        ),
        in_specs=[pl.BlockSpec(memory_space=pltpu.VMEM)] * 4,
        out_specs=(pl.BlockSpec(memory_space=pltpu.VMEM),) * 3,
        scratch_shapes=[
            pltpu.VMEM(blocks.shape, jnp.float32),
            pltpu.VMEM((n_tensor,) + tile, jnp.float32),
            pltpu.VMEM((n_dp,) + tile, jnp.float32),
            pltpu.VMEM(tile, jnp.float32),
            pltpu.VMEM(tile, jnp.float32),
            pltpu.SemaphoreType.DMA((n_tensor,)),
            pltpu.SemaphoreType.DMA((n_tensor,)),
            pltpu.SemaphoreType.DMA((n_tensor,)),
            pltpu.SemaphoreType.DMA((n_tensor,)),
            pltpu.SemaphoreType.DMA((n_dp,)),
            pltpu.SemaphoreType.DMA((n_dp,)),
        ],
        compiler_params=pltpu.CompilerParams(collective_id=3, has_side_effects=True),
    )(blocks, spans, ids, spread)


def prep_kernel(hidden_ref, gain_ref, mask_ref, ids_ref, out_ref):
    width = hidden_ref.shape[1]
    own_rows = hidden_ref.shape[0]
    widened = hidden_ref[...].astype(jnp.float32)
    inverse_rms = lax.rsqrt(jnp.mean(widened * widened, axis=1, keepdims=True) + EPSILON)
    normed = (widened * inverse_rms * gain_ref[...]).astype(jnp.bfloat16)
    live = jnp.broadcast_to(mask_ref[...].astype(jnp.float32), (8, own_rows))
    upper = (
        lax.broadcasted_iota(jnp.int32, (own_rows, own_rows), 0)
        <= lax.broadcasted_iota(jnp.int32, (own_rows, own_rows), 1)
    ).astype(jnp.float32)
    live_sum = jnp.dot(live, upper, preferred_element_type=jnp.float32)[0:1, :]
    rank = lax.broadcasted_iota(jnp.int32, (LIVE, own_rows), 0).astype(jnp.float32)
    chosen = ((live[0:1, :] == 1.0) & (live_sum - 1.0 == rank)).astype(jnp.bfloat16)
    out_ref[:, :width] = jnp.dot(chosen, normed, preferred_element_type=jnp.float32).astype(jnp.bfloat16)
    ids = ids_ref[...]
    high = lax.shift_right_logical(ids, 8).astype(jnp.float32)
    low = jnp.bitwise_and(ids, 255).astype(jnp.float32)
    row = lax.broadcasted_iota(jnp.int32, (128, own_rows), 0)
    meta_in = jnp.where(row == 0, high, jnp.where(row == 1, low, 0.0)).astype(jnp.bfloat16)
    meta = lax.dot_general(
        chosen, meta_in, (((1,), (1,)), ((), ())), preferred_element_type=jnp.float32
    )
    out_ref[:, width:] = meta.astype(jnp.bfloat16)


def prep(hidden, norm_gain, slot_mask, token_ids):
    own_rows, width = hidden.shape
    return pl.pallas_call(
        prep_kernel,
        out_shape=jax.ShapeDtypeStruct((LIVE, width + 128), jnp.bfloat16),
        in_specs=[pl.BlockSpec(memory_space=pltpu.VMEM)] * 4,
        out_specs=pl.BlockSpec(memory_space=pltpu.VMEM),
    )(hidden, norm_gain.reshape(1, width), slot_mask.reshape(1, own_rows), token_ids.reshape(1, own_rows))


def stats_kernel(x_ref, w_ref, out_ref):
    depth, vocab = w_ref.shape
    logits = jnp.dot(x_ref[:, :depth], w_ref[...], preferred_element_type=jnp.float32)
    meta = x_ref[:, depth:depth + 128].astype(jnp.float32)
    token = (meta[:, 0:1] * 256.0 + meta[:, 1:2]).astype(jnp.int32) - lax.axis_index("tensor") * vocab
    peak = jnp.max(logits, axis=1, keepdims=True)
    shifted = logits - peak
    weights = jnp.exp(shifted)
    mass = jnp.sum(weights, axis=1, keepdims=True)
    spread = jnp.sum(weights * shifted, axis=1, keepdims=True)
    column = lax.broadcasted_iota(jnp.int32, logits.shape, 1)
    target = jnp.sum(jnp.where(column == token, logits, 0.0), axis=1, keepdims=True)
    lane = lax.broadcasted_iota(jnp.int32, out_ref.shape, 1)
    out_ref[...] = jnp.where(
        lane == 0, peak, jnp.where(lane == 1, mass, jnp.where(lane == 2, spread, target))
    )


def row_stats(rows, weight, tile):
    count = rows.shape[0]
    depth, vocab = weight.shape
    return pl.pallas_call(
        stats_kernel,
        out_shape=jax.ShapeDtypeStruct((count, 128), jnp.float32),
        grid=(count // tile,),
        in_specs=[
            pl.BlockSpec((tile, rows.shape[1]), lambda i: (i, 0)),
            pl.BlockSpec((depth, vocab), lambda i: (0, 0)),
        ],
        out_specs=pl.BlockSpec((tile, 128), lambda i: (i, 0)),
        compiler_params=pltpu.CompilerParams(vmem_limit_bytes=56 * 1024 * 1024),
        cost_estimate=pl.CostEstimate(
            flops=2 * count * depth * vocab,
            transcendentals=count * vocab,
            bytes_accessed=2 * count * rows.shape[1] + 2 * depth * vocab + 512 * count,
        ),
    )(rows, weight)


def on_device(
    hidden, norm_gain, head_weight, value_weight, token_ids, slot_mask, lengths, request_order
):
    own_rows = hidden.shape[0]
    vocab_local = head_weight.shape[1]
    n_tensor = lax.axis_size("tensor")
    n_dp = lax.axis_size("dp")
    tensor_index = lax.axis_index("tensor")
    widened = hidden.astype(jnp.float32)
    inverse_rms = lax.rsqrt(jnp.mean(widened * widened, axis=1, keepdims=True) + EPSILON)
    normed = (widened * inverse_rms * norm_gain).astype(jnp.bfloat16)
    weight_mask = slot_mask.astype(jnp.float32)
    token_value = weight_mask * jnp.dot(normed, value_weight, preferred_element_type=jnp.float32)

    width = hidden.shape[1]
    live_sum = jnp.cumsum(slot_mask)
    slot_index = jnp.arange(own_rows, dtype=jnp.int32)
    chosen = (slot_mask[None, :] == 1) & (
        live_sum[None, :] - 1 == jnp.arange(LIVE, dtype=jnp.int32)[:, None]
    )
    source = jnp.sum(jnp.where(chosen, slot_index[None, :], 0), axis=1)
    block = prep(hidden, norm_gain, slot_mask, token_ids)
    gathered = lax.all_gather(block, "tensor", axis=0, tiled=True)
    row_count = gathered.shape[0]
    stats = row_stats(gathered, head_weight, 256 if row_count % 256 == 0 else row_count)
    blocks = stats[:, :4].reshape(n_tensor, LIVE, 4).transpose(0, 2, 1)
    request_count = lengths.shape[1]
    span_lengths = lengths[0]
    span_ends = jnp.cumsum(span_lengths)
    slot_ids = tensor_index * own_rows + source
    position = jnp.sum((slot_ids[:, None] >= span_ends[None, :]).astype(jnp.int32), axis=1)
    live = jnp.arange(LIVE, dtype=jnp.int32) < live_sum[-1]
    member = (position[None, :] == jnp.arange(8, dtype=jnp.int32)[:, None]) & live[None, :]
    spans = (
        jnp.zeros((8, 128), jnp.float32)
        .at[:, :LIVE].set(member.astype(jnp.float32))
        .at[:, 127].set(jnp.ones((8,), jnp.float32).at[:request_count].set(span_lengths.astype(jnp.float32)))
    )
    ids_tile = jnp.zeros((8, 128), jnp.float32).at[:request_count, 1].set(request_order.astype(jnp.float32))
    place = live_sum - 1
    spread = ((place[:, None] == jnp.arange(LIVE, dtype=jnp.int32)[None, :]) & (slot_mask[:, None] == 1))
    logprob_row, entropy_row, score_row = finish(
        blocks, spans, ids_tile, spread.astype(jnp.float32), n_tensor, n_dp, request_count
    )
    token_logprob = logprob_row.reshape(own_rows)
    token_entropy = entropy_row.reshape(own_rows)
    request_score = score_row.reshape(request_count)
    return (token_logprob, token_entropy, token_value, request_score)


def solution(mesh):
    return jax.shard_map(
        on_device,
        mesh=mesh,
        in_specs=(
            P(("dp", "tensor"), None),
            P(),
            P(None, "tensor"),
            P(),
            P(("dp", "tensor")),
            P(("dp", "tensor")),
            P("dp", None),
            P("dp"),
        ),
        out_specs=(P(("dp", "tensor")), P(("dp", "tensor")), P(("dp", "tensor")), P("dp")),
        check_vma=False,
    )
```

```python
import jax
import jax.numpy as jnp
from jax import lax
from jax.experimental import pallas as pl
from jax.experimental.pallas import tpu as pltpu
from jax.sharding import PartitionSpec as P

EPSILON = 1e-06
MESH = pl.DeviceIdType.MESH
LIVE = 48


def finish_kernel(n_tensor, n_dp, count, send_ref, span_ref, ids_ref, spread_ref, result_ref,
                  held, t_held, d_held, part_msg, route_msg,
                  a_send, a_recv, t_send, t_recv, d_send, d_recv):
    me = lax.axis_index("tensor")
    dp = lax.axis_index("dp")
    barrier = pltpu.get_barrier_semaphore()
    for offset in range(1, n_tensor):
        peer = lax.rem(me + offset, n_tensor)
        pl.semaphore_signal(barrier, inc=1, device_id=(dp, peer), device_id_type=MESH)
    for offset in range(1, n_dp):
        peer = lax.rem(dp + offset, n_dp)
        pl.semaphore_signal(barrier, inc=1, device_id=(peer, me), device_id_type=MESH)
    pl.semaphore_wait(barrier, n_tensor - 1 + n_dp - 1)

    held[me] = send_ref[me]
    copies = []
    for offset in range(1, n_tensor):
        peer = lax.rem(me + offset, n_tensor)
        copy = pltpu.make_async_remote_copy(
            src_ref=send_ref.at[peer], dst_ref=held.at[me],
            send_sem=a_send.at[offset], recv_sem=a_recv.at[offset],
            device_id=(dp, peer), device_id_type=MESH,
        )
        copy.start()
        copies.append(copy)
    for copy in copies:
        copy.wait_send()
    for offset in range(1, n_tensor):
        source = lax.rem(me + n_tensor - offset, n_tensor)
        pltpu.make_async_remote_copy(
            src_ref=send_ref.at[source], dst_ref=held.at[source],
            send_sem=a_send.at[offset], recv_sem=a_recv.at[offset],
            device_id=(dp, source), device_id_type=MESH,
        ).wait_recv()

    lanes = held.shape[2]
    peak = lax.fori_loop(
        0, n_tensor, lambda p, m: jnp.maximum(m, held[p][0:1, :]),
        jnp.full((1, lanes), -jnp.inf, jnp.float32),
    )

    def gather_sums(p, sums):
        mass, spread, target = sums
        block = held[p]
        gap = block[0:1, :] - peak
        factor = jnp.exp(gap)
        mass = mass + factor * block[1:2, :]
        spread = spread + factor * (block[2:3, :] + gap * block[1:2, :])
        return mass, spread, target + block[3:4, :]

    zero = jnp.zeros((1, lanes), jnp.float32)
    mass, spread, target = lax.fori_loop(0, n_tensor, gather_sums, (zero, zero, zero))
    log_mass = jnp.log(mass)
    logprob = target - peak - log_mass
    entropy = log_mass - spread / mass
    slots = spread_ref.shape[0]
    placed = spread_ref[...] > 0.0
    same = (
        lax.broadcasted_iota(jnp.int32, (slots, slots), 0)
        == lax.broadcasted_iota(jnp.int32, (slots, slots), 1)
    )
    result_ref[...] = jnp.zeros(result_ref.shape, jnp.float32)
    for index, value in enumerate((logprob, entropy)):
        column = jnp.sum(jnp.where(placed, value, 0.0), axis=1, keepdims=True)
        result_ref[index:index + 1, :slots] = jnp.sum(jnp.where(same, column, 0.0), axis=0, keepdims=True)

    spans = span_ref[...]
    partial = jnp.sum(spans[:, :lanes] * logprob, axis=1, keepdims=True) / spans[:, 127:128]
    part_msg[...] = jnp.broadcast_to(partial, part_msg.shape)
    t_held[me] = part_msg[...]
    copies = []
    for offset in range(1, n_tensor):
        peer = lax.rem(me + offset, n_tensor)
        copy = pltpu.make_async_remote_copy(
            src_ref=part_msg, dst_ref=t_held.at[me],
            send_sem=t_send.at[offset], recv_sem=t_recv.at[offset],
            device_id=(dp, peer), device_id_type=MESH,
        )
        copy.start()
        copies.append(copy)
    for copy in copies:
        copy.wait_send()
    for offset in range(1, n_tensor):
        source = lax.rem(me + n_tensor - offset, n_tensor)
        pltpu.make_async_remote_copy(
            src_ref=part_msg, dst_ref=t_held.at[source],
            send_sem=t_send.at[offset], recv_sem=t_recv.at[offset],
            device_id=(dp, source), device_id_type=MESH,
        ).wait_recv()

    total = jnp.sum(t_held[...], axis=0)
    lane = lax.broadcasted_iota(jnp.int32, total.shape, 1)
    route_msg[...] = jnp.where(lane == 0, total, jnp.where(lane == 1, ids_ref[...], 0.0))
    d_held[dp] = route_msg[...]
    copies = []
    for offset in range(1, n_dp):
        peer = lax.rem(dp + offset, n_dp)
        copy = pltpu.make_async_remote_copy(
            src_ref=route_msg, dst_ref=d_held.at[dp],
            send_sem=d_send.at[offset], recv_sem=d_recv.at[offset],
            device_id=(peer, me), device_id_type=MESH,
        )
        copy.start()
        copies.append(copy)
    for copy in copies:
        copy.wait_send()
    for offset in range(1, n_dp):
        source = lax.rem(dp + n_dp - offset, n_dp)
        pltpu.make_async_remote_copy(
            src_ref=route_msg, dst_ref=d_held.at[source],
            send_sem=d_send.at[offset], recv_sem=d_recv.at[offset],
            device_id=(source, me), device_id_type=MESH,
        ).wait_recv()
    wanted = (dp * count + lax.broadcasted_iota(jnp.int32, (1, count), 1)).astype(jnp.float32)
    score = jnp.zeros((1, count), jnp.float32)
    for group in range(n_dp):
        block = d_held[group]
        hit = block[:count, 1:2] == wanted
        score = score + jnp.sum(jnp.where(hit, block[:count, 0:1], 0.0), axis=0, keepdims=True)
    result_ref[2:3, :count] = score


def finish(blocks, spans, ids, spread, n_tensor, n_dp, count):
    tile = spans.shape
    lanes = blocks.shape[2]
    return pl.pallas_call(
        lambda *refs: finish_kernel(n_tensor, n_dp, count, *refs),
        out_shape=jax.ShapeDtypeStruct((8, 128), jnp.float32),
        in_specs=[pl.BlockSpec(memory_space=pltpu.VMEM)] * 4,
        out_specs=pl.BlockSpec(memory_space=pltpu.VMEM),
        scratch_shapes=[
            pltpu.VMEM(blocks.shape, jnp.float32),
            pltpu.VMEM((n_tensor,) + tile, jnp.float32),
            pltpu.VMEM((n_dp,) + tile, jnp.float32),
            pltpu.VMEM(tile, jnp.float32),
            pltpu.VMEM(tile, jnp.float32),
            pltpu.SemaphoreType.DMA((n_tensor,)),
            pltpu.SemaphoreType.DMA((n_tensor,)),
            pltpu.SemaphoreType.DMA((n_tensor,)),
            pltpu.SemaphoreType.DMA((n_tensor,)),
            pltpu.SemaphoreType.DMA((n_dp,)),
            pltpu.SemaphoreType.DMA((n_dp,)),
        ],
        compiler_params=pltpu.CompilerParams(collective_id=3, has_side_effects=True),
    )(blocks, spans, ids, spread)


def prep_kernel(hidden_ref, gain_ref, mask_ref, ids_ref, out_ref):
    width = hidden_ref.shape[1]
    own_rows = hidden_ref.shape[0]
    widened = hidden_ref[...].astype(jnp.float32)
    inverse_rms = lax.rsqrt(jnp.mean(widened * widened, axis=1, keepdims=True) + EPSILON)
    normed = (widened * inverse_rms * gain_ref[...]).astype(jnp.bfloat16)
    live = jnp.broadcast_to(mask_ref[...].astype(jnp.float32), (8, own_rows))
    upper = (
        lax.broadcasted_iota(jnp.int32, (own_rows, own_rows), 0)
        <= lax.broadcasted_iota(jnp.int32, (own_rows, own_rows), 1)
    ).astype(jnp.float32)
    live_sum = jnp.dot(live, upper, preferred_element_type=jnp.float32)[0:1, :]
    rank = lax.broadcasted_iota(jnp.int32, (LIVE, own_rows), 0).astype(jnp.float32)
    chosen = ((live[0:1, :] == 1.0) & (live_sum - 1.0 == rank)).astype(jnp.bfloat16)
    out_ref[:, :width] = jnp.dot(chosen, normed, preferred_element_type=jnp.float32).astype(jnp.bfloat16)
    ids = ids_ref[...]
    high = lax.shift_right_logical(ids, 8).astype(jnp.float32)
    low = jnp.bitwise_and(ids, 255).astype(jnp.float32)
    row = lax.broadcasted_iota(jnp.int32, (128, own_rows), 0)
    meta_in = jnp.where(row == 0, high, jnp.where(row == 1, low, 0.0)).astype(jnp.bfloat16)
    meta = lax.dot_general(
        chosen, meta_in, (((1,), (1,)), ((), ())), preferred_element_type=jnp.float32
    )
    out_ref[:, width:] = meta.astype(jnp.bfloat16)


def prep(hidden, norm_gain, slot_mask, token_ids):
    own_rows, width = hidden.shape
    return pl.pallas_call(
        prep_kernel,
        out_shape=jax.ShapeDtypeStruct((LIVE, width + 128), jnp.bfloat16),
        in_specs=[pl.BlockSpec(memory_space=pltpu.VMEM)] * 4,
        out_specs=pl.BlockSpec(memory_space=pltpu.VMEM),
    )(hidden, norm_gain.reshape(1, width), slot_mask.reshape(1, own_rows), token_ids.reshape(1, own_rows))


def stats_kernel(x_ref, w_ref, out_ref):
    depth, vocab = w_ref.shape
    logits = jnp.dot(x_ref[:, :depth], w_ref[...], preferred_element_type=jnp.float32)
    meta = x_ref[:, depth:depth + 128].astype(jnp.float32)
    token = (meta[:, 0:1] * 256.0 + meta[:, 1:2]).astype(jnp.int32) - lax.axis_index("tensor") * vocab
    peak = jnp.max(logits, axis=1, keepdims=True)
    shifted = logits - peak
    weights = jnp.exp(shifted)
    mass = jnp.sum(weights, axis=1, keepdims=True)
    spread = jnp.sum(weights * shifted, axis=1, keepdims=True)
    column = lax.broadcasted_iota(jnp.int32, logits.shape, 1)
    target = jnp.sum(jnp.where(column == token, logits, 0.0), axis=1, keepdims=True)
    lane = lax.broadcasted_iota(jnp.int32, out_ref.shape, 1)
    out_ref[...] = jnp.where(
        lane == 0, peak, jnp.where(lane == 1, mass, jnp.where(lane == 2, spread, target))
    )


def row_stats(rows, weight, tile):
    count = rows.shape[0]
    depth, vocab = weight.shape
    return pl.pallas_call(
        stats_kernel,
        out_shape=jax.ShapeDtypeStruct((count, 128), jnp.float32),
        grid=(count // tile,),
        in_specs=[
            pl.BlockSpec((tile, rows.shape[1]), lambda i: (i, 0)),
            pl.BlockSpec((depth, vocab), lambda i: (0, 0)),
        ],
        out_specs=pl.BlockSpec((tile, 128), lambda i: (i, 0)),
        compiler_params=pltpu.CompilerParams(vmem_limit_bytes=56 * 1024 * 1024),
        cost_estimate=pl.CostEstimate(
            flops=2 * count * depth * vocab,
            transcendentals=count * vocab,
            bytes_accessed=2 * count * rows.shape[1] + 2 * depth * vocab + 512 * count,
        ),
    )(rows, weight)


def on_device(
    hidden, norm_gain, head_weight, value_weight, token_ids, slot_mask, lengths, request_order
):
    own_rows = hidden.shape[0]
    vocab_local = head_weight.shape[1]
    n_tensor = lax.axis_size("tensor")
    n_dp = lax.axis_size("dp")
    tensor_index = lax.axis_index("tensor")
    widened = hidden.astype(jnp.float32)
    inverse_rms = lax.rsqrt(jnp.mean(widened * widened, axis=1, keepdims=True) + EPSILON)
    normed = (widened * inverse_rms * norm_gain).astype(jnp.bfloat16)
    weight_mask = slot_mask.astype(jnp.float32)
    token_value = weight_mask * jnp.dot(normed, value_weight, preferred_element_type=jnp.float32)

    width = hidden.shape[1]
    live_sum = jnp.cumsum(slot_mask)
    slot_index = jnp.arange(own_rows, dtype=jnp.int32)
    chosen = (slot_mask[None, :] == 1) & (
        live_sum[None, :] - 1 == jnp.arange(LIVE, dtype=jnp.int32)[:, None]
    )
    source = jnp.sum(jnp.where(chosen, slot_index[None, :], 0), axis=1)
    block = prep(hidden, norm_gain, slot_mask, token_ids)
    gathered = lax.all_gather(block, "tensor", axis=0, tiled=True)
    row_count = gathered.shape[0]
    stats = row_stats(gathered, head_weight, 256 if row_count % 256 == 0 else row_count)
    blocks = stats[:, :4].reshape(n_tensor, LIVE, 4).transpose(0, 2, 1)
    request_count = lengths.shape[1]
    span_lengths = lengths[0]
    span_ends = jnp.cumsum(span_lengths)
    slot_ids = tensor_index * own_rows + source
    position = jnp.sum((slot_ids[:, None] >= span_ends[None, :]).astype(jnp.int32), axis=1)
    live = jnp.arange(LIVE, dtype=jnp.int32) < live_sum[-1]
    member = (position[None, :] == jnp.arange(8, dtype=jnp.int32)[:, None]) & live[None, :]
    spans = (
        jnp.zeros((8, 128), jnp.float32)
        .at[:, :LIVE].set(member.astype(jnp.float32))
        .at[:, 127].set(jnp.ones((8,), jnp.float32).at[:request_count].set(span_lengths.astype(jnp.float32)))
    )
    ids_tile = jnp.zeros((8, 128), jnp.float32).at[:request_count, 1].set(request_order.astype(jnp.float32))
    place = live_sum - 1
    spread = ((place[:, None] == jnp.arange(LIVE, dtype=jnp.int32)[None, :]) & (slot_mask[:, None] == 1))
    result = finish(blocks, spans, ids_tile, spread.astype(jnp.float32), n_tensor, n_dp, request_count)
    token_logprob = result[0, :own_rows]
    token_entropy = result[1, :own_rows]
    request_score = result[2, :request_count]
    return (token_logprob, token_entropy, token_value, request_score)


def solution(mesh):
    return jax.shard_map(
        on_device,
        mesh=mesh,
        in_specs=(
            P(("dp", "tensor"), None),
            P(),
            P(None, "tensor"),
            P(),
            P(("dp", "tensor")),
            P(("dp", "tensor")),
            P("dp", None),
            P("dp"),
        ),
        out_specs=(P(("dp", "tensor")), P(("dp", "tensor")), P(("dp", "tensor")), P("dp")),
        check_vma=False,
    )
```

```python
import jax
import jax.numpy as jnp
from jax import lax
from jax.experimental import pallas as pl
from jax.experimental.pallas import tpu as pltpu
from jax.sharding import PartitionSpec as P

EPSILON = 1e-06
MESH = pl.DeviceIdType.MESH
LIVE = 48


def finish_kernel(n_tensor, n_dp, count, send_ref, span_ref, ids_ref, spread_ref, result_ref,
                  held, t_held, d_held, part_msg, route_msg,
                  a_send, a_recv, t_send, t_recv, d_send, d_recv):
    me = lax.axis_index("tensor")
    dp = lax.axis_index("dp")
    barrier = pltpu.get_barrier_semaphore()
    for offset in range(1, n_tensor):
        peer = lax.rem(me + offset, n_tensor)
        pl.semaphore_signal(barrier, inc=1, device_id=(dp, peer), device_id_type=MESH)
    for offset in range(1, n_dp):
        peer = lax.rem(dp + offset, n_dp)
        pl.semaphore_signal(barrier, inc=1, device_id=(peer, me), device_id_type=MESH)
    pl.semaphore_wait(barrier, n_tensor - 1 + n_dp - 1)

    held[me] = send_ref[me]
    copies = []
    for offset in range(1, n_tensor):
        peer = lax.rem(me + offset, n_tensor)
        copy = pltpu.make_async_remote_copy(
            src_ref=send_ref.at[peer], dst_ref=held.at[me],
            send_sem=a_send.at[offset], recv_sem=a_recv.at[offset],
            device_id=(dp, peer), device_id_type=MESH,
        )
        copy.start()
        copies.append(copy)
    for copy in copies:
        copy.wait_send()
    for offset in range(1, n_tensor):
        source = lax.rem(me + n_tensor - offset, n_tensor)
        pltpu.make_async_remote_copy(
            src_ref=send_ref.at[source], dst_ref=held.at[source],
            send_sem=a_send.at[offset], recv_sem=a_recv.at[offset],
            device_id=(dp, source), device_id_type=MESH,
        ).wait_recv()

    lanes = held.shape[2]
    peak = lax.fori_loop(
        0, n_tensor, lambda p, m: jnp.maximum(m, held[p][0:1, :]),
        jnp.full((1, lanes), -jnp.inf, jnp.float32),
    )

    def gather_sums(p, sums):
        mass, spread, target = sums
        block = held[p]
        gap = block[0:1, :] - peak
        factor = jnp.exp(gap)
        mass = mass + factor * block[1:2, :]
        spread = spread + factor * (block[2:3, :] + gap * block[1:2, :])
        return mass, spread, target + block[3:4, :]

    zero = jnp.zeros((1, lanes), jnp.float32)
    mass, spread, target = lax.fori_loop(0, n_tensor, gather_sums, (zero, zero, zero))
    log_mass = jnp.log(mass)
    logprob = target - peak - log_mass
    entropy = log_mass - spread / mass
    slots = spread_ref.shape[0]
    placed = spread_ref[...] > 0.0
    same = (
        lax.broadcasted_iota(jnp.int32, (slots, slots), 0)
        == lax.broadcasted_iota(jnp.int32, (slots, slots), 1)
    )
    result_ref[...] = jnp.zeros(result_ref.shape, jnp.float32)
    for index, value in enumerate((logprob, entropy)):
        column = jnp.sum(jnp.where(placed, value, 0.0), axis=1, keepdims=True)
        result_ref[index:index + 1, :slots] = jnp.sum(jnp.where(same, column, 0.0), axis=0, keepdims=True)

    spans = span_ref[...]
    partial = jnp.sum(spans[:, :lanes] * logprob, axis=1, keepdims=True) / spans[:, 127:128]
    part_msg[...] = jnp.broadcast_to(partial, part_msg.shape)
    t_held[me] = part_msg[...]
    copies = []
    for offset in range(1, n_tensor):
        peer = lax.rem(me + offset, n_tensor)
        copy = pltpu.make_async_remote_copy(
            src_ref=part_msg, dst_ref=t_held.at[me],
            send_sem=t_send.at[offset], recv_sem=t_recv.at[offset],
            device_id=(dp, peer), device_id_type=MESH,
        )
        copy.start()
        copies.append(copy)
    for copy in copies:
        copy.wait_send()
    for offset in range(1, n_tensor):
        source = lax.rem(me + n_tensor - offset, n_tensor)
        pltpu.make_async_remote_copy(
            src_ref=part_msg, dst_ref=t_held.at[source],
            send_sem=t_send.at[offset], recv_sem=t_recv.at[offset],
            device_id=(dp, source), device_id_type=MESH,
        ).wait_recv()

    total = jnp.sum(t_held[...], axis=0)
    lane = lax.broadcasted_iota(jnp.int32, total.shape, 1)
    route_msg[...] = jnp.where(lane == 0, total, jnp.where(lane == 1, ids_ref[...], 0.0))
    d_held[dp] = route_msg[...]
    copies = []
    for offset in range(1, n_dp):
        peer = lax.rem(dp + offset, n_dp)
        copy = pltpu.make_async_remote_copy(
            src_ref=route_msg, dst_ref=d_held.at[dp],
            send_sem=d_send.at[offset], recv_sem=d_recv.at[offset],
            device_id=(peer, me), device_id_type=MESH,
        )
        copy.start()
        copies.append(copy)
    for copy in copies:
        copy.wait_send()
    for offset in range(1, n_dp):
        source = lax.rem(dp + n_dp - offset, n_dp)
        pltpu.make_async_remote_copy(
            src_ref=route_msg, dst_ref=d_held.at[source],
            send_sem=d_send.at[offset], recv_sem=d_recv.at[offset],
            device_id=(source, me), device_id_type=MESH,
        ).wait_recv()
    wanted = (dp * count + lax.broadcasted_iota(jnp.int32, (1, count), 1)).astype(jnp.float32)
    score = jnp.zeros((1, count), jnp.float32)
    for group in range(n_dp):
        block = d_held[group]
        hit = block[:count, 1:2] == wanted
        score = score + jnp.sum(jnp.where(hit, block[:count, 0:1], 0.0), axis=0, keepdims=True)
    result_ref[2:3, :count] = score


def finish(blocks, spans, ids, spread, n_tensor, n_dp, count):
    tile = spans.shape
    lanes = blocks.shape[2]
    return pl.pallas_call(
        lambda *refs: finish_kernel(n_tensor, n_dp, count, *refs),
        out_shape=jax.ShapeDtypeStruct((8, 128), jnp.float32),
        in_specs=[pl.BlockSpec(memory_space=pltpu.VMEM)] * 4,
        out_specs=pl.BlockSpec(memory_space=pltpu.VMEM),
        scratch_shapes=[
            pltpu.VMEM(blocks.shape, jnp.float32),
            pltpu.VMEM((n_tensor,) + tile, jnp.float32),
            pltpu.VMEM((n_dp,) + tile, jnp.float32),
            pltpu.VMEM(tile, jnp.float32),
            pltpu.VMEM(tile, jnp.float32),
            pltpu.SemaphoreType.DMA((n_tensor,)),
            pltpu.SemaphoreType.DMA((n_tensor,)),
            pltpu.SemaphoreType.DMA((n_tensor,)),
            pltpu.SemaphoreType.DMA((n_tensor,)),
            pltpu.SemaphoreType.DMA((n_dp,)),
            pltpu.SemaphoreType.DMA((n_dp,)),
        ],
        compiler_params=pltpu.CompilerParams(collective_id=3, has_side_effects=True),
    )(blocks, spans, ids, spread)


def prep_kernel(hidden_ref, gain_ref, mask_ref, ids_ref, out_ref):
    width = hidden_ref.shape[1]
    own_rows = hidden_ref.shape[0]
    widened = hidden_ref[...].astype(jnp.float32)
    inverse_rms = lax.rsqrt(jnp.mean(widened * widened, axis=1, keepdims=True) + EPSILON)
    normed = (widened * inverse_rms * gain_ref[...]).astype(jnp.bfloat16)
    live = jnp.broadcast_to(mask_ref[...].astype(jnp.float32), (8, own_rows))
    upper = (
        lax.broadcasted_iota(jnp.int32, (own_rows, own_rows), 0)
        <= lax.broadcasted_iota(jnp.int32, (own_rows, own_rows), 1)
    ).astype(jnp.float32)
    live_sum = jnp.dot(live, upper, preferred_element_type=jnp.float32)[0:1, :]
    rank = lax.broadcasted_iota(jnp.int32, (LIVE, own_rows), 0).astype(jnp.float32)
    chosen = ((live[0:1, :] == 1.0) & (live_sum - 1.0 == rank)).astype(jnp.bfloat16)
    out_ref[:, :width] = jnp.dot(chosen, normed, preferred_element_type=jnp.float32).astype(jnp.bfloat16)
    ids = ids_ref[...]
    high = lax.shift_right_logical(ids, 8).astype(jnp.float32)
    low = jnp.bitwise_and(ids, 255).astype(jnp.float32)
    row = lax.broadcasted_iota(jnp.int32, (128, own_rows), 0)
    meta_in = jnp.where(row == 0, high, jnp.where(row == 1, low, 0.0)).astype(jnp.bfloat16)
    meta = lax.dot_general(
        chosen, meta_in, (((1,), (1,)), ((), ())), preferred_element_type=jnp.float32
    )
    out_ref[:, width:] = meta.astype(jnp.bfloat16)


def prep(hidden, norm_gain, slot_mask, token_ids):
    own_rows, width = hidden.shape
    return pl.pallas_call(
        prep_kernel,
        out_shape=jax.ShapeDtypeStruct((LIVE, width + 128), jnp.bfloat16),
        in_specs=[pl.BlockSpec(memory_space=pltpu.VMEM)] * 4,
        out_specs=pl.BlockSpec(memory_space=pltpu.VMEM),
    )(hidden, norm_gain.reshape(1, width), slot_mask.reshape(1, own_rows), token_ids.reshape(1, own_rows))


def stats_kernel(x_ref, wt_ref, out_ref):
    vocab, depth = wt_ref.shape
    contract_last = (((1,), (1,)), ((), ()))
    logits = lax.dot_general(wt_ref[...], x_ref[:, :depth], contract_last, preferred_element_type=jnp.float32)
    pick = (
        lax.broadcasted_iota(jnp.int32, (8, 128), 0) == lax.broadcasted_iota(jnp.int32, (8, 128), 1)
    ).astype(jnp.bfloat16)
    meta = lax.dot_general(pick, x_ref[:, depth:depth + 128], contract_last, preferred_element_type=jnp.float32)
    token = (meta[0:1, :] * 256.0 + meta[1:2, :]).astype(jnp.int32) - lax.axis_index("tensor") * vocab
    peak = jnp.max(logits, axis=0, keepdims=True)
    shifted = logits - peak
    weights = jnp.exp(shifted)
    mass = jnp.sum(weights, axis=0, keepdims=True)
    spread = jnp.sum(weights * shifted, axis=0, keepdims=True)
    entry = lax.broadcasted_iota(jnp.int32, logits.shape, 0)
    target = jnp.sum(jnp.where(entry == token, logits, 0.0), axis=0, keepdims=True)
    row = lax.broadcasted_iota(jnp.int32, out_ref.shape, 0)
    out_ref[...] = jnp.where(
        row == 0, peak,
        jnp.where(row == 1, mass, jnp.where(row == 2, spread, jnp.where(row == 3, target, 0.0))),
    )


def row_stats(rows, weight_t, tile):
    count = rows.shape[0]
    vocab, depth = weight_t.shape
    return pl.pallas_call(
        stats_kernel,
        out_shape=jax.ShapeDtypeStruct((8, count), jnp.float32),
        grid=(count // tile,),
        in_specs=[
            pl.BlockSpec((tile, rows.shape[1]), lambda i: (i, 0)),
            pl.BlockSpec((vocab, depth), lambda i: (0, 0)),
        ],
        out_specs=pl.BlockSpec((8, tile), lambda i: (0, i)),
        compiler_params=pltpu.CompilerParams(vmem_limit_bytes=56 * 1024 * 1024),
        cost_estimate=pl.CostEstimate(
            flops=2 * count * depth * vocab,
            transcendentals=count * vocab,
            bytes_accessed=2 * count * rows.shape[1] + 2 * depth * vocab + 32 * count,
        ),
    )(rows, weight_t)


def on_device(
    hidden, norm_gain, head_weight, value_weight, token_ids, slot_mask, lengths, request_order
):
    own_rows = hidden.shape[0]
    vocab_local = head_weight.shape[1]
    n_tensor = lax.axis_size("tensor")
    n_dp = lax.axis_size("dp")
    tensor_index = lax.axis_index("tensor")
    widened = hidden.astype(jnp.float32)
    inverse_rms = lax.rsqrt(jnp.mean(widened * widened, axis=1, keepdims=True) + EPSILON)
    normed = (widened * inverse_rms * norm_gain).astype(jnp.bfloat16)
    weight_mask = slot_mask.astype(jnp.float32)
    token_value = weight_mask * jnp.dot(normed, value_weight, preferred_element_type=jnp.float32)

    width = hidden.shape[1]
    live_sum = jnp.cumsum(slot_mask)
    slot_index = jnp.arange(own_rows, dtype=jnp.int32)
    chosen = (slot_mask[None, :] == 1) & (
        live_sum[None, :] - 1 == jnp.arange(LIVE, dtype=jnp.int32)[:, None]
    )
    source = jnp.sum(jnp.where(chosen, slot_index[None, :], 0), axis=1)
    block = prep(hidden, norm_gain, slot_mask, token_ids)
    gathered = lax.all_gather(block, "tensor", axis=0, tiled=True)
    row_count = gathered.shape[0]
    stats = row_stats(gathered, head_weight.T, 256 if row_count % 256 == 0 else row_count)
    blocks = stats[:4].reshape(4, n_tensor, LIVE).transpose(1, 0, 2)
    request_count = lengths.shape[1]
    span_lengths = lengths[0]
    span_ends = jnp.cumsum(span_lengths)
    slot_ids = tensor_index * own_rows + source
    position = jnp.sum((slot_ids[:, None] >= span_ends[None, :]).astype(jnp.int32), axis=1)
    live = jnp.arange(LIVE, dtype=jnp.int32) < live_sum[-1]
    member = (position[None, :] == jnp.arange(8, dtype=jnp.int32)[:, None]) & live[None, :]
    spans = (
        jnp.zeros((8, 128), jnp.float32)
        .at[:, :LIVE].set(member.astype(jnp.float32))
        .at[:, 127].set(jnp.ones((8,), jnp.float32).at[:request_count].set(span_lengths.astype(jnp.float32)))
    )
    ids_tile = jnp.zeros((8, 128), jnp.float32).at[:request_count, 1].set(request_order.astype(jnp.float32))
    place = live_sum - 1
    spread = ((place[:, None] == jnp.arange(LIVE, dtype=jnp.int32)[None, :]) & (slot_mask[:, None] == 1))
    result = finish(blocks, spans, ids_tile, spread.astype(jnp.float32), n_tensor, n_dp, request_count)
    token_logprob = result[0, :own_rows]
    token_entropy = result[1, :own_rows]
    request_score = result[2, :request_count]
    return (token_logprob, token_entropy, token_value, request_score)


def solution(mesh):
    return jax.shard_map(
        on_device,
        mesh=mesh,
        in_specs=(
            P(("dp", "tensor"), None),
            P(),
            P(None, "tensor"),
            P(),
            P(("dp", "tensor")),
            P(("dp", "tensor")),
            P("dp", None),
            P("dp"),
        ),
        out_specs=(P(("dp", "tensor")), P(("dp", "tensor")), P(("dp", "tensor")), P("dp")),
        check_vma=False,
    )
```

```python
import jax
import jax.numpy as jnp
from jax import lax
from jax.experimental import pallas as pl
from jax.experimental.pallas import tpu as pltpu
from jax.sharding import PartitionSpec as P

EPSILON = 1e-06
MESH = pl.DeviceIdType.MESH
LIVE = 48


def finish_kernel(n_tensor, n_dp, count, send_ref, span_ref, ids_ref, spread_ref, result_ref,
                  held, t_held, d_held, part_msg, route_msg,
                  a_send, a_recv, t_send, t_recv, d_send, d_recv):
    me = lax.axis_index("tensor")
    dp = lax.axis_index("dp")
    barrier = pltpu.get_barrier_semaphore()
    for offset in range(1, n_tensor):
        peer = lax.rem(me + offset, n_tensor)
        pl.semaphore_signal(barrier, inc=1, device_id=(dp, peer), device_id_type=MESH)
    for offset in range(1, n_dp):
        peer = lax.rem(dp + offset, n_dp)
        pl.semaphore_signal(barrier, inc=1, device_id=(peer, me), device_id_type=MESH)
    pl.semaphore_wait(barrier, n_tensor - 1 + n_dp - 1)

    held[me] = send_ref[me]
    copies = []
    for offset in range(1, n_tensor):
        peer = lax.rem(me + offset, n_tensor)
        copy = pltpu.make_async_remote_copy(
            src_ref=send_ref.at[peer], dst_ref=held.at[me],
            send_sem=a_send.at[offset], recv_sem=a_recv.at[offset],
            device_id=(dp, peer), device_id_type=MESH,
        )
        copy.start()
        copies.append(copy)
    for copy in copies:
        copy.wait_send()
    for offset in range(1, n_tensor):
        source = lax.rem(me + n_tensor - offset, n_tensor)
        pltpu.make_async_remote_copy(
            src_ref=send_ref.at[source], dst_ref=held.at[source],
            send_sem=a_send.at[offset], recv_sem=a_recv.at[offset],
            device_id=(dp, source), device_id_type=MESH,
        ).wait_recv()

    lanes = held.shape[2]
    peak = lax.fori_loop(
        0, n_tensor, lambda p, m: jnp.maximum(m, held[p][0:1, :]),
        jnp.full((1, lanes), -jnp.inf, jnp.float32),
    )

    def gather_sums(p, sums):
        mass, spread, target = sums
        block = held[p]
        gap = block[0:1, :] - peak
        factor = jnp.exp(gap)
        mass = mass + factor * block[1:2, :]
        spread = spread + factor * (block[2:3, :] + gap * block[1:2, :])
        return mass, spread, target + block[3:4, :]

    zero = jnp.zeros((1, lanes), jnp.float32)
    mass, spread, target = lax.fori_loop(0, n_tensor, gather_sums, (zero, zero, zero))
    log_mass = jnp.log(mass)
    logprob = target - peak - log_mass
    entropy = log_mass - spread / mass
    slots = spread_ref.shape[0]
    placed = spread_ref[...] > 0.0
    same = (
        lax.broadcasted_iota(jnp.int32, (slots, slots), 0)
        == lax.broadcasted_iota(jnp.int32, (slots, slots), 1)
    )
    result_ref[...] = jnp.zeros(result_ref.shape, jnp.float32)
    for index, value in enumerate((logprob, entropy)):
        column = jnp.sum(jnp.where(placed, value, 0.0), axis=1, keepdims=True)
        result_ref[index:index + 1, :slots] = jnp.sum(jnp.where(same, column, 0.0), axis=0, keepdims=True)

    spans = span_ref[...]
    partial = jnp.sum(spans[:, :lanes] * logprob, axis=1, keepdims=True) / spans[:, 127:128]
    part_msg[...] = jnp.broadcast_to(partial, part_msg.shape)
    t_held[me] = part_msg[...]
    copies = []
    for offset in range(1, n_tensor):
        peer = lax.rem(me + offset, n_tensor)
        copy = pltpu.make_async_remote_copy(
            src_ref=part_msg, dst_ref=t_held.at[me],
            send_sem=t_send.at[offset], recv_sem=t_recv.at[offset],
            device_id=(dp, peer), device_id_type=MESH,
        )
        copy.start()
        copies.append(copy)
    for copy in copies:
        copy.wait_send()
    for offset in range(1, n_tensor):
        source = lax.rem(me + n_tensor - offset, n_tensor)
        pltpu.make_async_remote_copy(
            src_ref=part_msg, dst_ref=t_held.at[source],
            send_sem=t_send.at[offset], recv_sem=t_recv.at[offset],
            device_id=(dp, source), device_id_type=MESH,
        ).wait_recv()

    total = jnp.sum(t_held[...], axis=0)
    lane = lax.broadcasted_iota(jnp.int32, total.shape, 1)
    route_msg[...] = jnp.where(lane == 0, total, jnp.where(lane == 1, ids_ref[...], 0.0))
    d_held[dp] = route_msg[...]
    copies = []
    for offset in range(1, n_dp):
        peer = lax.rem(dp + offset, n_dp)
        copy = pltpu.make_async_remote_copy(
            src_ref=route_msg, dst_ref=d_held.at[dp],
            send_sem=d_send.at[offset], recv_sem=d_recv.at[offset],
            device_id=(peer, me), device_id_type=MESH,
        )
        copy.start()
        copies.append(copy)
    for copy in copies:
        copy.wait_send()
    for offset in range(1, n_dp):
        source = lax.rem(dp + n_dp - offset, n_dp)
        pltpu.make_async_remote_copy(
            src_ref=route_msg, dst_ref=d_held.at[source],
            send_sem=d_send.at[offset], recv_sem=d_recv.at[offset],
            device_id=(source, me), device_id_type=MESH,
        ).wait_recv()
    wanted = (dp * count + lax.broadcasted_iota(jnp.int32, (1, count), 1)).astype(jnp.float32)
    score = jnp.zeros((1, count), jnp.float32)
    for group in range(n_dp):
        block = d_held[group]
        hit = block[:count, 1:2] == wanted
        score = score + jnp.sum(jnp.where(hit, block[:count, 0:1], 0.0), axis=0, keepdims=True)
    result_ref[2:3, :count] = score


def finish(blocks, spans, ids, spread, n_tensor, n_dp, count):
    tile = spans.shape
    lanes = blocks.shape[2]
    return pl.pallas_call(
        lambda *refs: finish_kernel(n_tensor, n_dp, count, *refs),
        out_shape=jax.ShapeDtypeStruct((8, 128), jnp.float32),
        in_specs=[pl.BlockSpec(memory_space=pltpu.VMEM)] * 4,
        out_specs=pl.BlockSpec(memory_space=pltpu.VMEM),
        scratch_shapes=[
            pltpu.VMEM(blocks.shape, jnp.float32),
            pltpu.VMEM((n_tensor,) + tile, jnp.float32),
            pltpu.VMEM((n_dp,) + tile, jnp.float32),
            pltpu.VMEM(tile, jnp.float32),
            pltpu.VMEM(tile, jnp.float32),
            pltpu.SemaphoreType.DMA((n_tensor,)),
            pltpu.SemaphoreType.DMA((n_tensor,)),
            pltpu.SemaphoreType.DMA((n_tensor,)),
            pltpu.SemaphoreType.DMA((n_tensor,)),
            pltpu.SemaphoreType.DMA((n_dp,)),
            pltpu.SemaphoreType.DMA((n_dp,)),
        ],
        compiler_params=pltpu.CompilerParams(collective_id=3, has_side_effects=True),
    )(blocks, spans, ids, spread)


def prep_kernel(hidden_ref, gain_ref, mask_ref, ids_ref, out_ref):
    width = hidden_ref.shape[1]
    own_rows = hidden_ref.shape[0]
    widened = hidden_ref[...].astype(jnp.float32)
    inverse_rms = lax.rsqrt(jnp.mean(widened * widened, axis=1, keepdims=True) + EPSILON)
    normed = (widened * inverse_rms * gain_ref[...]).astype(jnp.bfloat16)
    live = jnp.broadcast_to(mask_ref[...].astype(jnp.float32), (8, own_rows))
    upper = (
        lax.broadcasted_iota(jnp.int32, (own_rows, own_rows), 0)
        <= lax.broadcasted_iota(jnp.int32, (own_rows, own_rows), 1)
    ).astype(jnp.float32)
    live_sum = jnp.dot(live, upper, preferred_element_type=jnp.float32)[0:1, :]
    rank = lax.broadcasted_iota(jnp.int32, (LIVE, own_rows), 0).astype(jnp.float32)
    chosen = ((live[0:1, :] == 1.0) & (live_sum - 1.0 == rank)).astype(jnp.bfloat16)
    out_ref[:, :width] = jnp.dot(chosen, normed, preferred_element_type=jnp.float32).astype(jnp.bfloat16)
    ids = ids_ref[...]
    high = lax.shift_right_logical(ids, 8).astype(jnp.float32)
    low = jnp.bitwise_and(ids, 255).astype(jnp.float32)
    row = lax.broadcasted_iota(jnp.int32, (128, own_rows), 0)
    meta_in = jnp.where(row == 0, high, jnp.where(row == 1, low, 0.0)).astype(jnp.bfloat16)
    meta = lax.dot_general(
        chosen, meta_in, (((1,), (1,)), ((), ())), preferred_element_type=jnp.float32
    )
    out_ref[:, width:] = meta.astype(jnp.bfloat16)


def prep(hidden, norm_gain, slot_mask, token_ids):
    own_rows, width = hidden.shape
    return pl.pallas_call(
        prep_kernel,
        out_shape=jax.ShapeDtypeStruct((LIVE, width + 128), jnp.bfloat16),
        in_specs=[pl.BlockSpec(memory_space=pltpu.VMEM)] * 4,
        out_specs=pl.BlockSpec(memory_space=pltpu.VMEM),
    )(hidden, norm_gain.reshape(1, width), slot_mask.reshape(1, own_rows), token_ids.reshape(1, own_rows))


def stats_kernel(x_ref, wt_ref, out_ref):
    vocab, depth = wt_ref.shape
    contract_last = (((1,), (1,)), ((), ()))
    logits = lax.dot_general(wt_ref[...], x_ref[:, :depth], contract_last, preferred_element_type=jnp.float32)
    pick = (
        lax.broadcasted_iota(jnp.int32, (8, 128), 0) == lax.broadcasted_iota(jnp.int32, (8, 128), 1)
    ).astype(jnp.bfloat16)
    meta = lax.dot_general(pick, x_ref[:, depth:depth + 128], contract_last, preferred_element_type=jnp.float32)
    token = (meta[0:1, :] * 256.0 + meta[1:2, :]).astype(jnp.int32) - lax.axis_index("tensor") * vocab
    peak = jnp.max(logits, axis=0, keepdims=True)
    shifted = logits - peak
    weights = jnp.exp(shifted)
    mass = jnp.sum(weights, axis=0, keepdims=True)
    spread = jnp.sum(weights * shifted, axis=0, keepdims=True)
    entry = lax.broadcasted_iota(jnp.int32, logits.shape, 0)
    target = jnp.sum(jnp.where(entry == token, logits, 0.0), axis=0, keepdims=True)
    row = lax.broadcasted_iota(jnp.int32, out_ref.shape, 0)
    out_ref[...] = jnp.where(
        row == 0, peak,
        jnp.where(row == 1, mass, jnp.where(row == 2, spread, jnp.where(row == 3, target, 0.0))),
    )


def row_stats(rows, weight_t, tile):
    count = rows.shape[0]
    vocab, depth = weight_t.shape
    return pl.pallas_call(
        stats_kernel,
        out_shape=jax.ShapeDtypeStruct((8, count), jnp.float32),
        grid=(count // tile,),
        in_specs=[
            pl.BlockSpec((tile, rows.shape[1]), lambda i: (i, 0)),
            pl.BlockSpec((vocab, depth), lambda i: (0, 0)),
        ],
        out_specs=pl.BlockSpec((8, tile), lambda i: (0, i)),
        compiler_params=pltpu.CompilerParams(vmem_limit_bytes=56 * 1024 * 1024),
        cost_estimate=pl.CostEstimate(
            flops=2 * count * depth * vocab,
            transcendentals=count * vocab,
            bytes_accessed=2 * count * rows.shape[1] + 2 * depth * vocab + 32 * count,
        ),
    )(rows, weight_t)


def on_device(
    hidden, norm_gain, head_weight, value_weight, token_ids, slot_mask, lengths, request_order
):
    own_rows = hidden.shape[0]
    vocab_local = head_weight.shape[1]
    n_tensor = lax.axis_size("tensor")
    n_dp = lax.axis_size("dp")
    tensor_index = lax.axis_index("tensor")
    widened = hidden.astype(jnp.float32)
    inverse_rms = lax.rsqrt(jnp.mean(widened * widened, axis=1, keepdims=True) + EPSILON)
    normed = (widened * inverse_rms * norm_gain).astype(jnp.bfloat16)
    weight_mask = slot_mask.astype(jnp.float32)
    token_value = weight_mask * jnp.dot(normed, value_weight, preferred_element_type=jnp.float32)

    width = hidden.shape[1]
    live_sum = jnp.cumsum(slot_mask)
    slot_index = jnp.arange(own_rows, dtype=jnp.int32)
    chosen = (slot_mask[None, :] == 1) & (
        live_sum[None, :] - 1 == jnp.arange(LIVE, dtype=jnp.int32)[:, None]
    )
    source = jnp.sum(jnp.where(chosen, slot_index[None, :], 0), axis=1)
    block = prep(hidden, norm_gain, slot_mask, token_ids)
    gathered = lax.all_gather(block, "tensor", axis=0, tiled=True)
    row_count = gathered.shape[0]
    stats = row_stats(gathered, head_weight.T, 512 if row_count % 512 == 0 else row_count)
    blocks = stats[:4].reshape(4, n_tensor, LIVE).transpose(1, 0, 2)
    request_count = lengths.shape[1]
    span_lengths = lengths[0]
    span_ends = jnp.cumsum(span_lengths)
    slot_ids = tensor_index * own_rows + source
    position = jnp.sum((slot_ids[:, None] >= span_ends[None, :]).astype(jnp.int32), axis=1)
    live = jnp.arange(LIVE, dtype=jnp.int32) < live_sum[-1]
    member = (position[None, :] == jnp.arange(8, dtype=jnp.int32)[:, None]) & live[None, :]
    spans = (
        jnp.zeros((8, 128), jnp.float32)
        .at[:, :LIVE].set(member.astype(jnp.float32))
        .at[:, 127].set(jnp.ones((8,), jnp.float32).at[:request_count].set(span_lengths.astype(jnp.float32)))
    )
    ids_tile = jnp.zeros((8, 128), jnp.float32).at[:request_count, 1].set(request_order.astype(jnp.float32))
    place = live_sum - 1
    spread = ((place[:, None] == jnp.arange(LIVE, dtype=jnp.int32)[None, :]) & (slot_mask[:, None] == 1))
    result = finish(blocks, spans, ids_tile, spread.astype(jnp.float32), n_tensor, n_dp, request_count)
    token_logprob = result[0, :own_rows]
    token_entropy = result[1, :own_rows]
    request_score = result[2, :request_count]
    return (token_logprob, token_entropy, token_value, request_score)


def solution(mesh):
    return jax.shard_map(
        on_device,
        mesh=mesh,
        in_specs=(
            P(("dp", "tensor"), None),
            P(),
            P(None, "tensor"),
            P(),
            P(("dp", "tensor")),
            P(("dp", "tensor")),
            P("dp", None),
            P("dp"),
        ),
        out_specs=(P(("dp", "tensor")), P(("dp", "tensor")), P(("dp", "tensor")), P("dp")),
        check_vma=False,
    )
```

```python
import jax
import jax.numpy as jnp
from jax import lax
from jax.experimental import pallas as pl
from jax.experimental.pallas import tpu as pltpu
from jax.sharding import PartitionSpec as P

EPSILON = 1e-06
MESH = pl.DeviceIdType.MESH
LIVE = 48


def finish_kernel(n_tensor, n_dp, count, send_ref, span_ref, ids_ref, spread_ref, result_ref,
                  held, t_held, d_held, part_msg, route_msg,
                  a_send, a_recv, t_send, t_recv, d_send, d_recv):
    me = lax.axis_index("tensor")
    dp = lax.axis_index("dp")
    barrier = pltpu.get_barrier_semaphore()
    for offset in range(1, n_tensor):
        peer = lax.rem(me + offset, n_tensor)
        pl.semaphore_signal(barrier, inc=1, device_id=(dp, peer), device_id_type=MESH)
    for offset in range(1, n_dp):
        peer = lax.rem(dp + offset, n_dp)
        pl.semaphore_signal(barrier, inc=1, device_id=(peer, me), device_id_type=MESH)
    pl.semaphore_wait(barrier, n_tensor - 1 + n_dp - 1)

    held[me] = send_ref[me]
    copies = []
    for offset in range(1, n_tensor):
        peer = lax.rem(me + offset, n_tensor)
        copy = pltpu.make_async_remote_copy(
            src_ref=send_ref.at[peer], dst_ref=held.at[me],
            send_sem=a_send.at[offset], recv_sem=a_recv.at[offset],
            device_id=(dp, peer), device_id_type=MESH,
        )
        copy.start()
        copies.append(copy)
    for copy in copies:
        copy.wait_send()
    for offset in range(1, n_tensor):
        source = lax.rem(me + n_tensor - offset, n_tensor)
        pltpu.make_async_remote_copy(
            src_ref=send_ref.at[source], dst_ref=held.at[source],
            send_sem=a_send.at[offset], recv_sem=a_recv.at[offset],
            device_id=(dp, source), device_id_type=MESH,
        ).wait_recv()

    lanes = held.shape[2]
    peak = lax.fori_loop(
        0, n_tensor, lambda p, m: jnp.maximum(m, held[p][0:1, :]),
        jnp.full((1, lanes), -jnp.inf, jnp.float32),
    )

    def gather_sums(p, sums):
        mass, spread, target = sums
        block = held[p]
        gap = block[0:1, :] - peak
        factor = jnp.exp(gap)
        mass = mass + factor * block[1:2, :]
        spread = spread + factor * (block[2:3, :] + gap * block[1:2, :])
        return mass, spread, target + block[3:4, :]

    zero = jnp.zeros((1, lanes), jnp.float32)
    mass, spread, target = lax.fori_loop(0, n_tensor, gather_sums, (zero, zero, zero))
    log_mass = jnp.log(mass)
    logprob = target - peak - log_mass
    entropy = log_mass - spread / mass
    slots = spread_ref.shape[0]
    placed = spread_ref[...] > 0.0
    same = (
        lax.broadcasted_iota(jnp.int32, (slots, slots), 0)
        == lax.broadcasted_iota(jnp.int32, (slots, slots), 1)
    )
    result_ref[...] = jnp.zeros(result_ref.shape, jnp.float32)
    for index, value in enumerate((logprob, entropy)):
        column = jnp.sum(jnp.where(placed, value, 0.0), axis=1, keepdims=True)
        result_ref[index:index + 1, :slots] = jnp.sum(jnp.where(same, column, 0.0), axis=0, keepdims=True)

    spans = span_ref[...]
    partial = jnp.sum(spans[:, :lanes] * logprob, axis=1, keepdims=True) / spans[:, 127:128]
    part_msg[...] = jnp.broadcast_to(partial, part_msg.shape)
    t_held[me] = part_msg[...]
    copies = []
    for offset in range(1, n_tensor):
        peer = lax.rem(me + offset, n_tensor)
        copy = pltpu.make_async_remote_copy(
            src_ref=part_msg, dst_ref=t_held.at[me],
            send_sem=t_send.at[offset], recv_sem=t_recv.at[offset],
            device_id=(dp, peer), device_id_type=MESH,
        )
        copy.start()
        copies.append(copy)
    for copy in copies:
        copy.wait_send()
    for offset in range(1, n_tensor):
        source = lax.rem(me + n_tensor - offset, n_tensor)
        pltpu.make_async_remote_copy(
            src_ref=part_msg, dst_ref=t_held.at[source],
            send_sem=t_send.at[offset], recv_sem=t_recv.at[offset],
            device_id=(dp, source), device_id_type=MESH,
        ).wait_recv()

    total = jnp.sum(t_held[...], axis=0)
    lane = lax.broadcasted_iota(jnp.int32, total.shape, 1)
    route_msg[...] = jnp.where(lane == 0, total, jnp.where(lane == 1, ids_ref[...], 0.0))
    d_held[dp] = route_msg[...]
    copies = []
    for offset in range(1, n_dp):
        peer = lax.rem(dp + offset, n_dp)
        copy = pltpu.make_async_remote_copy(
            src_ref=route_msg, dst_ref=d_held.at[dp],
            send_sem=d_send.at[offset], recv_sem=d_recv.at[offset],
            device_id=(peer, me), device_id_type=MESH,
        )
        copy.start()
        copies.append(copy)
    for copy in copies:
        copy.wait_send()
    for offset in range(1, n_dp):
        source = lax.rem(dp + n_dp - offset, n_dp)
        pltpu.make_async_remote_copy(
            src_ref=route_msg, dst_ref=d_held.at[source],
            send_sem=d_send.at[offset], recv_sem=d_recv.at[offset],
            device_id=(source, me), device_id_type=MESH,
        ).wait_recv()
    wanted = (dp * count + lax.broadcasted_iota(jnp.int32, (1, count), 1)).astype(jnp.float32)
    score = jnp.zeros((1, count), jnp.float32)
    for group in range(n_dp):
        block = d_held[group]
        hit = block[:count, 1:2] == wanted
        score = score + jnp.sum(jnp.where(hit, block[:count, 0:1], 0.0), axis=0, keepdims=True)
    result_ref[2:3, :count] = score


def finish(blocks, spans, ids, spread, n_tensor, n_dp, count):
    tile = spans.shape
    lanes = blocks.shape[2]
    return pl.pallas_call(
        lambda *refs: finish_kernel(n_tensor, n_dp, count, *refs),
        out_shape=jax.ShapeDtypeStruct((8, 128), jnp.float32),
        in_specs=[pl.BlockSpec(memory_space=pltpu.VMEM)] * 4,
        out_specs=pl.BlockSpec(memory_space=pltpu.VMEM),
        scratch_shapes=[
            pltpu.VMEM(blocks.shape, jnp.float32),
            pltpu.VMEM((n_tensor,) + tile, jnp.float32),
            pltpu.VMEM((n_dp,) + tile, jnp.float32),
            pltpu.VMEM(tile, jnp.float32),
            pltpu.VMEM(tile, jnp.float32),
            pltpu.SemaphoreType.DMA((n_tensor,)),
            pltpu.SemaphoreType.DMA((n_tensor,)),
            pltpu.SemaphoreType.DMA((n_tensor,)),
            pltpu.SemaphoreType.DMA((n_tensor,)),
            pltpu.SemaphoreType.DMA((n_dp,)),
            pltpu.SemaphoreType.DMA((n_dp,)),
        ],
        compiler_params=pltpu.CompilerParams(collective_id=3, has_side_effects=True),
    )(blocks, spans, ids, spread)


def prep_kernel(hidden_ref, gain_ref, mask_ref, ids_ref, out_ref):
    width = hidden_ref.shape[1]
    own_rows = hidden_ref.shape[0]
    widened = hidden_ref[...].astype(jnp.float32)
    inverse_rms = lax.rsqrt(jnp.mean(widened * widened, axis=1, keepdims=True) + EPSILON)
    normed = (widened * inverse_rms * gain_ref[...]).astype(jnp.bfloat16)
    live = jnp.broadcast_to(mask_ref[...].astype(jnp.float32), (8, own_rows))
    upper = (
        lax.broadcasted_iota(jnp.int32, (own_rows, own_rows), 0)
        <= lax.broadcasted_iota(jnp.int32, (own_rows, own_rows), 1)
    ).astype(jnp.float32)
    live_sum = jnp.dot(live, upper, preferred_element_type=jnp.float32)[0:1, :]
    rank = lax.broadcasted_iota(jnp.int32, (LIVE, own_rows), 0).astype(jnp.float32)
    chosen = ((live[0:1, :] == 1.0) & (live_sum - 1.0 == rank)).astype(jnp.bfloat16)
    out_ref[:, :width] = jnp.dot(chosen, normed, preferred_element_type=jnp.float32).astype(jnp.bfloat16)
    ids = ids_ref[...]
    high = lax.shift_right_logical(ids, 8).astype(jnp.float32)
    low = jnp.bitwise_and(ids, 255).astype(jnp.float32)
    row = lax.broadcasted_iota(jnp.int32, (128, own_rows), 0)
    meta_in = jnp.where(row == 0, high, jnp.where(row == 1, low, 0.0)).astype(jnp.bfloat16)
    meta = lax.dot_general(
        chosen, meta_in, (((1,), (1,)), ((), ())), preferred_element_type=jnp.float32
    )
    out_ref[:, width:] = meta.astype(jnp.bfloat16)


def prep(hidden, norm_gain, slot_mask, token_ids):
    own_rows, width = hidden.shape
    return pl.pallas_call(
        prep_kernel,
        out_shape=jax.ShapeDtypeStruct((LIVE, width + 128), jnp.bfloat16),
        in_specs=[pl.BlockSpec(memory_space=pltpu.VMEM)] * 4,
        out_specs=pl.BlockSpec(memory_space=pltpu.VMEM),
    )(hidden, norm_gain.reshape(1, width), slot_mask.reshape(1, own_rows), token_ids.reshape(1, own_rows))


def stats_kernel(x_ref, wt_ref, out_ref):
    vocab, depth = wt_ref.shape
    contract_last = (((1,), (1,)), ((), ()))
    logits = lax.dot_general(wt_ref[...], x_ref[:, :depth], contract_last, preferred_element_type=jnp.float32)
    pick = (
        lax.broadcasted_iota(jnp.int32, (8, 128), 0) == lax.broadcasted_iota(jnp.int32, (8, 128), 1)
    ).astype(jnp.bfloat16)
    meta = lax.dot_general(pick, x_ref[:, depth:depth + 128], contract_last, preferred_element_type=jnp.float32)
    token = (meta[0:1, :] * 256.0 + meta[1:2, :]).astype(jnp.int32) - lax.axis_index("tensor") * vocab
    peak = jnp.max(logits, axis=0, keepdims=True)
    shifted = logits - peak
    weights = jnp.exp(shifted)
    ones = jnp.ones((8, vocab), jnp.float32)
    column_sum = lambda value: jnp.dot(
        ones, value, preferred_element_type=jnp.float32, precision=lax.Precision.HIGHEST
    )[0:1, :]
    mass = column_sum(weights)
    spread = column_sum(weights * shifted)
    entry = lax.broadcasted_iota(jnp.int32, logits.shape, 0)
    target = jnp.sum(jnp.where(entry == token, logits, 0.0), axis=0, keepdims=True)
    row = lax.broadcasted_iota(jnp.int32, out_ref.shape, 0)
    out_ref[...] = jnp.where(
        row == 0, peak,
        jnp.where(row == 1, mass, jnp.where(row == 2, spread, jnp.where(row == 3, target, 0.0))),
    )


def row_stats(rows, weight_t, tile):
    count = rows.shape[0]
    vocab, depth = weight_t.shape
    return pl.pallas_call(
        stats_kernel,
        out_shape=jax.ShapeDtypeStruct((8, count), jnp.float32),
        grid=(count // tile,),
        in_specs=[
            pl.BlockSpec((tile, rows.shape[1]), lambda i: (i, 0)),
            pl.BlockSpec((vocab, depth), lambda i: (0, 0)),
        ],
        out_specs=pl.BlockSpec((8, tile), lambda i: (0, i)),
        compiler_params=pltpu.CompilerParams(vmem_limit_bytes=56 * 1024 * 1024),
        cost_estimate=pl.CostEstimate(
            flops=2 * count * depth * vocab,
            transcendentals=count * vocab,
            bytes_accessed=2 * count * rows.shape[1] + 2 * depth * vocab + 32 * count,
        ),
    )(rows, weight_t)


def on_device(
    hidden, norm_gain, head_weight, value_weight, token_ids, slot_mask, lengths, request_order
):
    own_rows = hidden.shape[0]
    vocab_local = head_weight.shape[1]
    n_tensor = lax.axis_size("tensor")
    n_dp = lax.axis_size("dp")
    tensor_index = lax.axis_index("tensor")
    widened = hidden.astype(jnp.float32)
    inverse_rms = lax.rsqrt(jnp.mean(widened * widened, axis=1, keepdims=True) + EPSILON)
    normed = (widened * inverse_rms * norm_gain).astype(jnp.bfloat16)
    weight_mask = slot_mask.astype(jnp.float32)
    token_value = weight_mask * jnp.dot(normed, value_weight, preferred_element_type=jnp.float32)

    width = hidden.shape[1]
    live_sum = jnp.cumsum(slot_mask)
    slot_index = jnp.arange(own_rows, dtype=jnp.int32)
    chosen = (slot_mask[None, :] == 1) & (
        live_sum[None, :] - 1 == jnp.arange(LIVE, dtype=jnp.int32)[:, None]
    )
    source = jnp.sum(jnp.where(chosen, slot_index[None, :], 0), axis=1)
    block = prep(hidden, norm_gain, slot_mask, token_ids)
    gathered = lax.all_gather(block, "tensor", axis=0, tiled=True)
    row_count = gathered.shape[0]
    stats = row_stats(gathered, head_weight.T, 256 if row_count % 256 == 0 else row_count)
    blocks = stats[:4].reshape(4, n_tensor, LIVE).transpose(1, 0, 2)
    request_count = lengths.shape[1]
    span_lengths = lengths[0]
    span_ends = jnp.cumsum(span_lengths)
    slot_ids = tensor_index * own_rows + source
    position = jnp.sum((slot_ids[:, None] >= span_ends[None, :]).astype(jnp.int32), axis=1)
    live = jnp.arange(LIVE, dtype=jnp.int32) < live_sum[-1]
    member = (position[None, :] == jnp.arange(8, dtype=jnp.int32)[:, None]) & live[None, :]
    spans = (
        jnp.zeros((8, 128), jnp.float32)
        .at[:, :LIVE].set(member.astype(jnp.float32))
        .at[:, 127].set(jnp.ones((8,), jnp.float32).at[:request_count].set(span_lengths.astype(jnp.float32)))
    )
    ids_tile = jnp.zeros((8, 128), jnp.float32).at[:request_count, 1].set(request_order.astype(jnp.float32))
    place = live_sum - 1
    spread = ((place[:, None] == jnp.arange(LIVE, dtype=jnp.int32)[None, :]) & (slot_mask[:, None] == 1))
    result = finish(blocks, spans, ids_tile, spread.astype(jnp.float32), n_tensor, n_dp, request_count)
    token_logprob = result[0, :own_rows]
    token_entropy = result[1, :own_rows]
    request_score = result[2, :request_count]
    return (token_logprob, token_entropy, token_value, request_score)


def solution(mesh):
    return jax.shard_map(
        on_device,
        mesh=mesh,
        in_specs=(
            P(("dp", "tensor"), None),
            P(),
            P(None, "tensor"),
            P(),
            P(("dp", "tensor")),
            P(("dp", "tensor")),
            P("dp", None),
            P("dp"),
        ),
        out_specs=(P(("dp", "tensor")), P(("dp", "tensor")), P(("dp", "tensor")), P("dp")),
        check_vma=False,
    )
```

```python
import jax
import jax.numpy as jnp
from jax import lax
from jax.experimental import pallas as pl
from jax.experimental.pallas import tpu as pltpu
from jax.sharding import PartitionSpec as P

EPSILON = 1e-06
MESH = pl.DeviceIdType.MESH
LIVE = 48


def finish_kernel(n_tensor, n_dp, count, send_ref, span_ref, ids_ref, spread_ref, result_ref,
                  held, t_held, d_held, part_msg, route_msg,
                  a_send, a_recv, t_send, t_recv, d_send, d_recv):
    me = lax.axis_index("tensor")
    dp = lax.axis_index("dp")
    barrier = pltpu.get_barrier_semaphore()
    for offset in range(1, n_tensor):
        peer = lax.rem(me + offset, n_tensor)
        pl.semaphore_signal(barrier, inc=1, device_id=(dp, peer), device_id_type=MESH)
    for offset in range(1, n_dp):
        peer = lax.rem(dp + offset, n_dp)
        pl.semaphore_signal(barrier, inc=1, device_id=(peer, me), device_id_type=MESH)
    pl.semaphore_wait(barrier, n_tensor - 1 + n_dp - 1)

    held[me] = send_ref[me]
    copies = []
    for offset in range(1, n_tensor):
        peer = lax.rem(me + offset, n_tensor)
        copy = pltpu.make_async_remote_copy(
            src_ref=send_ref.at[peer], dst_ref=held.at[me],
            send_sem=a_send.at[offset], recv_sem=a_recv.at[offset],
            device_id=(dp, peer), device_id_type=MESH,
        )
        copy.start()
        copies.append(copy)
    for copy in copies:
        copy.wait_send()
    for offset in range(1, n_tensor):
        source = lax.rem(me + n_tensor - offset, n_tensor)
        pltpu.make_async_remote_copy(
            src_ref=send_ref.at[source], dst_ref=held.at[source],
            send_sem=a_send.at[offset], recv_sem=a_recv.at[offset],
            device_id=(dp, source), device_id_type=MESH,
        ).wait_recv()

    lanes = held.shape[2]
    peak = lax.fori_loop(
        0, n_tensor, lambda p, m: jnp.maximum(m, held[p][0:1, :]),
        jnp.full((1, lanes), -jnp.inf, jnp.float32),
    )

    def gather_sums(p, sums):
        mass, spread, target = sums
        block = held[p]
        gap = block[0:1, :] - peak
        factor = jnp.exp(gap)
        mass = mass + factor * block[1:2, :]
        spread = spread + factor * (block[2:3, :] + gap * block[1:2, :])
        return mass, spread, target + block[3:4, :]

    zero = jnp.zeros((1, lanes), jnp.float32)
    mass, spread, target = lax.fori_loop(0, n_tensor, gather_sums, (zero, zero, zero))
    log_mass = jnp.log(mass)
    logprob = target - peak - log_mass
    entropy = log_mass - spread / mass

    spans = span_ref[...]
    partial = jnp.sum(spans[:, :lanes] * logprob, axis=1, keepdims=True) / spans[:, 127:128]
    part_msg[...] = jnp.broadcast_to(partial, part_msg.shape)
    t_held[me] = part_msg[...]
    copies = []
    for offset in range(1, n_tensor):
        peer = lax.rem(me + offset, n_tensor)
        copy = pltpu.make_async_remote_copy(
            src_ref=part_msg, dst_ref=t_held.at[me],
            send_sem=t_send.at[offset], recv_sem=t_recv.at[offset],
            device_id=(dp, peer), device_id_type=MESH,
        )
        copy.start()
        copies.append(copy)
    slots = spread_ref.shape[0]
    placed = spread_ref[...] > 0.0
    same = (
        lax.broadcasted_iota(jnp.int32, (slots, slots), 0)
        == lax.broadcasted_iota(jnp.int32, (slots, slots), 1)
    )
    result_ref[...] = jnp.zeros(result_ref.shape, jnp.float32)
    for index, value in enumerate((logprob, entropy)):
        column = jnp.sum(jnp.where(placed, value, 0.0), axis=1, keepdims=True)
        result_ref[index:index + 1, :slots] = jnp.sum(jnp.where(same, column, 0.0), axis=0, keepdims=True)
    for copy in copies:
        copy.wait_send()
    for offset in range(1, n_tensor):
        source = lax.rem(me + n_tensor - offset, n_tensor)
        pltpu.make_async_remote_copy(
            src_ref=part_msg, dst_ref=t_held.at[source],
            send_sem=t_send.at[offset], recv_sem=t_recv.at[offset],
            device_id=(dp, source), device_id_type=MESH,
        ).wait_recv()

    total = jnp.sum(t_held[...], axis=0)
    lane = lax.broadcasted_iota(jnp.int32, total.shape, 1)
    route_msg[...] = jnp.where(lane == 0, total, jnp.where(lane == 1, ids_ref[...], 0.0))
    d_held[dp] = route_msg[...]
    copies = []
    for offset in range(1, n_dp):
        peer = lax.rem(dp + offset, n_dp)
        copy = pltpu.make_async_remote_copy(
            src_ref=route_msg, dst_ref=d_held.at[dp],
            send_sem=d_send.at[offset], recv_sem=d_recv.at[offset],
            device_id=(peer, me), device_id_type=MESH,
        )
        copy.start()
        copies.append(copy)
    for copy in copies:
        copy.wait_send()
    for offset in range(1, n_dp):
        source = lax.rem(dp + n_dp - offset, n_dp)
        pltpu.make_async_remote_copy(
            src_ref=route_msg, dst_ref=d_held.at[source],
            send_sem=d_send.at[offset], recv_sem=d_recv.at[offset],
            device_id=(source, me), device_id_type=MESH,
        ).wait_recv()
    wanted = (dp * count + lax.broadcasted_iota(jnp.int32, (1, count), 1)).astype(jnp.float32)
    score = jnp.zeros((1, count), jnp.float32)
    for group in range(n_dp):
        block = d_held[group]
        hit = block[:count, 1:2] == wanted
        score = score + jnp.sum(jnp.where(hit, block[:count, 0:1], 0.0), axis=0, keepdims=True)
    result_ref[2:3, :count] = score


def finish(blocks, spans, ids, spread, n_tensor, n_dp, count):
    tile = spans.shape
    lanes = blocks.shape[2]
    return pl.pallas_call(
        lambda *refs: finish_kernel(n_tensor, n_dp, count, *refs),
        out_shape=jax.ShapeDtypeStruct((8, 128), jnp.float32),
        in_specs=[pl.BlockSpec(memory_space=pltpu.VMEM)] * 4,
        out_specs=pl.BlockSpec(memory_space=pltpu.VMEM),
        scratch_shapes=[
            pltpu.VMEM(blocks.shape, jnp.float32),
            pltpu.VMEM((n_tensor,) + tile, jnp.float32),
            pltpu.VMEM((n_dp,) + tile, jnp.float32),
            pltpu.VMEM(tile, jnp.float32),
            pltpu.VMEM(tile, jnp.float32),
            pltpu.SemaphoreType.DMA((n_tensor,)),
            pltpu.SemaphoreType.DMA((n_tensor,)),
            pltpu.SemaphoreType.DMA((n_tensor,)),
            pltpu.SemaphoreType.DMA((n_tensor,)),
            pltpu.SemaphoreType.DMA((n_dp,)),
            pltpu.SemaphoreType.DMA((n_dp,)),
        ],
        compiler_params=pltpu.CompilerParams(collective_id=3, has_side_effects=True),
    )(blocks, spans, ids, spread)


def prep_kernel(hidden_ref, gain_ref, mask_ref, ids_ref, out_ref):
    width = hidden_ref.shape[1]
    own_rows = hidden_ref.shape[0]
    widened = hidden_ref[...].astype(jnp.float32)
    inverse_rms = lax.rsqrt(jnp.mean(widened * widened, axis=1, keepdims=True) + EPSILON)
    normed = (widened * inverse_rms * gain_ref[...]).astype(jnp.bfloat16)
    live = jnp.broadcast_to(mask_ref[...].astype(jnp.float32), (8, own_rows))
    upper = (
        lax.broadcasted_iota(jnp.int32, (own_rows, own_rows), 0)
        <= lax.broadcasted_iota(jnp.int32, (own_rows, own_rows), 1)
    ).astype(jnp.float32)
    live_sum = jnp.dot(live, upper, preferred_element_type=jnp.float32)[0:1, :]
    rank = lax.broadcasted_iota(jnp.int32, (LIVE, own_rows), 0).astype(jnp.float32)
    chosen = ((live[0:1, :] == 1.0) & (live_sum - 1.0 == rank)).astype(jnp.bfloat16)
    out_ref[:, :width] = jnp.dot(chosen, normed, preferred_element_type=jnp.float32).astype(jnp.bfloat16)
    ids = ids_ref[...]
    high = lax.shift_right_logical(ids, 8).astype(jnp.float32)
    low = jnp.bitwise_and(ids, 255).astype(jnp.float32)
    row = lax.broadcasted_iota(jnp.int32, (128, own_rows), 0)
    meta_in = jnp.where(row == 0, high, jnp.where(row == 1, low, 0.0)).astype(jnp.bfloat16)
    meta = lax.dot_general(
        chosen, meta_in, (((1,), (1,)), ((), ())), preferred_element_type=jnp.float32
    )
    out_ref[:, width:] = meta.astype(jnp.bfloat16)


def prep(hidden, norm_gain, slot_mask, token_ids):
    own_rows, width = hidden.shape
    return pl.pallas_call(
        prep_kernel,
        out_shape=jax.ShapeDtypeStruct((LIVE, width + 128), jnp.bfloat16),
        in_specs=[pl.BlockSpec(memory_space=pltpu.VMEM)] * 4,
        out_specs=pl.BlockSpec(memory_space=pltpu.VMEM),
    )(hidden, norm_gain.reshape(1, width), slot_mask.reshape(1, own_rows), token_ids.reshape(1, own_rows))


def stats_kernel(x_ref, wt_ref, out_ref):
    vocab, depth = wt_ref.shape
    contract_last = (((1,), (1,)), ((), ()))
    logits = lax.dot_general(wt_ref[...], x_ref[:, :depth], contract_last, preferred_element_type=jnp.float32)
    pick = (
        lax.broadcasted_iota(jnp.int32, (8, 128), 0) == lax.broadcasted_iota(jnp.int32, (8, 128), 1)
    ).astype(jnp.bfloat16)
    meta = lax.dot_general(pick, x_ref[:, depth:depth + 128], contract_last, preferred_element_type=jnp.float32)
    token = (meta[0:1, :] * 256.0 + meta[1:2, :]).astype(jnp.int32) - lax.axis_index("tensor") * vocab
    peak = jnp.max(logits, axis=0, keepdims=True)
    shifted = logits - peak
    weights = jnp.exp(shifted)
    mass = jnp.sum(weights, axis=0, keepdims=True)
    spread = jnp.sum(weights * shifted, axis=0, keepdims=True)
    entry = lax.broadcasted_iota(jnp.int32, logits.shape, 0)
    target = jnp.sum(jnp.where(entry == token, logits, 0.0), axis=0, keepdims=True)
    row = lax.broadcasted_iota(jnp.int32, out_ref.shape, 0)
    out_ref[...] = jnp.where(
        row == 0, peak,
        jnp.where(row == 1, mass, jnp.where(row == 2, spread, jnp.where(row == 3, target, 0.0))),
    )


def row_stats(rows, weight_t, tile):
    count = rows.shape[0]
    vocab, depth = weight_t.shape
    return pl.pallas_call(
        stats_kernel,
        out_shape=jax.ShapeDtypeStruct((8, count), jnp.float32),
        grid=(count // tile,),
        in_specs=[
            pl.BlockSpec((tile, rows.shape[1]), lambda i: (i, 0)),
            pl.BlockSpec((vocab, depth), lambda i: (0, 0)),
        ],
        out_specs=pl.BlockSpec((8, tile), lambda i: (0, i)),
        compiler_params=pltpu.CompilerParams(vmem_limit_bytes=56 * 1024 * 1024),
        cost_estimate=pl.CostEstimate(
            flops=2 * count * depth * vocab,
            transcendentals=count * vocab,
            bytes_accessed=2 * count * rows.shape[1] + 2 * depth * vocab + 32 * count,
        ),
    )(rows, weight_t)


def on_device(
    hidden, norm_gain, head_weight, value_weight, token_ids, slot_mask, lengths, request_order
):
    own_rows = hidden.shape[0]
    vocab_local = head_weight.shape[1]
    n_tensor = lax.axis_size("tensor")
    n_dp = lax.axis_size("dp")
    tensor_index = lax.axis_index("tensor")
    widened = hidden.astype(jnp.float32)
    inverse_rms = lax.rsqrt(jnp.mean(widened * widened, axis=1, keepdims=True) + EPSILON)
    normed = (widened * inverse_rms * norm_gain).astype(jnp.bfloat16)
    weight_mask = slot_mask.astype(jnp.float32)
    token_value = weight_mask * jnp.dot(normed, value_weight, preferred_element_type=jnp.float32)

    width = hidden.shape[1]
    live_sum = jnp.cumsum(slot_mask)
    slot_index = jnp.arange(own_rows, dtype=jnp.int32)
    chosen = (slot_mask[None, :] == 1) & (
        live_sum[None, :] - 1 == jnp.arange(LIVE, dtype=jnp.int32)[:, None]
    )
    source = jnp.sum(jnp.where(chosen, slot_index[None, :], 0), axis=1)
    block = prep(hidden, norm_gain, slot_mask, token_ids)
    gathered = lax.all_gather(block, "tensor", axis=0, tiled=True)
    row_count = gathered.shape[0]
    stats = row_stats(gathered, head_weight.T, 256 if row_count % 256 == 0 else row_count)
    blocks = stats[:4].reshape(4, n_tensor, LIVE).transpose(1, 0, 2)
    request_count = lengths.shape[1]
    span_lengths = lengths[0]
    span_ends = jnp.cumsum(span_lengths)
    slot_ids = tensor_index * own_rows + source
    position = jnp.sum((slot_ids[:, None] >= span_ends[None, :]).astype(jnp.int32), axis=1)
    live = jnp.arange(LIVE, dtype=jnp.int32) < live_sum[-1]
    member = (position[None, :] == jnp.arange(8, dtype=jnp.int32)[:, None]) & live[None, :]
    spans = (
        jnp.zeros((8, 128), jnp.float32)
        .at[:, :LIVE].set(member.astype(jnp.float32))
        .at[:, 127].set(jnp.ones((8,), jnp.float32).at[:request_count].set(span_lengths.astype(jnp.float32)))
    )
    ids_tile = jnp.zeros((8, 128), jnp.float32).at[:request_count, 1].set(request_order.astype(jnp.float32))
    place = live_sum - 1
    spread = ((place[:, None] == jnp.arange(LIVE, dtype=jnp.int32)[None, :]) & (slot_mask[:, None] == 1))
    result = finish(blocks, spans, ids_tile, spread.astype(jnp.float32), n_tensor, n_dp, request_count)
    token_logprob = result[0, :own_rows]
    token_entropy = result[1, :own_rows]
    request_score = result[2, :request_count]
    return (token_logprob, token_entropy, token_value, request_score)


def solution(mesh):
    return jax.shard_map(
        on_device,
        mesh=mesh,
        in_specs=(
            P(("dp", "tensor"), None),
            P(),
            P(None, "tensor"),
            P(),
            P(("dp", "tensor")),
            P(("dp", "tensor")),
            P("dp", None),
            P("dp"),
        ),
        out_specs=(P(("dp", "tensor")), P(("dp", "tensor")), P(("dp", "tensor")), P("dp")),
        check_vma=False,
    )
```

```python
import jax
import jax.numpy as jnp
from jax import lax
from jax.experimental import pallas as pl
from jax.experimental.pallas import tpu as pltpu
from jax.sharding import PartitionSpec as P

EPSILON = 1e-06
MESH = pl.DeviceIdType.MESH
LIVE = 48


def finish_kernel(n_tensor, n_dp, count, send_ref, span_ref, ids_ref, spread_ref, result_ref,
                  held, t_held, d_held, part_msg, route_msg,
                  a_send, a_recv, t_send, t_recv, d_send, d_recv):
    me = lax.axis_index("tensor")
    dp = lax.axis_index("dp")
    barrier = pltpu.get_barrier_semaphore()
    for offset in range(1, n_tensor):
        peer = lax.rem(me + offset, n_tensor)
        pl.semaphore_signal(barrier, inc=1, device_id=(dp, peer), device_id_type=MESH)
    for offset in range(1, n_dp):
        peer = lax.rem(dp + offset, n_dp)
        pl.semaphore_signal(barrier, inc=1, device_id=(peer, me), device_id_type=MESH)
    pl.semaphore_wait(barrier, n_tensor - 1 + n_dp - 1)

    held[me] = send_ref[me]
    copies = []
    for offset in range(1, n_tensor):
        peer = lax.rem(me + offset, n_tensor)
        copy = pltpu.make_async_remote_copy(
            src_ref=send_ref.at[peer], dst_ref=held.at[me],
            send_sem=a_send.at[offset], recv_sem=a_recv.at[offset],
            device_id=(dp, peer), device_id_type=MESH,
        )
        copy.start()
        copies.append(copy)
    for copy in copies:
        copy.wait_send()
    for offset in range(1, n_tensor):
        source = lax.rem(me + n_tensor - offset, n_tensor)
        pltpu.make_async_remote_copy(
            src_ref=send_ref.at[source], dst_ref=held.at[source],
            send_sem=a_send.at[offset], recv_sem=a_recv.at[offset],
            device_id=(dp, source), device_id_type=MESH,
        ).wait_recv()

    lanes = held.shape[2]
    peak = lax.fori_loop(
        0, n_tensor, lambda p, m: jnp.maximum(m, held[p][0:1, :]),
        jnp.full((1, lanes), -jnp.inf, jnp.float32),
    )

    def gather_sums(p, sums):
        mass, spread, target = sums
        block = held[p]
        gap = block[0:1, :] - peak
        factor = jnp.exp(gap)
        mass = mass + factor * block[1:2, :]
        spread = spread + factor * (block[2:3, :] + gap * block[1:2, :])
        return mass, spread, target + block[3:4, :]

    zero = jnp.zeros((1, lanes), jnp.float32)
    mass, spread, target = lax.fori_loop(0, n_tensor, gather_sums, (zero, zero, zero))
    log_mass = jnp.log(mass)
    logprob = target - peak - log_mass
    entropy = log_mass - spread / mass
    slots = spread_ref.shape[0]
    placed = spread_ref[...] > 0.0
    same = (
        lax.broadcasted_iota(jnp.int32, (slots, slots), 0)
        == lax.broadcasted_iota(jnp.int32, (slots, slots), 1)
    )
    result_ref[...] = jnp.zeros(result_ref.shape, jnp.float32)
    for index, value in enumerate((logprob, entropy)):
        column = jnp.sum(jnp.where(placed, value, 0.0), axis=1, keepdims=True)
        result_ref[index:index + 1, :slots] = jnp.sum(jnp.where(same, column, 0.0), axis=0, keepdims=True)

    spans = span_ref[...]
    partial = jnp.sum(spans[:, :lanes] * logprob, axis=1, keepdims=True) / spans[:, 127:128]
    part_msg[...] = jnp.broadcast_to(partial, part_msg.shape)
    t_held[me] = part_msg[...]
    copies = []
    for offset in range(1, n_tensor):
        peer = lax.rem(me + offset, n_tensor)
        copy = pltpu.make_async_remote_copy(
            src_ref=part_msg, dst_ref=t_held.at[me],
            send_sem=t_send.at[offset], recv_sem=t_recv.at[offset],
            device_id=(dp, peer), device_id_type=MESH,
        )
        copy.start()
        copies.append(copy)
    for copy in copies:
        copy.wait_send()
    for offset in range(1, n_tensor):
        source = lax.rem(me + n_tensor - offset, n_tensor)
        pltpu.make_async_remote_copy(
            src_ref=part_msg, dst_ref=t_held.at[source],
            send_sem=t_send.at[offset], recv_sem=t_recv.at[offset],
            device_id=(dp, source), device_id_type=MESH,
        ).wait_recv()

    total = jnp.sum(t_held[...], axis=0)
    lane = lax.broadcasted_iota(jnp.int32, total.shape, 1)
    route_msg[...] = jnp.where(lane == 0, total, jnp.where(lane == 1, ids_ref[...], 0.0))
    d_held[dp] = route_msg[...]
    copies = []
    for offset in range(1, n_dp):
        peer = lax.rem(dp + offset, n_dp)
        copy = pltpu.make_async_remote_copy(
            src_ref=route_msg, dst_ref=d_held.at[dp],
            send_sem=d_send.at[offset], recv_sem=d_recv.at[offset],
            device_id=(peer, me), device_id_type=MESH,
        )
        copy.start()
        copies.append(copy)
    for copy in copies:
        copy.wait_send()
    for offset in range(1, n_dp):
        source = lax.rem(dp + n_dp - offset, n_dp)
        pltpu.make_async_remote_copy(
            src_ref=route_msg, dst_ref=d_held.at[source],
            send_sem=d_send.at[offset], recv_sem=d_recv.at[offset],
            device_id=(source, me), device_id_type=MESH,
        ).wait_recv()
    wanted = (dp * count + lax.broadcasted_iota(jnp.int32, (1, count), 1)).astype(jnp.float32)
    score = jnp.zeros((1, count), jnp.float32)
    for group in range(n_dp):
        block = d_held[group]
        hit = block[:count, 1:2] == wanted
        score = score + jnp.sum(jnp.where(hit, block[:count, 0:1], 0.0), axis=0, keepdims=True)
    result_ref[2:3, :count] = score


def finish(blocks, spans, ids, spread, n_tensor, n_dp, count):
    tile = spans.shape
    lanes = blocks.shape[2]
    return pl.pallas_call(
        lambda *refs: finish_kernel(n_tensor, n_dp, count, *refs),
        out_shape=jax.ShapeDtypeStruct((8, 128), jnp.float32),
        in_specs=[pl.BlockSpec(memory_space=pltpu.VMEM)] * 4,
        out_specs=pl.BlockSpec(memory_space=pltpu.VMEM),
        scratch_shapes=[
            pltpu.VMEM(blocks.shape, jnp.float32),
            pltpu.VMEM((n_tensor,) + tile, jnp.float32),
            pltpu.VMEM((n_dp,) + tile, jnp.float32),
            pltpu.VMEM(tile, jnp.float32),
            pltpu.VMEM(tile, jnp.float32),
            pltpu.SemaphoreType.DMA((n_tensor,)),
            pltpu.SemaphoreType.DMA((n_tensor,)),
            pltpu.SemaphoreType.DMA((n_tensor,)),
            pltpu.SemaphoreType.DMA((n_tensor,)),
            pltpu.SemaphoreType.DMA((n_dp,)),
            pltpu.SemaphoreType.DMA((n_dp,)),
        ],
        compiler_params=pltpu.CompilerParams(collective_id=3, has_side_effects=True),
    )(blocks, spans, ids, spread)


def prep_kernel(hidden_ref, gain_ref, mask_ref, ids_ref, out_ref):
    width = hidden_ref.shape[1]
    own_rows = hidden_ref.shape[0]
    widened = hidden_ref[...].astype(jnp.float32)
    inverse_rms = lax.rsqrt(jnp.mean(widened * widened, axis=1, keepdims=True) + EPSILON)
    normed = (widened * inverse_rms * gain_ref[...]).astype(jnp.bfloat16)
    live = jnp.broadcast_to(mask_ref[...].astype(jnp.float32), (8, own_rows))
    upper = (
        lax.broadcasted_iota(jnp.int32, (own_rows, own_rows), 0)
        <= lax.broadcasted_iota(jnp.int32, (own_rows, own_rows), 1)
    ).astype(jnp.float32)
    live_sum = jnp.dot(live, upper, preferred_element_type=jnp.float32)[0:1, :]
    rank = lax.broadcasted_iota(jnp.int32, (LIVE, own_rows), 0).astype(jnp.float32)
    chosen = ((live[0:1, :] == 1.0) & (live_sum - 1.0 == rank)).astype(jnp.bfloat16)
    out_ref[:, :width] = jnp.dot(chosen, normed, preferred_element_type=jnp.float32).astype(jnp.bfloat16)
    ids = ids_ref[...]
    high = lax.shift_right_logical(ids, 8).astype(jnp.float32)
    low = jnp.bitwise_and(ids, 255).astype(jnp.float32)
    row = lax.broadcasted_iota(jnp.int32, (128, own_rows), 0)
    meta_in = jnp.where(row == 0, high, jnp.where(row == 1, low, 0.0)).astype(jnp.bfloat16)
    meta = lax.dot_general(
        chosen, meta_in, (((1,), (1,)), ((), ())), preferred_element_type=jnp.float32
    )
    out_ref[:, width:] = meta.astype(jnp.bfloat16)


def prep(hidden, norm_gain, slot_mask, token_ids):
    own_rows, width = hidden.shape
    return pl.pallas_call(
        prep_kernel,
        out_shape=jax.ShapeDtypeStruct((LIVE, width + 128), jnp.bfloat16),
        in_specs=[pl.BlockSpec(memory_space=pltpu.VMEM)] * 4,
        out_specs=pl.BlockSpec(memory_space=pltpu.VMEM),
    )(hidden, norm_gain.reshape(1, width), slot_mask.reshape(1, own_rows), token_ids.reshape(1, own_rows))


def stats_kernel(x_ref, wt_ref, out_ref, logits_ref):
    vocab, depth = wt_ref.shape
    tile = x_ref.shape[0]
    contract_last = (((1,), (1,)), ((), ()))
    logits_ref[...] = lax.dot_general(
        wt_ref[...], x_ref[:, :depth], contract_last, preferred_element_type=jnp.float32
    )
    pick = (
        lax.broadcasted_iota(jnp.int32, (8, 128), 0) == lax.broadcasted_iota(jnp.int32, (8, 128), 1)
    ).astype(jnp.bfloat16)
    meta = lax.dot_general(pick, x_ref[:, depth:depth + 128], contract_last, preferred_element_type=jnp.float32)
    token = (meta[0:1, :] * 256.0 + meta[1:2, :]).astype(jnp.int32) - lax.axis_index("tensor") * vocab
    chunks = vocab // 8
    rest = vocab - chunks * 8

    def top(c, m):
        return jnp.maximum(m, logits_ref[pl.ds(pl.multiple_of(c * 8, 8), 8), :])

    peak = jnp.max(lax.fori_loop(0, chunks, top, jnp.full((8, tile), -jnp.inf, jnp.float32)), axis=0, keepdims=True)
    if rest:
        peak = jnp.maximum(peak, jnp.max(logits_ref[chunks * 8:vocab, :], axis=0, keepdims=True))

    def accumulate(block, first, sums):
        mass, spread, target = sums
        shifted = block - peak
        weights = jnp.exp(shifted)
        entry = first + lax.broadcasted_iota(jnp.int32, block.shape, 0)
        return (
            mass + jnp.sum(weights, axis=0, keepdims=True) if block.shape[0] != 8 else mass + weights,
            spread + jnp.sum(weights * shifted, axis=0, keepdims=True) if block.shape[0] != 8 else spread + weights * shifted,
            target + jnp.sum(jnp.where(entry == token, block, 0.0), axis=0, keepdims=True)
            if block.shape[0] != 8 else target + jnp.where(entry == token, block, 0.0),
        )

    def body(c, sums):
        start = pl.multiple_of(c * 8, 8)
        return accumulate(logits_ref[pl.ds(start, 8), :], start, sums)

    zero = jnp.zeros((8, tile), jnp.float32)
    sums = lax.fori_loop(0, chunks, body, (zero, zero, zero))
    mass, spread, target = (jnp.sum(value, axis=0, keepdims=True) for value in sums)
    if rest:
        one = jnp.zeros((1, tile), jnp.float32)
        extra = accumulate(logits_ref[chunks * 8:vocab, :], chunks * 8, (one, one, one))
        mass, spread, target = mass + extra[0], spread + extra[1], target + extra[2]
    row = lax.broadcasted_iota(jnp.int32, out_ref.shape, 0)
    out_ref[...] = jnp.where(
        row == 0, peak,
        jnp.where(row == 1, mass, jnp.where(row == 2, spread, jnp.where(row == 3, target, 0.0))),
    )


def row_stats(rows, weight_t, tile):
    count = rows.shape[0]
    vocab, depth = weight_t.shape
    return pl.pallas_call(
        stats_kernel,
        out_shape=jax.ShapeDtypeStruct((8, count), jnp.float32),
        grid=(count // tile,),
        in_specs=[
            pl.BlockSpec((tile, rows.shape[1]), lambda i: (i, 0)),
            pl.BlockSpec((vocab, depth), lambda i: (0, 0)),
        ],
        out_specs=pl.BlockSpec((8, tile), lambda i: (0, i)),
        scratch_shapes=[pltpu.VMEM((vocab, tile), jnp.float32)],
        compiler_params=pltpu.CompilerParams(vmem_limit_bytes=56 * 1024 * 1024),
        cost_estimate=pl.CostEstimate(
            flops=2 * count * depth * vocab,
            transcendentals=count * vocab,
            bytes_accessed=2 * count * rows.shape[1] + 2 * depth * vocab + 32 * count,
        ),
    )(rows, weight_t)


def on_device(
    hidden, norm_gain, head_weight, value_weight, token_ids, slot_mask, lengths, request_order
):
    own_rows = hidden.shape[0]
    vocab_local = head_weight.shape[1]
    n_tensor = lax.axis_size("tensor")
    n_dp = lax.axis_size("dp")
    tensor_index = lax.axis_index("tensor")
    widened = hidden.astype(jnp.float32)
    inverse_rms = lax.rsqrt(jnp.mean(widened * widened, axis=1, keepdims=True) + EPSILON)
    normed = (widened * inverse_rms * norm_gain).astype(jnp.bfloat16)
    weight_mask = slot_mask.astype(jnp.float32)
    token_value = weight_mask * jnp.dot(normed, value_weight, preferred_element_type=jnp.float32)

    width = hidden.shape[1]
    live_sum = jnp.cumsum(slot_mask)
    slot_index = jnp.arange(own_rows, dtype=jnp.int32)
    chosen = (slot_mask[None, :] == 1) & (
        live_sum[None, :] - 1 == jnp.arange(LIVE, dtype=jnp.int32)[:, None]
    )
    source = jnp.sum(jnp.where(chosen, slot_index[None, :], 0), axis=1)
    block = prep(hidden, norm_gain, slot_mask, token_ids)
    gathered = lax.all_gather(block, "tensor", axis=0, tiled=True)
    row_count = gathered.shape[0]
    stats = row_stats(gathered, head_weight.T, 256 if row_count % 256 == 0 else row_count)
    blocks = stats[:4].reshape(4, n_tensor, LIVE).transpose(1, 0, 2)
    request_count = lengths.shape[1]
    span_lengths = lengths[0]
    span_ends = jnp.cumsum(span_lengths)
    slot_ids = tensor_index * own_rows + source
    position = jnp.sum((slot_ids[:, None] >= span_ends[None, :]).astype(jnp.int32), axis=1)
    live = jnp.arange(LIVE, dtype=jnp.int32) < live_sum[-1]
    member = (position[None, :] == jnp.arange(8, dtype=jnp.int32)[:, None]) & live[None, :]
    spans = (
        jnp.zeros((8, 128), jnp.float32)
        .at[:, :LIVE].set(member.astype(jnp.float32))
        .at[:, 127].set(jnp.ones((8,), jnp.float32).at[:request_count].set(span_lengths.astype(jnp.float32)))
    )
    ids_tile = jnp.zeros((8, 128), jnp.float32).at[:request_count, 1].set(request_order.astype(jnp.float32))
    place = live_sum - 1
    spread = ((place[:, None] == jnp.arange(LIVE, dtype=jnp.int32)[None, :]) & (slot_mask[:, None] == 1))
    result = finish(blocks, spans, ids_tile, spread.astype(jnp.float32), n_tensor, n_dp, request_count)
    token_logprob = result[0, :own_rows]
    token_entropy = result[1, :own_rows]
    request_score = result[2, :request_count]
    return (token_logprob, token_entropy, token_value, request_score)


def solution(mesh):
    return jax.shard_map(
        on_device,
        mesh=mesh,
        in_specs=(
            P(("dp", "tensor"), None),
            P(),
            P(None, "tensor"),
            P(),
            P(("dp", "tensor")),
            P(("dp", "tensor")),
            P("dp", None),
            P("dp"),
        ),
        out_specs=(P(("dp", "tensor")), P(("dp", "tensor")), P(("dp", "tensor")), P("dp")),
        check_vma=False,
    )
```

```python
import jax
import jax.numpy as jnp
from jax import lax
from jax.experimental import pallas as pl
from jax.experimental.pallas import tpu as pltpu
from jax.sharding import PartitionSpec as P

EPSILON = 1e-06
MESH = pl.DeviceIdType.MESH
LIVE = 48


def finish_kernel(n_tensor, n_dp, count, send_ref, span_ref, ids_ref, spread_ref, result_ref,
                  held, t_held, d_held, part_msg, route_msg,
                  a_send, a_recv, t_send, t_recv, d_send, d_recv):
    me = lax.axis_index("tensor")
    dp = lax.axis_index("dp")
    barrier = pltpu.get_barrier_semaphore()
    for offset in range(1, n_tensor):
        peer = lax.rem(me + offset, n_tensor)
        pl.semaphore_signal(barrier, inc=1, device_id=(dp, peer), device_id_type=MESH)
    for offset in range(1, n_dp):
        peer = lax.rem(dp + offset, n_dp)
        pl.semaphore_signal(barrier, inc=1, device_id=(peer, me), device_id_type=MESH)
    pl.semaphore_wait(barrier, n_tensor - 1 + n_dp - 1)

    held[me] = send_ref[me]
    copies = []
    for offset in range(1, n_tensor):
        peer = lax.rem(me + offset, n_tensor)
        copy = pltpu.make_async_remote_copy(
            src_ref=send_ref.at[peer], dst_ref=held.at[me],
            send_sem=a_send.at[offset], recv_sem=a_recv.at[offset],
            device_id=(dp, peer), device_id_type=MESH,
        )
        copy.start()
        copies.append(copy)
    for copy in copies:
        copy.wait_send()
    for offset in range(1, n_tensor):
        source = lax.rem(me + n_tensor - offset, n_tensor)
        pltpu.make_async_remote_copy(
            src_ref=send_ref.at[source], dst_ref=held.at[source],
            send_sem=a_send.at[offset], recv_sem=a_recv.at[offset],
            device_id=(dp, source), device_id_type=MESH,
        ).wait_recv()

    lanes = held.shape[2]
    peak = lax.fori_loop(
        0, n_tensor, lambda p, m: jnp.maximum(m, held[p][0:1, :]),
        jnp.full((1, lanes), -jnp.inf, jnp.float32),
    )

    def gather_sums(p, sums):
        mass, spread, target = sums
        block = held[p]
        gap = block[0:1, :] - peak
        factor = jnp.exp(gap)
        mass = mass + factor * block[1:2, :]
        spread = spread + factor * (block[2:3, :] + gap * block[1:2, :])
        return mass, spread, target + block[3:4, :]

    zero = jnp.zeros((1, lanes), jnp.float32)
    mass, spread, target = lax.fori_loop(0, n_tensor, gather_sums, (zero, zero, zero))
    log_mass = jnp.log(mass)
    logprob = target - peak - log_mass
    entropy = log_mass - spread / mass
    slots = spread_ref.shape[0]
    placed = spread_ref[...] > 0.0
    same = (
        lax.broadcasted_iota(jnp.int32, (slots, slots), 0)
        == lax.broadcasted_iota(jnp.int32, (slots, slots), 1)
    )
    result_ref[...] = jnp.zeros(result_ref.shape, jnp.float32)
    for index, value in enumerate((logprob, entropy)):
        column = jnp.sum(jnp.where(placed, value, 0.0), axis=1, keepdims=True)
        result_ref[index:index + 1, :slots] = jnp.sum(jnp.where(same, column, 0.0), axis=0, keepdims=True)

    spans = span_ref[...]
    partial = jnp.sum(spans[:, :lanes] * logprob, axis=1, keepdims=True) / spans[:, 127:128]
    part_msg[...] = jnp.broadcast_to(partial, part_msg.shape)
    t_held[me] = part_msg[...]
    copies = []
    for offset in range(1, n_tensor):
        peer = lax.rem(me + offset, n_tensor)
        copy = pltpu.make_async_remote_copy(
            src_ref=part_msg, dst_ref=t_held.at[me],
            send_sem=t_send.at[offset], recv_sem=t_recv.at[offset],
            device_id=(dp, peer), device_id_type=MESH,
        )
        copy.start()
        copies.append(copy)
    for copy in copies:
        copy.wait_send()
    for offset in range(1, n_tensor):
        source = lax.rem(me + n_tensor - offset, n_tensor)
        pltpu.make_async_remote_copy(
            src_ref=part_msg, dst_ref=t_held.at[source],
            send_sem=t_send.at[offset], recv_sem=t_recv.at[offset],
            device_id=(dp, source), device_id_type=MESH,
        ).wait_recv()

    total = jnp.sum(t_held[...], axis=0)
    lane = lax.broadcasted_iota(jnp.int32, total.shape, 1)
    route_msg[...] = jnp.where(lane == 0, total, jnp.where(lane == 1, ids_ref[...], 0.0))
    d_held[dp] = route_msg[...]
    copies = []
    for offset in range(1, n_dp):
        peer = lax.rem(dp + offset, n_dp)
        copy = pltpu.make_async_remote_copy(
            src_ref=route_msg, dst_ref=d_held.at[dp],
            send_sem=d_send.at[offset], recv_sem=d_recv.at[offset],
            device_id=(peer, me), device_id_type=MESH,
        )
        copy.start()
        copies.append(copy)
    for copy in copies:
        copy.wait_send()
    for offset in range(1, n_dp):
        source = lax.rem(dp + n_dp - offset, n_dp)
        pltpu.make_async_remote_copy(
            src_ref=route_msg, dst_ref=d_held.at[source],
            send_sem=d_send.at[offset], recv_sem=d_recv.at[offset],
            device_id=(source, me), device_id_type=MESH,
        ).wait_recv()
    wanted = (dp * count + lax.broadcasted_iota(jnp.int32, (1, count), 1)).astype(jnp.float32)
    score = jnp.zeros((1, count), jnp.float32)
    for group in range(n_dp):
        block = d_held[group]
        hit = block[:count, 1:2] == wanted
        score = score + jnp.sum(jnp.where(hit, block[:count, 0:1], 0.0), axis=0, keepdims=True)
    result_ref[2:3, :count] = score


def finish(blocks, spans, ids, spread, n_tensor, n_dp, count):
    tile = spans.shape
    lanes = blocks.shape[2]
    return pl.pallas_call(
        lambda *refs: finish_kernel(n_tensor, n_dp, count, *refs),
        out_shape=jax.ShapeDtypeStruct((8, 128), jnp.float32),
        in_specs=[pl.BlockSpec(memory_space=pltpu.VMEM)] * 4,
        out_specs=pl.BlockSpec(memory_space=pltpu.VMEM),
        scratch_shapes=[
            pltpu.VMEM(blocks.shape, jnp.float32),
            pltpu.VMEM((n_tensor,) + tile, jnp.float32),
            pltpu.VMEM((n_dp,) + tile, jnp.float32),
            pltpu.VMEM(tile, jnp.float32),
            pltpu.VMEM(tile, jnp.float32),
            pltpu.SemaphoreType.DMA((n_tensor,)),
            pltpu.SemaphoreType.DMA((n_tensor,)),
            pltpu.SemaphoreType.DMA((n_tensor,)),
            pltpu.SemaphoreType.DMA((n_tensor,)),
            pltpu.SemaphoreType.DMA((n_dp,)),
            pltpu.SemaphoreType.DMA((n_dp,)),
        ],
        compiler_params=pltpu.CompilerParams(collective_id=3, has_side_effects=True),
    )(blocks, spans, ids, spread)


def prep_kernel(hidden_ref, gain_ref, mask_ref, ids_ref, out_ref):
    width = hidden_ref.shape[1]
    own_rows = hidden_ref.shape[0]
    widened = hidden_ref[...].astype(jnp.float32)
    inverse_rms = lax.rsqrt(jnp.mean(widened * widened, axis=1, keepdims=True) + EPSILON)
    normed = (widened * inverse_rms * gain_ref[...]).astype(jnp.bfloat16)
    live = jnp.broadcast_to(mask_ref[...].astype(jnp.float32), (8, own_rows))
    upper = (
        lax.broadcasted_iota(jnp.int32, (own_rows, own_rows), 0)
        <= lax.broadcasted_iota(jnp.int32, (own_rows, own_rows), 1)
    ).astype(jnp.float32)
    live_sum = jnp.dot(live, upper, preferred_element_type=jnp.float32)[0:1, :]
    rank = lax.broadcasted_iota(jnp.int32, (LIVE, own_rows), 0).astype(jnp.float32)
    chosen = ((live[0:1, :] == 1.0) & (live_sum - 1.0 == rank)).astype(jnp.bfloat16)
    out_ref[:, :width] = jnp.dot(chosen, normed, preferred_element_type=jnp.float32).astype(jnp.bfloat16)
    ids = ids_ref[...]
    high = lax.shift_right_logical(ids, 8).astype(jnp.float32)
    low = jnp.bitwise_and(ids, 255).astype(jnp.float32)
    row = lax.broadcasted_iota(jnp.int32, (128, own_rows), 0)
    meta_in = jnp.where(row == 0, high, jnp.where(row == 1, low, 0.0)).astype(jnp.bfloat16)
    meta = lax.dot_general(
        chosen, meta_in, (((1,), (1,)), ((), ())), preferred_element_type=jnp.float32
    )
    out_ref[:, width:] = meta.astype(jnp.bfloat16)


def prep(hidden, norm_gain, slot_mask, token_ids):
    own_rows, width = hidden.shape
    return pl.pallas_call(
        prep_kernel,
        out_shape=jax.ShapeDtypeStruct((LIVE, width + 128), jnp.bfloat16),
        in_specs=[pl.BlockSpec(memory_space=pltpu.VMEM)] * 4,
        out_specs=pl.BlockSpec(memory_space=pltpu.VMEM),
    )(hidden, norm_gain.reshape(1, width), slot_mask.reshape(1, own_rows), token_ids.reshape(1, own_rows))


def stats_kernel(x_ref, wt_ref, out_ref, logits_ref):
    vocab, depth = wt_ref.shape
    tile = x_ref.shape[0]
    contract_last = (((1,), (1,)), ((), ()))
    logits_ref[...] = lax.dot_general(
        wt_ref[...], x_ref[:, :depth], contract_last, preferred_element_type=jnp.float32
    )
    pick = (
        lax.broadcasted_iota(jnp.int32, (8, 128), 0) == lax.broadcasted_iota(jnp.int32, (8, 128), 1)
    ).astype(jnp.bfloat16)
    meta = lax.dot_general(pick, x_ref[:, depth:depth + 128], contract_last, preferred_element_type=jnp.float32)
    token = (meta[0:1, :] * 256.0 + meta[1:2, :]).astype(jnp.int32) - lax.axis_index("tensor") * vocab
    chunks = vocab // 8
    rest = vocab - chunks * 8

    def top(c, m):
        return jnp.maximum(m, logits_ref[pl.ds(pl.multiple_of(c * 8, 8), 8), :])

    peak = jnp.max(
        lax.fori_loop(0, chunks, top, jnp.full((8, tile), -jnp.inf, jnp.float32), unroll=7), axis=0, keepdims=True
    )
    if rest:
        peak = jnp.maximum(peak, jnp.max(logits_ref[chunks * 8:vocab, :], axis=0, keepdims=True))

    def accumulate(block, first, sums):
        mass, spread, target = sums
        shifted = block - peak
        weights = jnp.exp(shifted)
        entry = first + lax.broadcasted_iota(jnp.int32, block.shape, 0)
        return (
            mass + jnp.sum(weights, axis=0, keepdims=True) if block.shape[0] != 8 else mass + weights,
            spread + jnp.sum(weights * shifted, axis=0, keepdims=True) if block.shape[0] != 8 else spread + weights * shifted,
            target + jnp.sum(jnp.where(entry == token, block, 0.0), axis=0, keepdims=True)
            if block.shape[0] != 8 else target + jnp.where(entry == token, block, 0.0),
        )

    def body(c, sums):
        start = pl.multiple_of(c * 8, 8)
        return accumulate(logits_ref[pl.ds(start, 8), :], start, sums)

    zero = jnp.zeros((8, tile), jnp.float32)
    sums = lax.fori_loop(0, chunks, body, (zero, zero, zero), unroll=7)
    mass, spread, target = (jnp.sum(value, axis=0, keepdims=True) for value in sums)
    if rest:
        one = jnp.zeros((1, tile), jnp.float32)
        extra = accumulate(logits_ref[chunks * 8:vocab, :], chunks * 8, (one, one, one))
        mass, spread, target = mass + extra[0], spread + extra[1], target + extra[2]
    row = lax.broadcasted_iota(jnp.int32, out_ref.shape, 0)
    out_ref[...] = jnp.where(
        row == 0, peak,
        jnp.where(row == 1, mass, jnp.where(row == 2, spread, jnp.where(row == 3, target, 0.0))),
    )


def row_stats(rows, weight_t, tile):
    count = rows.shape[0]
    vocab, depth = weight_t.shape
    return pl.pallas_call(
        stats_kernel,
        out_shape=jax.ShapeDtypeStruct((8, count), jnp.float32),
        grid=(count // tile,),
        in_specs=[
            pl.BlockSpec((tile, rows.shape[1]), lambda i: (i, 0)),
            pl.BlockSpec((vocab, depth), lambda i: (0, 0)),
        ],
        out_specs=pl.BlockSpec((8, tile), lambda i: (0, i)),
        scratch_shapes=[pltpu.VMEM((vocab, tile), jnp.float32)],
        compiler_params=pltpu.CompilerParams(vmem_limit_bytes=56 * 1024 * 1024),
        cost_estimate=pl.CostEstimate(
            flops=2 * count * depth * vocab,
            transcendentals=count * vocab,
            bytes_accessed=2 * count * rows.shape[1] + 2 * depth * vocab + 32 * count,
        ),
    )(rows, weight_t)


def on_device(
    hidden, norm_gain, head_weight, value_weight, token_ids, slot_mask, lengths, request_order
):
    own_rows = hidden.shape[0]
    vocab_local = head_weight.shape[1]
    n_tensor = lax.axis_size("tensor")
    n_dp = lax.axis_size("dp")
    tensor_index = lax.axis_index("tensor")
    widened = hidden.astype(jnp.float32)
    inverse_rms = lax.rsqrt(jnp.mean(widened * widened, axis=1, keepdims=True) + EPSILON)
    normed = (widened * inverse_rms * norm_gain).astype(jnp.bfloat16)
    weight_mask = slot_mask.astype(jnp.float32)
    token_value = weight_mask * jnp.dot(normed, value_weight, preferred_element_type=jnp.float32)

    width = hidden.shape[1]
    live_sum = jnp.cumsum(slot_mask)
    slot_index = jnp.arange(own_rows, dtype=jnp.int32)
    chosen = (slot_mask[None, :] == 1) & (
        live_sum[None, :] - 1 == jnp.arange(LIVE, dtype=jnp.int32)[:, None]
    )
    source = jnp.sum(jnp.where(chosen, slot_index[None, :], 0), axis=1)
    block = prep(hidden, norm_gain, slot_mask, token_ids)
    gathered = lax.all_gather(block, "tensor", axis=0, tiled=True)
    row_count = gathered.shape[0]
    stats = row_stats(gathered, head_weight.T, 256 if row_count % 256 == 0 else row_count)
    blocks = stats[:4].reshape(4, n_tensor, LIVE).transpose(1, 0, 2)
    request_count = lengths.shape[1]
    span_lengths = lengths[0]
    span_ends = jnp.cumsum(span_lengths)
    slot_ids = tensor_index * own_rows + source
    position = jnp.sum((slot_ids[:, None] >= span_ends[None, :]).astype(jnp.int32), axis=1)
    live = jnp.arange(LIVE, dtype=jnp.int32) < live_sum[-1]
    member = (position[None, :] == jnp.arange(8, dtype=jnp.int32)[:, None]) & live[None, :]
    spans = (
        jnp.zeros((8, 128), jnp.float32)
        .at[:, :LIVE].set(member.astype(jnp.float32))
        .at[:, 127].set(jnp.ones((8,), jnp.float32).at[:request_count].set(span_lengths.astype(jnp.float32)))
    )
    ids_tile = jnp.zeros((8, 128), jnp.float32).at[:request_count, 1].set(request_order.astype(jnp.float32))
    place = live_sum - 1
    spread = ((place[:, None] == jnp.arange(LIVE, dtype=jnp.int32)[None, :]) & (slot_mask[:, None] == 1))
    result = finish(blocks, spans, ids_tile, spread.astype(jnp.float32), n_tensor, n_dp, request_count)
    token_logprob = result[0, :own_rows]
    token_entropy = result[1, :own_rows]
    request_score = result[2, :request_count]
    return (token_logprob, token_entropy, token_value, request_score)


def solution(mesh):
    return jax.shard_map(
        on_device,
        mesh=mesh,
        in_specs=(
            P(("dp", "tensor"), None),
            P(),
            P(None, "tensor"),
            P(),
            P(("dp", "tensor")),
            P(("dp", "tensor")),
            P("dp", None),
            P("dp"),
        ),
        out_specs=(P(("dp", "tensor")), P(("dp", "tensor")), P(("dp", "tensor")), P("dp")),
        check_vma=False,
    )
```

```python
import jax
import jax.numpy as jnp
from jax import lax
from jax.experimental import pallas as pl
from jax.experimental.pallas import tpu as pltpu
from jax.sharding import PartitionSpec as P

EPSILON = 1e-06
MESH = pl.DeviceIdType.MESH
LIVE = 48


def finish_kernel(n_tensor, n_dp, count, send_ref, span_ref, ids_ref, spread_ref, result_ref,
                  held, t_held, d_held, part_msg, route_msg,
                  a_send, a_recv, t_send, t_recv, d_send, d_recv):
    me = lax.axis_index("tensor")
    dp = lax.axis_index("dp")
    barrier = pltpu.get_barrier_semaphore()
    for offset in range(1, n_tensor):
        peer = lax.rem(me + offset, n_tensor)
        pl.semaphore_signal(barrier, inc=1, device_id=(dp, peer), device_id_type=MESH)
    for offset in range(1, n_dp):
        peer = lax.rem(dp + offset, n_dp)
        pl.semaphore_signal(barrier, inc=1, device_id=(peer, me), device_id_type=MESH)
    pl.semaphore_wait(barrier, n_tensor - 1 + n_dp - 1)

    held[me] = send_ref[me]
    copies = []
    for offset in range(1, n_tensor):
        peer = lax.rem(me + offset, n_tensor)
        copy = pltpu.make_async_remote_copy(
            src_ref=send_ref.at[peer], dst_ref=held.at[me],
            send_sem=a_send.at[offset], recv_sem=a_recv.at[offset],
            device_id=(dp, peer), device_id_type=MESH,
        )
        copy.start()
        copies.append(copy)
    for copy in copies:
        copy.wait_send()
    for offset in range(1, n_tensor):
        source = lax.rem(me + n_tensor - offset, n_tensor)
        pltpu.make_async_remote_copy(
            src_ref=send_ref.at[source], dst_ref=held.at[source],
            send_sem=a_send.at[offset], recv_sem=a_recv.at[offset],
            device_id=(dp, source), device_id_type=MESH,
        ).wait_recv()

    lanes = held.shape[2]
    peak = lax.fori_loop(
        0, n_tensor, lambda p, m: jnp.maximum(m, held[p][0:1, :]),
        jnp.full((1, lanes), -jnp.inf, jnp.float32),
    )

    def gather_sums(p, sums):
        mass, spread, target = sums
        block = held[p]
        gap = block[0:1, :] - peak
        factor = jnp.exp(gap)
        mass = mass + factor * block[1:2, :]
        spread = spread + factor * (block[2:3, :] + gap * block[1:2, :])
        return mass, spread, target + block[3:4, :]

    zero = jnp.zeros((1, lanes), jnp.float32)
    mass, spread, target = lax.fori_loop(0, n_tensor, gather_sums, (zero, zero, zero))
    log_mass = jnp.log(mass)
    logprob = target - peak - log_mass
    entropy = log_mass - spread / mass
    slots = spread_ref.shape[0]
    placed = spread_ref[...] > 0.0
    same = (
        lax.broadcasted_iota(jnp.int32, (slots, slots), 0)
        == lax.broadcasted_iota(jnp.int32, (slots, slots), 1)
    )
    result_ref[...] = jnp.zeros(result_ref.shape, jnp.float32)
    for index, value in enumerate((logprob, entropy)):
        column = jnp.sum(jnp.where(placed, value, 0.0), axis=1, keepdims=True)
        result_ref[index:index + 1, :slots] = jnp.sum(jnp.where(same, column, 0.0), axis=0, keepdims=True)

    spans = span_ref[...]
    partial = jnp.sum(spans[:, :lanes] * logprob, axis=1, keepdims=True) / spans[:, 127:128]
    part_msg[...] = jnp.broadcast_to(partial, part_msg.shape)
    t_held[me] = part_msg[...]
    copies = []
    for offset in range(1, n_tensor):
        peer = lax.rem(me + offset, n_tensor)
        copy = pltpu.make_async_remote_copy(
            src_ref=part_msg, dst_ref=t_held.at[me],
            send_sem=t_send.at[offset], recv_sem=t_recv.at[offset],
            device_id=(dp, peer), device_id_type=MESH,
        )
        copy.start()
        copies.append(copy)
    for copy in copies:
        copy.wait_send()
    for offset in range(1, n_tensor):
        source = lax.rem(me + n_tensor - offset, n_tensor)
        pltpu.make_async_remote_copy(
            src_ref=part_msg, dst_ref=t_held.at[source],
            send_sem=t_send.at[offset], recv_sem=t_recv.at[offset],
            device_id=(dp, source), device_id_type=MESH,
        ).wait_recv()

    total = jnp.sum(t_held[...], axis=0)
    lane = lax.broadcasted_iota(jnp.int32, total.shape, 1)
    route_msg[...] = jnp.where(lane == 0, total, jnp.where(lane == 1, ids_ref[...], 0.0))
    d_held[dp] = route_msg[...]
    copies = []
    for offset in range(1, n_dp):
        peer = lax.rem(dp + offset, n_dp)
        copy = pltpu.make_async_remote_copy(
            src_ref=route_msg, dst_ref=d_held.at[dp],
            send_sem=d_send.at[offset], recv_sem=d_recv.at[offset],
            device_id=(peer, me), device_id_type=MESH,
        )
        copy.start()
        copies.append(copy)
    for copy in copies:
        copy.wait_send()
    for offset in range(1, n_dp):
        source = lax.rem(dp + n_dp - offset, n_dp)
        pltpu.make_async_remote_copy(
            src_ref=route_msg, dst_ref=d_held.at[source],
            send_sem=d_send.at[offset], recv_sem=d_recv.at[offset],
            device_id=(source, me), device_id_type=MESH,
        ).wait_recv()
    wanted = (dp * count + lax.broadcasted_iota(jnp.int32, (1, count), 1)).astype(jnp.float32)
    score = jnp.zeros((1, count), jnp.float32)
    for group in range(n_dp):
        block = d_held[group]
        hit = block[:count, 1:2] == wanted
        score = score + jnp.sum(jnp.where(hit, block[:count, 0:1], 0.0), axis=0, keepdims=True)
    result_ref[2:3, :count] = score


def finish(blocks, spans, ids, spread, n_tensor, n_dp, count):
    tile = spans.shape
    lanes = blocks.shape[2]
    return pl.pallas_call(
        lambda *refs: finish_kernel(n_tensor, n_dp, count, *refs),
        out_shape=jax.ShapeDtypeStruct((8, 128), jnp.float32),
        in_specs=[pl.BlockSpec(memory_space=pltpu.VMEM)] * 4,
        out_specs=pl.BlockSpec(memory_space=pltpu.VMEM),
        scratch_shapes=[
            pltpu.VMEM(blocks.shape, jnp.float32),
            pltpu.VMEM((n_tensor,) + tile, jnp.float32),
            pltpu.VMEM((n_dp,) + tile, jnp.float32),
            pltpu.VMEM(tile, jnp.float32),
            pltpu.VMEM(tile, jnp.float32),
            pltpu.SemaphoreType.DMA((n_tensor,)),
            pltpu.SemaphoreType.DMA((n_tensor,)),
            pltpu.SemaphoreType.DMA((n_tensor,)),
            pltpu.SemaphoreType.DMA((n_tensor,)),
            pltpu.SemaphoreType.DMA((n_dp,)),
            pltpu.SemaphoreType.DMA((n_dp,)),
        ],
        compiler_params=pltpu.CompilerParams(collective_id=3, has_side_effects=True),
    )(blocks, spans, ids, spread)


def prep_kernel(hidden_ref, gain_ref, mask_ref, ids_ref, out_ref):
    width = hidden_ref.shape[1]
    own_rows = hidden_ref.shape[0]
    widened = hidden_ref[...].astype(jnp.float32)
    inverse_rms = lax.rsqrt(jnp.mean(widened * widened, axis=1, keepdims=True) + EPSILON)
    normed = (widened * inverse_rms * gain_ref[...]).astype(jnp.bfloat16)
    live = jnp.broadcast_to(mask_ref[...].astype(jnp.float32), (8, own_rows))
    upper = (
        lax.broadcasted_iota(jnp.int32, (own_rows, own_rows), 0)
        <= lax.broadcasted_iota(jnp.int32, (own_rows, own_rows), 1)
    ).astype(jnp.float32)
    live_sum = jnp.dot(live, upper, preferred_element_type=jnp.float32)[0:1, :]
    rank = lax.broadcasted_iota(jnp.int32, (LIVE, own_rows), 0).astype(jnp.float32)
    chosen = ((live[0:1, :] == 1.0) & (live_sum - 1.0 == rank)).astype(jnp.bfloat16)
    out_ref[:, :width] = jnp.dot(chosen, normed, preferred_element_type=jnp.float32).astype(jnp.bfloat16)
    ids = ids_ref[...]
    high = lax.shift_right_logical(ids, 8).astype(jnp.float32)
    low = jnp.bitwise_and(ids, 255).astype(jnp.float32)
    row = lax.broadcasted_iota(jnp.int32, (128, own_rows), 0)
    meta_in = jnp.where(row == 0, high, jnp.where(row == 1, low, 0.0)).astype(jnp.bfloat16)
    meta = lax.dot_general(
        chosen, meta_in, (((1,), (1,)), ((), ())), preferred_element_type=jnp.float32
    )
    out_ref[:, width:] = meta.astype(jnp.bfloat16)


def prep(hidden, norm_gain, slot_mask, token_ids):
    own_rows, width = hidden.shape
    return pl.pallas_call(
        prep_kernel,
        out_shape=jax.ShapeDtypeStruct((LIVE, width + 128), jnp.bfloat16),
        in_specs=[pl.BlockSpec(memory_space=pltpu.VMEM)] * 4,
        out_specs=pl.BlockSpec(memory_space=pltpu.VMEM),
    )(hidden, norm_gain.reshape(1, width), slot_mask.reshape(1, own_rows), token_ids.reshape(1, own_rows))


def stats_kernel(x_ref, wt_ref, out_ref, logits_ref):
    vocab, depth = wt_ref.shape
    tile = x_ref.shape[0]
    contract_last = (((1,), (1,)), ((), ()))
    logits_ref[...] = lax.dot_general(
        wt_ref[...], x_ref[:, :depth], contract_last, preferred_element_type=jnp.float32
    )
    pick = (
        lax.broadcasted_iota(jnp.int32, (8, 128), 0) == lax.broadcasted_iota(jnp.int32, (8, 128), 1)
    ).astype(jnp.bfloat16)
    meta = lax.dot_general(pick, x_ref[:, depth:depth + 128], contract_last, preferred_element_type=jnp.float32)
    token = (meta[0:1, :] * 256.0 + meta[1:2, :]).astype(jnp.int32) - lax.axis_index("tensor") * vocab
    chunks = vocab // 8
    rest = vocab - chunks * 8

    def top(c, m):
        return jnp.maximum(m, logits_ref[pl.ds(pl.multiple_of(c * 8, 8), 8), :])

    peak = jnp.max(
        lax.fori_loop(0, chunks, top, jnp.full((8, tile), -jnp.inf, jnp.float32), unroll=28), axis=0, keepdims=True
    )
    if rest:
        peak = jnp.maximum(peak, jnp.max(logits_ref[chunks * 8:vocab, :], axis=0, keepdims=True))

    def accumulate(block, first, sums):
        mass, spread, target = sums
        shifted = block - peak
        weights = jnp.exp(shifted)
        entry = first + lax.broadcasted_iota(jnp.int32, block.shape, 0)
        return (
            mass + jnp.sum(weights, axis=0, keepdims=True) if block.shape[0] != 8 else mass + weights,
            spread + jnp.sum(weights * shifted, axis=0, keepdims=True) if block.shape[0] != 8 else spread + weights * shifted,
            target + jnp.sum(jnp.where(entry == token, block, 0.0), axis=0, keepdims=True)
            if block.shape[0] != 8 else target + jnp.where(entry == token, block, 0.0),
        )

    def body(c, sums):
        start = pl.multiple_of(c * 8, 8)
        return accumulate(logits_ref[pl.ds(start, 8), :], start, sums)

    zero = jnp.zeros((8, tile), jnp.float32)
    sums = lax.fori_loop(0, chunks, body, (zero, zero, zero), unroll=28)
    mass, spread, target = (jnp.sum(value, axis=0, keepdims=True) for value in sums)
    if rest:
        one = jnp.zeros((1, tile), jnp.float32)
        extra = accumulate(logits_ref[chunks * 8:vocab, :], chunks * 8, (one, one, one))
        mass, spread, target = mass + extra[0], spread + extra[1], target + extra[2]
    row = lax.broadcasted_iota(jnp.int32, out_ref.shape, 0)
    out_ref[...] = jnp.where(
        row == 0, peak,
        jnp.where(row == 1, mass, jnp.where(row == 2, spread, jnp.where(row == 3, target, 0.0))),
    )


def row_stats(rows, weight_t, tile):
    count = rows.shape[0]
    vocab, depth = weight_t.shape
    return pl.pallas_call(
        stats_kernel,
        out_shape=jax.ShapeDtypeStruct((8, count), jnp.float32),
        grid=(count // tile,),
        in_specs=[
            pl.BlockSpec((tile, rows.shape[1]), lambda i: (i, 0)),
            pl.BlockSpec((vocab, depth), lambda i: (0, 0)),
        ],
        out_specs=pl.BlockSpec((8, tile), lambda i: (0, i)),
        scratch_shapes=[pltpu.VMEM((vocab, tile), jnp.float32)],
        compiler_params=pltpu.CompilerParams(vmem_limit_bytes=56 * 1024 * 1024),
        cost_estimate=pl.CostEstimate(
            flops=2 * count * depth * vocab,
            transcendentals=count * vocab,
            bytes_accessed=2 * count * rows.shape[1] + 2 * depth * vocab + 32 * count,
        ),
    )(rows, weight_t)


def on_device(
    hidden, norm_gain, head_weight, value_weight, token_ids, slot_mask, lengths, request_order
):
    own_rows = hidden.shape[0]
    vocab_local = head_weight.shape[1]
    n_tensor = lax.axis_size("tensor")
    n_dp = lax.axis_size("dp")
    tensor_index = lax.axis_index("tensor")
    widened = hidden.astype(jnp.float32)
    inverse_rms = lax.rsqrt(jnp.mean(widened * widened, axis=1, keepdims=True) + EPSILON)
    normed = (widened * inverse_rms * norm_gain).astype(jnp.bfloat16)
    weight_mask = slot_mask.astype(jnp.float32)
    token_value = weight_mask * jnp.dot(normed, value_weight, preferred_element_type=jnp.float32)

    width = hidden.shape[1]
    live_sum = jnp.cumsum(slot_mask)
    slot_index = jnp.arange(own_rows, dtype=jnp.int32)
    chosen = (slot_mask[None, :] == 1) & (
        live_sum[None, :] - 1 == jnp.arange(LIVE, dtype=jnp.int32)[:, None]
    )
    source = jnp.sum(jnp.where(chosen, slot_index[None, :], 0), axis=1)
    block = prep(hidden, norm_gain, slot_mask, token_ids)
    gathered = lax.all_gather(block, "tensor", axis=0, tiled=True)
    row_count = gathered.shape[0]
    stats = row_stats(gathered, head_weight.T, 256 if row_count % 256 == 0 else row_count)
    blocks = stats[:4].reshape(4, n_tensor, LIVE).transpose(1, 0, 2)
    request_count = lengths.shape[1]
    span_lengths = lengths[0]
    span_ends = jnp.cumsum(span_lengths)
    slot_ids = tensor_index * own_rows + source
    position = jnp.sum((slot_ids[:, None] >= span_ends[None, :]).astype(jnp.int32), axis=1)
    live = jnp.arange(LIVE, dtype=jnp.int32) < live_sum[-1]
    member = (position[None, :] == jnp.arange(8, dtype=jnp.int32)[:, None]) & live[None, :]
    spans = (
        jnp.zeros((8, 128), jnp.float32)
        .at[:, :LIVE].set(member.astype(jnp.float32))
        .at[:, 127].set(jnp.ones((8,), jnp.float32).at[:request_count].set(span_lengths.astype(jnp.float32)))
    )
    ids_tile = jnp.zeros((8, 128), jnp.float32).at[:request_count, 1].set(request_order.astype(jnp.float32))
    place = live_sum - 1
    spread = ((place[:, None] == jnp.arange(LIVE, dtype=jnp.int32)[None, :]) & (slot_mask[:, None] == 1))
    result = finish(blocks, spans, ids_tile, spread.astype(jnp.float32), n_tensor, n_dp, request_count)
    token_logprob = result[0, :own_rows]
    token_entropy = result[1, :own_rows]
    request_score = result[2, :request_count]
    return (token_logprob, token_entropy, token_value, request_score)


def solution(mesh):
    return jax.shard_map(
        on_device,
        mesh=mesh,
        in_specs=(
            P(("dp", "tensor"), None),
            P(),
            P(None, "tensor"),
            P(),
            P(("dp", "tensor")),
            P(("dp", "tensor")),
            P("dp", None),
            P("dp"),
        ),
        out_specs=(P(("dp", "tensor")), P(("dp", "tensor")), P(("dp", "tensor")), P("dp")),
        check_vma=False,
    )
```
